32 devices in a mesh: groups: 2 (over y), ctx: 4 (over z), tp: 4 (over x, core).
Axes of the slice: x: 2, y: 2, z: 4, core: 2. Of those that a mesh axis runs over, the one named last changes fastest.
Arguments:
- queries: bfloat16 [1152, 8192], P(('groups', 'ctx'), 'tp'), parts along dimension 0, may hold values from -6 to 6
- keys: bfloat16 [1152, 1024], P(('groups', 'ctx'), 'tp'), parts along dimension 0, may hold values from -6 to 6
- values: bfloat16 [1152, 1024], P(('groups', 'ctx'), 'tp'), parts along dimension 0, may hold values from -6 to 6
- residual: bfloat16 [1152, 8192], P(('groups', 'ctx'), 'tp'), parts along dimension 0, may hold values from -4 to 4
- out_weight: bfloat16 [8192, 8192], P('tp', 'ctx'), may hold values from -0.0625 to 0.0625
- value_head: bfloat16 [8192], P('tp'), may hold values from -0.5 to 0.5
- segment_ids: int32 [1152], P(('groups', 'ctx')), parts along dimension 0, may hold values from 0 to 3, as said below
- positions: int32 [1152], P(('groups', 'ctx')), parts along dimension 0, may hold values from 0 to 251, as said below
- turn_ids: int32 [1152], P(('groups', 'ctx')), parts along dimension 0, may hold values from 0 to 15, as said below
Outputs:
- hidden_out: bfloat16 [1152, 8192], P(('groups', 'ctx'), 'tp'), parts along dimension 0
- turn_means: float32 [32], P('groups'), parts along dimension 0
The draws below stay inside these ranges and needn't reach their ends.
There are 2 independent parts, one for each index of `groups`. The reference program is written for one: setup_inputs(seed, part) draws one part's arguments, and reference() takes and returns one part's arrays. A program takes and returns all parts, laid end to end along the dimension named above; an argument that names none is the same for every part. Nothing has to cross between parts.
Inputs may be any that keep to these rules, and one draw needn't show every extreme that they name: `segment_ids`: in token order (the stored order reverted) segment ids never fall; the sequence holds 4 rollouts of 36 to 252 tokens, one of exactly 252. `positions`: A row's position is its token's offset from the first token of its rollout. `turn_ids`: A row's turn id is 4 times its segment id plus how many of its rollout's three turn starts lie at or before its position; turn starts lie at positions 1 to the rollout's length minus 1 and may coincide.
All inputs are finite; a program needn't handle non-finite values.
Results may differ from the reference program's by a relative error of at most 0.013.
Values may be sent and summed in bfloat16 or wider, within the bound.
A program may use at most 64 MiB of HBM per device.

```python
import math
import jax
import jax.numpy as jnp
from jax import lax

D = 8192
QUERY_HEADS = 64
KEY_VALUE_HEADS = 8
HEAD_SIZE = 128
TOK_DEV = 144
SEGS = 4
PACKED_TOKENS = 576
SEG_MEAN = 144
TURNS = 16
N_TP = 4


def layout(base_key):
    ctx_count = PACKED_TOKENS // TOK_DEV
    half_rows = TOK_DEV // 2
    row_index = jnp.arange(PACKED_TOKENS, dtype=jnp.int32)
    block_index = row_index // TOK_DEV
    inner_index = row_index % TOK_DEV
    token_of_row = jnp.where(inner_index < half_rows, block_index * half_rows + inner_index, (2 * ctx_count - 1 - block_index) * half_rows + inner_index - half_rows)
    segment_total = SEGS
    pair_total = segment_total // 2
    lengths_first = jax.random.randint(jax.random.fold_in(base_key, 1), (pair_total,), SEG_MEAN // 4, 7 * SEG_MEAN // 4 + 1)
    lengths_first = jnp.where(jnp.arange(pair_total) == 0, 7 * SEG_MEAN // 4, lengths_first)
    seg_lengths = jnp.concatenate([lengths_first, 2 * SEG_MEAN - lengths_first]).astype(jnp.int32)
    rest_order = jax.random.permutation(jax.random.fold_in(base_key, 3), segment_total - 1) + 1
    order = jnp.concatenate([jnp.zeros((1,), jnp.int32), rest_order.astype(jnp.int32)])
    seg_lengths = seg_lengths[order]
    seg_ends = jnp.cumsum(seg_lengths).astype(jnp.int32)
    seg_starts = seg_ends - seg_lengths
    token_index = jnp.arange(PACKED_TOKENS, dtype=jnp.int32)
    seg_of_token = jnp.sum((token_index[:, None] >= seg_ends[None, :]).astype(jnp.int32), axis=1)
    pos_of_token = token_index - seg_starts[seg_of_token]
    turn_cuts = jax.random.randint(jax.random.fold_in(base_key, 4), (segment_total, 3), 1, seg_lengths[:, None])
    turn_of_token = 4 * seg_of_token + jnp.sum((pos_of_token[:, None] >= turn_cuts[seg_of_token]).astype(jnp.int32), axis=1)
    return (token_of_row, seg_of_token, pos_of_token, turn_of_token)


def draw_segment_ids(base_key, part_index):
    token_of_row, seg_of_token, pos_of_token, turn_of_token = layout(base_key)
    return seg_of_token[token_of_row].astype(jnp.int32)


def draw_positions(base_key, part_index):
    token_of_row, seg_of_token, pos_of_token, turn_of_token = layout(base_key)
    return pos_of_token[token_of_row].astype(jnp.int32)


def draw_turn_ids(base_key, part_index):
    token_of_row, seg_of_token, pos_of_token, turn_of_token = layout(base_key)
    return turn_of_token[token_of_row].astype(jnp.int32)


def draw_queries(base_key, part_index):
    complete_shape = (PACKED_TOKENS, QUERY_HEADS * HEAD_SIZE)
    sampled_inputs = jax.random.truncated_normal(jax.random.fold_in(base_key, 11), -4.0, 4.0, complete_shape) * 1.5
    return sampled_inputs.astype(jnp.bfloat16)


def draw_keys(base_key, part_index):
    complete_shape = (PACKED_TOKENS, KEY_VALUE_HEADS * HEAD_SIZE)
    sampled_inputs = jax.random.truncated_normal(jax.random.fold_in(base_key, 12), -4.0, 4.0, complete_shape) * 1.5
    return sampled_inputs.astype(jnp.bfloat16)


def block_scale(key, extent, pieces, smallest, top_value):
    level = 1.0
    for dim, blocks in pieces:
        heights = jax.random.uniform(jax.random.fold_in(jax.random.fold_in(key, 6), dim), (blocks,), jnp.float32, smallest / len(pieces), top_value / len(pieces))
        level = level * jnp.repeat(jnp.exp(heights), extent[dim] // blocks).reshape((-1,) + (1,) * (len(extent) - 1 - dim))
    return level


def scatter_about(rng, dims, scale, bound, cuts=(), held_as=jnp.bfloat16):
    drawn = jax.random.normal(rng, dims, jnp.float32) * scale
    if len(cuts) > 0:
        drawn = block_scale(rng, dims, cuts, -0.22, 0.18) * drawn
    return jnp.clip(drawn, min=-bound, max=bound).astype(held_as)


def setup_inputs(seed: int = 0, part: int = 0) -> dict:
    key_of = jax.random.split(jax.random.key(seed), 10)
    part_keys = jax.random.split(jax.random.fold_in(key_of[9], part), 10)
    return {
        "queries": draw_queries(jax.random.fold_in(jax.random.fold_in(key_of[9], part), 71), part),
        "keys": draw_keys(jax.random.fold_in(jax.random.fold_in(key_of[9], part), 71), part),
        "values": scatter_about(part_keys[2], (PACKED_TOKENS, KEY_VALUE_HEADS * HEAD_SIZE), 1.0, 6.0, ((0, 4), (1, 4))),
        "residual": scatter_about(part_keys[3], (PACKED_TOKENS, D), 0.5, 4.0, ((0, 4), (1, 4))),
        "out_weight": scatter_about(key_of[4], (QUERY_HEADS * HEAD_SIZE, D), (QUERY_HEADS * HEAD_SIZE) ** -0.5, 0.0625, ((0, 4), (1, 4))),
        "value_head": scatter_about(key_of[5], (D,), (D // 64) ** -0.5, 0.5, ((0, 4),)),
        "segment_ids": draw_segment_ids(jax.random.fold_in(jax.random.fold_in(key_of[9], part), 71), part),
        "positions": draw_positions(jax.random.fold_in(jax.random.fold_in(key_of[9], part), 71), part),
        "turn_ids": draw_turn_ids(jax.random.fold_in(jax.random.fold_in(key_of[9], part), 71), part),
    }


def reference(queries, keys, values, residual, out_weight, value_head, segment_ids, positions, turn_ids):
    sequence_length = queries.shape[0]
    query_head_group = QUERY_HEADS // KEY_VALUE_HEADS
    tile_row_count = math.gcd(sequence_length, 128)
    score_scale = 1.0 / math.sqrt(HEAD_SIZE)
    key_head_rows = keys.reshape(sequence_length, KEY_VALUE_HEADS, HEAD_SIZE).astype(jnp.float32)
    value_head_rows = values.reshape(sequence_length, KEY_VALUE_HEADS, HEAD_SIZE).astype(jnp.float32)

    def one_block(block_index):
        first_row = block_index * tile_row_count
        query_tile = lax.dynamic_slice_in_dim(queries, first_row, tile_row_count, 0)
        query_tile = query_tile.reshape(tile_row_count, KEY_VALUE_HEADS, query_head_group, HEAD_SIZE).astype(jnp.float32)
        seg_block = lax.dynamic_slice_in_dim(segment_ids, first_row, tile_row_count, 0)
        pos_block = lax.dynamic_slice_in_dim(positions, first_row, tile_row_count, 0)
        allowed = (seg_block[:, None] == segment_ids[None, :]) & (positions[None, :] <= pos_block[:, None])
        scores = jnp.einsum('qhgd,khd->hgqk', query_tile, key_head_rows) * score_scale
        scores = jnp.where(allowed, scores, -1e+30)
        row_max = lax.optimization_barrier(jnp.max(scores, axis=-1, keepdims=True))
        weights = jnp.where(allowed, jnp.exp(scores - row_max), 0.0)
        denominator = lax.optimization_barrier(jnp.sum(weights, axis=-1))
        rounded = lax.optimization_barrier(weights.astype(jnp.bfloat16)).astype(jnp.float32)
        numerator = jnp.einsum('hgqk,khd->hgqd', rounded, value_head_rows)
        outcome = numerator / denominator[..., None]
        return outcome.transpose(2, 0, 1, 3).reshape(tile_row_count, QUERY_HEADS * HEAD_SIZE).astype(jnp.bfloat16)
    attention = lax.map(one_block, jnp.arange(sequence_length // tile_row_count, dtype=jnp.int32))
    attention = attention.reshape(sequence_length, QUERY_HEADS * HEAD_SIZE)
    group_cols = QUERY_HEADS * HEAD_SIZE // N_TP
    projection = jnp.zeros((sequence_length, D), jnp.float32)
    for tp_group in range(N_TP):
        lower = tp_group * group_cols
        upper = lower + group_cols
        partial_term = jnp.dot(attention[:, lower:upper], out_weight[lower:upper], preferred_element_type=jnp.float32)
        projection = projection + lax.optimization_barrier(partial_term.astype(jnp.bfloat16)).astype(jnp.float32)
    hidden_out = (residual.astype(jnp.float32) + projection).astype(jnp.bfloat16)
    token_score = jnp.dot(hidden_out, value_head, preferred_element_type=jnp.float32)
    one_hot = (turn_ids[:, None] == jnp.arange(TURNS, dtype=jnp.int32)[None, :]).astype(jnp.float32)
    turn_sum = jnp.dot(token_score, one_hot, precision=lax.Precision.HIGHEST)
    turn_count = lax.optimization_barrier(jnp.sum(one_hot, axis=0))
    turn_means = turn_sum / jnp.maximum(turn_count, 1.0)
    return (hidden_out, turn_means)
```

```python
import functools
import math

import jax
import jax.numpy as jnp
from jax import lax
from jax.experimental import pallas as pl
from jax.experimental.pallas import tpu as pltpu
from jax.sharding import PartitionSpec as P

HEAD_SIZE = 128
TURNS = 16


def shards(
    queries, keys, values, residual, out_weight, value_head, segment_ids, positions, turn_ids
):
    tok_rows = queries.shape[0]
    kv_heads = keys.shape[1] // HEAD_SIZE
    query_head_group = queries.shape[1] // keys.shape[1]
    query_rows = query_head_group * tok_rows
    score_scale = 1.0 / math.sqrt(HEAD_SIZE)
    grouped = (
        queries.reshape(tok_rows, kv_heads, query_head_group, HEAD_SIZE)
        .transpose(1, 2, 0, 3)
        .reshape(kv_heads, query_rows, HEAD_SIZE)
    )
    seg_rows = jnp.tile(segment_ids, query_head_group)
    pos_rows = jnp.tile(positions, query_head_group)

    def update(running, key_block, value_block, seg_block, pos_block):
        allowed = (seg_rows[:, None] == seg_block[None, :]) & (
            pos_block[None, :] <= pos_rows[:, None]
        )
        numerator, row_max, denominator = running
        scores = (
            jnp.einsum("hqd,khd->hqk", grouped, key_block, preferred_element_type=jnp.float32)
            * score_scale
        )
        scores = jnp.where(allowed[None], scores, -1e30)
        new_max = jnp.maximum(row_max, jnp.max(scores, axis=2))
        weights = jnp.where(allowed[None], jnp.exp(scores - new_max[..., None]), 0.0)
        factor = jnp.exp(row_max - new_max)
        denominator = denominator * factor + jnp.sum(weights, axis=2)
        product = jnp.einsum(
            "hqk,khd->hqd",
            weights.astype(jnp.bfloat16),
            value_block,
            preferred_element_type=jnp.float32,
        )
        numerator = numerator * factor[..., None] + product
        return (numerator, new_max, denominator)

    initial = (
        jnp.zeros((kv_heads, query_rows, HEAD_SIZE), jnp.float32),
        jnp.full((kv_heads, query_rows), -1e30, jnp.float32),
        jnp.zeros((kv_heads, query_rows), jnp.float32),
    )
    running = initial
    key_piece = lax.all_gather(keys, "ctx", axis=0, tiled=True)
    value_piece = lax.all_gather(values, "ctx", axis=0, tiled=True)
    seg_piece = lax.all_gather(segment_ids, "ctx", axis=0, tiled=True)
    pos_piece = lax.all_gather(positions, "ctx", axis=0, tiled=True)
    row_count = key_piece.shape[0]
    key_piece = key_piece.reshape(row_count, kv_heads, HEAD_SIZE)
    value_piece = value_piece.reshape(row_count, kv_heads, HEAD_SIZE)
    block_width = math.gcd(row_count, 512)
    block_steps = row_count // block_width
    stacked = (
        key_piece.reshape(block_steps, block_width, kv_heads, HEAD_SIZE),
        value_piece.reshape(block_steps, block_width, kv_heads, HEAD_SIZE),
        seg_piece.reshape(block_steps, block_width),
        pos_piece.reshape(block_steps, block_width),
    )

    def block_step(running_state, block_set):
        return (update(running_state, block_set[0], block_set[1], block_set[2], block_set[3]), None)

    running, _ = lax.scan(block_step, running, stacked)
    numerator, row_max, denominator = running
    attention = (numerator / denominator[..., None]).reshape(
        kv_heads, query_head_group, tok_rows, HEAD_SIZE
    )
    attention = (
        attention.transpose(2, 0, 1, 3)
        .reshape(tok_rows, kv_heads * query_head_group * HEAD_SIZE)
        .astype(jnp.bfloat16)
    )
    partial_value = jnp.dot(
        lax.all_gather(attention, "ctx", axis=0, tiled=True),
        out_weight,
        preferred_element_type=jnp.float32,
    ).astype(jnp.bfloat16)
    term_rows = lax.all_to_all(
        partial_value, "ctx", split_axis=0, concat_axis=1, tiled=True
    ).astype(jnp.float32)
    summed = lax.psum_scatter(
        term_rows.astype(jnp.bfloat16), "tp", scatter_dimension=1, tiled=True
    ).astype(jnp.float32)
    hidden_out = (residual.astype(jnp.float32) + summed).astype(jnp.bfloat16)
    token_score = jnp.dot(hidden_out, value_head, preferred_element_type=jnp.float32)
    one_hot = (turn_ids[:, None] == jnp.arange(TURNS, dtype=jnp.int32)[None, :]).astype(jnp.float32)
    local_sum = jnp.dot(token_score, one_hot, precision=lax.Precision.HIGHEST)
    local_count = jnp.where(lax.axis_index("tp") == 0, jnp.sum(one_hot, axis=0), 0.0)
    totals, counts = lax.psum((local_sum, local_count), ("ctx", "tp"))
    turn_means = totals / jnp.maximum(counts, 1.0)
    return (hidden_out, turn_means)


MESH = pl.DeviceIdType.MESH
F32 = jnp.float32
BF16 = jnp.bfloat16
MASKED = -1e30


def kernel(
    dims, k_ref, v_ref, pos_ref, tid_ref, vh_ref, q_ref, res_hbm, w_hbm,
    out_ref, mean_ref,
    kvb, bias0, bias1, tcol, qrow, qs, ot, att, wv, acc, keep, sib_out, sib_in,
    xs_out, xs_in, red, fin, resv, tot,
    kv_send, kv_recv, att_send, att_recv, sib_send, sib_recv, xs_send, xs_recv,
    fin_send, fin_recv, tot_send, tot_recv, w_sem, res_sem, go_sem,
):
    n, tn, rows, groups, per, cb, pieces, reach = dims
    piece = rows // pieces
    half = rows // 2
    pad = -(-half // 16) * 16
    blocks = 2 * n
    lanes = per * pad
    chunks = groups * 2
    chunk = groups * per * HEAD_SIZE // chunks
    c = lax.axis_index("ctx")
    t = lax.axis_index("tp")
    core = lax.rem(t, 2)
    col = t // 2
    sibling = t + 1 - 2 * core
    across = lax.rem(t + 2, tn)
    own_q = 2 * core + col
    far_q = 2 * core + 1 - col
    scale = 1.0 / math.sqrt(HEAD_SIZE) * math.log2(math.e)

    barrier = pltpu.get_barrier_semaphore()

    for j in range(1, tn):
        pl.semaphore_signal(
            barrier, inc=1, device_id={"tp": lax.rem(t + j, tn)}, device_id_type=MESH
        )
    for away in (-1, 1):
        @pl.when((c + away >= 0) & (c + away < n))
        def _():
            pl.semaphore_signal(
                barrier, inc=1, device_id={"ctx": c + away}, device_id_type=MESH
            )

    def w_copy(i):
        return pltpu.make_async_copy(
            w_hbm.at[:, pl.ds(pl.multiple_of(i * cb, 128), cb)], wv.at[i], w_sem.at[i]
        )

    res_copy = pltpu.make_async_copy(res_hbm, resv, res_sem)

    def needs(d, b):
        late = blocks - 1 - d
        return d - reach <= b <= d or late - reach <= b <= late

    def owner(b):
        return b if b < n else blocks - 1 - b

    def carried(d, e, b):
        if not 0 <= e < n:
            return False
        beyond = range(0, e + 1) if e < d else range(e, n)
        behind = owner(b) >= d if e < d else owner(b) <= d
        return behind and any(needs(x, b) for x in beyond)

    def kv_copy(g, b, e, way):
        return pltpu.make_async_remote_copy(
            src_ref=kvb.at[g, b], dst_ref=kvb.at[g, b],
            send_sem=kv_send.at[g, b, way], recv_sem=kv_recv.at[g, b],
            device_id={"ctx": e}, device_id_type=MESH,
        )

    def on(d):
        return pl.when(c == d)

    def kv_pass(d, g, b):
        for way, e in ((0, d - 1), (1, d + 1)):
            if carried(d, e, b):
                kv_copy(g, b, e, way).start()

    def kv_arrivals(d, dist):
        return [
            b for b in range(blocks)
            if abs(owner(b) - d) == dist
            and (carried(d - 1, d, b) if owner(b) < d else carried(d + 1, d, b))
        ]

    def kv_own(g):
        for d in range(n):
            @on(d)
            def _():
                for b in (d, blocks - 1 - d):
                    kv_pass(d, g, b)

    def kv_take(g, dists):
        for d in range(n):
            @on(d)
            def _():
                for dist in dists:
                    for b in kv_arrivals(d, dist):
                        kv_copy(g, b, d, 0).wait_recv()
                        kv_pass(d, g, b)

    zeros = jnp.zeros((pad - half, HEAD_SIZE), F32)
    for g in range(groups):
        span = slice(g * HEAD_SIZE, (g + 1) * HEAD_SIZE)
        for ref, low in ((k_ref, 0), (v_ref, pad)):
            x = ref[:, span].astype(F32)
            kvb[g, c, low:low + pad, :] = jnp.concatenate([x[:half], zeros]).astype(BF16)
            kvb[g, blocks - 1 - c, low:low + pad, :] = jnp.concatenate(
                [x[half:], zeros]
            ).astype(BF16)
    for d in range(n):
        window = set(range(n)) | set(range(n - 1 - d, blocks - d))
        missing = [b for b in sorted(window) if owner(b) != d and not any(
            b in kv_arrivals(d, dist) for dist in range(1, n))]
        if missing:
            @on(d)
            def _():
                for g in range(groups):
                    for b in missing:
                        kvb[g, b] = jnp.zeros((2 * pad, HEAD_SIZE), BF16)


    def att_copy(s, q, d):
        return pltpu.make_async_remote_copy(
            src_ref=att.at[s, q], dst_ref=att.at[s, q],
            send_sem=att_send.at[d, s, q], recv_sem=att_recv.at[s, q],
            device_id={"ctx": c + 1 - 2 * d}, device_id_type=MESH,
        )

    def goes(s, d):
        if d == 0:
            return (s <= c) & (c < n - 1)
        return (s >= c) & (c > 0)

    def band(p):
        return pl.ds(p * piece, piece)

    def sib_copy(s, j):
        return pltpu.make_async_remote_copy(
            src_ref=sib_out.at[s, j], dst_ref=sib_in.at[s, j],
            send_sem=sib_send.at[s, j], recv_sem=sib_recv.at[s, j],
            device_id={"tp": sibling}, device_id_type=MESH,
        )

    def xs_copy(s, p):
        return pltpu.make_async_remote_copy(
            src_ref=xs_out.at[s, band(p)], dst_ref=xs_in.at[s, band(p)],
            send_sem=xs_send.at[s, p], recv_sem=xs_recv.at[s, p],
            device_id={"tp": across}, device_id_type=MESH,
        )

    def fin_copy(s, p):
        return pltpu.make_async_remote_copy(
            src_ref=red.at[s, band(p)], dst_ref=fin.at[own_q, band(p)],
            send_sem=fin_send.at[s, p], recv_sem=fin_recv.at[own_q, p],
            device_id={"ctx": s, "tp": c}, device_id_type=MESH,
        )

    def fin_arrival(i, p):
        return pltpu.make_async_remote_copy(
            src_ref=red.at[0, band(p)], dst_ref=fin.at[i, band(p)],
            send_sem=fin_send.at[0, p], recv_sem=fin_recv.at[i, p],
            device_id={"ctx": t}, device_id_type=MESH,
        )

    for i in range(tn):
        w_copy(i).start()
    res_copy.start()

    ids = jnp.concatenate(
        [pos_ref[...].reshape(1, rows), tid_ref[...].reshape(1, rows),
         jnp.zeros((126, rows), jnp.int32)], axis=0
    )
    idcol = jnp.concatenate(
        [ids, jnp.zeros((128, -rows % 128), jnp.int32)], axis=1
    ).T[:rows, :]
    tcol[...] = idcol[:, 1:2]
    offs = lax.broadcasted_iota(jnp.int32, (pad, 128), 0)
    blank = jnp.zeros((pad - half, 128), jnp.int32)
    for hh in range(2):
        place = (c if hh == 0 else blocks - 1 - c) * half
        posc = jnp.concatenate([idcol[hh * half:(hh + 1) * half, :], blank], axis=0)
        tok = place + offs
        lane = lax.broadcasted_iota(jnp.int32, (pad, 128), 1)
        both = jnp.where(lane == 0, tok - posc, tok)
        qrow[hh] = jnp.concatenate([both] * per, axis=0).T[0:8, :]

    def key_tokens(count, first):
        b = lax.broadcasted_iota(jnp.int32, (count, pad, 128), 0) + first
        r = lax.broadcasted_iota(jnp.int32, (count, pad, 128), 1)
        return jnp.where(r < half, b * half + r, blocks * rows).reshape(count * pad, 128)

    first = n - 1 - c

    def set_bias():
        for hh, count, base, where_to in ((0, n, 0, bias0), (1, n + 1, first, bias1)):
            def fill(i, _):
                span = pl.ds(pl.multiple_of(i * 128, 128), 128)
                tok = key_tokens(count, base)
                ok = (tok <= qrow[hh, 1:2, span]) & (tok >= qrow[hh, 0:1, span])
                where_to[:, span] = jnp.where(ok, 0.0, MASKED).astype(BF16)
                return 0

            lax.fori_loop(0, lanes // 128, fill, 0)

    zrow = jnp.zeros((pad - half, HEAD_SIZE), F32)

    def load_q(g):
        for h in range(per):
            at = (g * per + h) * HEAD_SIZE
            x = q_ref[:, at:at + HEAD_SIZE].astype(F32)
            for hh in range(2):
                qs[g, hh, h * pad:(h + 1) * pad, :] = jnp.concatenate(
                    [x[hh * half:(hh + 1) * half], zrow]
                ).astype(BF16)

    def attend(g):
        for hh, count, base, mask in ((0, n, 0, bias0), (1, n + 1, first, bias1)):
            keys = kvb[g, pl.ds(base, count), 0:pad, :].reshape(count * pad, HEAD_SIZE)
            vals = kvb[g, pl.ds(base, count), pad:2 * pad, :].reshape(count * pad, HEAD_SIZE)
            s = lax.dot_general(
                keys, qs[g, hh], (((1,), (1,)), ((), ())), preferred_element_type=F32
            ) * scale + mask[...].astype(F32)
            top = jnp.max(s, axis=0, keepdims=True)
            p = jnp.exp2(s - top)
            den = jnp.sum(p, axis=0, keepdims=True)
            o = lax.dot_general(
                vals, p.astype(BF16), (((0,), (0,)), ((), ())), preferred_element_type=F32
            )
            ot[hh] = (o * (1.0 / den)).T
        for h in range(per):
            q, at = divmod((g * per + h) * HEAD_SIZE, chunk)
            att[c, q, :, at:at + HEAD_SIZE] = jnp.concatenate(
                [ot[0, h * pad:h * pad + half, :], ot[1, h * pad:h * pad + half, :]]
            ).astype(BF16)
        for q in range(g * chunks // groups, (g + 1) * chunks // groups):
            for d in range(2):
                @pl.when(goes(c, d))
                def _():
                    att_copy(c, q, d).start()

    pl.semaphore_wait(barrier, tn - 1 + jnp.where((c == 0) | (c == n - 1), 1, 2))
    kv_own(0)
    set_bias()
    load_q(0)
    kv_take(0, (1,))
    for g in range(1, groups):
        kv_own(g)
    load_q(1)
    kv_take(0, range(2, n))
    attend(0)
    kv_take(1, range(1, n))
    attend(1)

    for i in range(tn):
        w_copy(i).wait()

    def column_of(j):
        k = jnp.where(lax.rem(j, 2) == 0, 1 - core, core)
        return 2 * k + jnp.where(j < 2, 1 - col, col)

    def project(s, side, q, whole):
        def column(j, _):
            i = column_of(j)
            if whole:
                prod = jnp.zeros((rows, cb), F32)
                for z in range(chunks):
                    prod = prod + jnp.dot(
                        att[s, z], wv[i, z * chunk:(z + 1) * chunk, :], preferred_element_type=F32
                    )
            else:
                prod = jnp.dot(
                    att[s, q], wv[i, q * chunk:(q + 1) * chunk, :], preferred_element_type=F32
                )
                if q > 0:
                    prod = acc[side, i] + prod
                if q < chunks - 1:
                    acc[side, i] = prod
                    return 0
            value = prod.astype(BF16)
            at = j // 2

            @pl.when(lax.rem(j, 2) == 0)
            def _():
                sib_out[s, at] = value
                sib_copy(s, at).start()

            @pl.when(lax.rem(j, 2) == 1)
            def _():
                keep[s, at] = value

            return 0

        lax.fori_loop(0, tn, column, 0)

    def pair_send(s):
        sib_copy(s, 0).wait_recv()
        for p in range(pieces):
            xs_out[s, band(p)] = (
                keep[s, 0, band(p)].astype(F32) + sib_in[s, 0, band(p)].astype(F32)
            ).astype(BF16)
            xs_copy(s, p).start()
        sib_copy(s, 1).wait_recv()

    def reduce_send(s):
        mine = (s == c) & (t == c)
        for p in range(pieces):
            xs_copy(s, p).wait_recv()
            summed = (
                keep[s, 1, band(p)].astype(F32) + sib_in[s, 1, band(p)].astype(F32)
                + xs_in[s, band(p)].astype(F32)
            ).astype(BF16)

            @pl.when(mine)
            def _():
                fin[own_q, band(p)] = summed

            @pl.when(jnp.logical_not(mine))
            def _():
                red[s, band(p)] = summed
                fin_copy(s, p).start()

    inner = (c > 0) & (c < n - 1)

    def att_drain(d):
        def one(s, _):
            @pl.when(goes(s, d))
            def _():
                for q in range(chunks):
                    att_copy(s, q, d).wait_send()

            return 0

        lax.fori_loop(0, n, one, 0)

    def both_sides(k, act):
        def one(side, _):
            s = c + k * (2 * side - 1)

            @pl.when((s >= 0) & (s < n))
            def _():
                act(s, side)

            return 0

        lax.fori_loop(0, 2, one, 0)

    project(c, 0, 0, True)

    def step(k, _):
        for q in range(chunks):
            def take(s, side):
                att_copy(s, q, 0).wait_recv()
                for d in range(2):
                    @pl.when(goes(s, d))
                    def _():
                        att_copy(s, q, d).start()

            both_sides(k, take)
            if q == 0:
                @pl.when(k == 1)
                def _():
                    pair_send(c)

                @pl.when(k > 1)
                def _():
                    both_sides(k - 1, lambda s, side: pair_send(s))
            both_sides(k, lambda s, side: project(s, side, q, False))
            if q == chunks - 1:
                @pl.when(k == 1)
                def _():
                    reduce_send(c)

                @pl.when(k > 1)
                def _():
                    def now(s, side):
                        @pl.when(jnp.logical_not(inner & ((s == 0) | (s == n - 1))))
                        def _():
                            reduce_send(s)

                    both_sides(k - 1, now)
        return 0

    lax.fori_loop(1, n, step, 0)

    @pl.when(inner)
    def _():
        near = jnp.where(c < n // 2, 0, n - 1)
        peer = n - 1 - c
        toward = jnp.where(c < n // 2, 1, 0)
        for d in range(2):
            @pl.when(toward == d)
            def _():
                att_drain(d)
        pl.semaphore_signal(go_sem, inc=1, device_id={"ctx": peer}, device_id_type=MESH)
        reduce_send(near)
        pl.semaphore_wait(go_sem, 1)
        reduce_send(n - 1 - near)

    both_sides(n - 1, lambda s, side: pair_send(s))
    both_sides(n - 1, lambda s, side: reduce_send(s))

    res_copy.wait()
    line = jnp.zeros((1, 128), F32)
    lane = lax.broadcasted_iota(jnp.int32, (piece, 128), 1)
    one = jnp.where(t == 0, 1.0, 0.0)
    for p in range(pieces):
        rng = slice(p * piece, (p + 1) * piece)
        score = jnp.zeros((piece, 1), F32)
        for i in range(tn):
            @pl.when(jnp.logical_not((c == t) & (own_q == i)))
            def _():
                fin_arrival(i, p).wait_recv()
            span = slice(i * cb, (i + 1) * cb)
            hidden = (resv[rng, span].astype(F32) + fin[i, rng, :].astype(F32)).astype(BF16)
            out_ref[rng, span] = hidden
            score = score + jnp.sum(
                hidden.astype(F32) * vh_ref[span].astype(F32).reshape(1, cb), axis=1, keepdims=True
            )
        turn = tcol[rng, :]
        terms = jnp.where(turn == lane, score, jnp.where(turn + 64 == lane, one, 0.0))
        line = line + jnp.sum(terms, axis=0, keepdims=True)
    me = c * tn + t
    tot[me] = line

    def tot_copy(j):
        other = lax.rem(me + j, n * tn)
        return pltpu.make_async_remote_copy(
            src_ref=tot.at[me], dst_ref=tot.at[me],
            send_sem=tot_send.at[other], recv_sem=tot_recv.at[me],
            device_id={"ctx": other // tn, "tp": lax.rem(other, tn)}, device_id_type=MESH,
        )

    def tot_arrival(j):
        other = lax.rem(me + j, n * tn)
        return pltpu.make_async_remote_copy(
            src_ref=tot.at[me], dst_ref=tot.at[other],
            send_sem=tot_send.at[other], recv_sem=tot_recv.at[other],
            device_id={"ctx": other // tn, "tp": lax.rem(other, tn)}, device_id_type=MESH,
        )

    def tot_start(j, _):
        tot_copy(j).start()
        return 0

    lax.fori_loop(1, n * tn, tot_start, 0)

    for d in range(n):
        @on(d)
        def _():
            for g in range(groups):
                for b in range(blocks):
                    held = owner(b) == d or any(
                        b in kv_arrivals(d, dist) for dist in range(1, n)
                    )
                    for way, e in ((0, d - 1), (1, d + 1)):
                        if held and carried(d, e, b):
                            kv_copy(g, b, e, way).wait_send()

    def drain(s, _):
        for j in range(2):
            sib_copy(s, j).wait_send()
        for p in range(pieces):
            xs_copy(s, p).wait_send()

        @pl.when(jnp.logical_not((s == c) & (t == c)))
        def _():
            for p in range(pieces):
                fin_copy(s, p).wait_send()

        return 0

    lax.fori_loop(0, n, drain, 0)
    for d in range(2):
        @pl.when(jnp.logical_not(inner & ((c < n // 2) == (d == 1))))
        def _():
            att_drain(d)


    def tot_wait(j, _):
        tot_arrival(j).wait_recv()
        tot_copy(j).wait_send()
        return 0

    lax.fori_loop(1, n * tn, tot_wait, 0)
    mean_ref[...] = jnp.sum(tot[...], axis=0)


def fused(
    n, tn, reach, queries, keys, values, residual, out_weight, value_head, segment_ids,
    positions, turn_ids
):
    rows, width = queries.shape
    groups = keys.shape[1] // HEAD_SIZE
    per = width // keys.shape[1]
    cols = out_weight.shape[1]
    cb = cols // tn
    pad = -(-(rows // 2) // 16) * 16
    pieces = 3 if rows % 48 == 0 else 1
    chunks = 2 * groups
    dims = (n, tn, rows, groups, per, cb, pieces, reach)
    vmem = pl.BlockSpec(memory_space=pltpu.VMEM)
    hbm = pl.BlockSpec(memory_space=pl.ANY)
    dma = pltpu.SemaphoreType.DMA
    out, means = pl.pallas_call(
        functools.partial(kernel, dims),
        out_shape=(
            jax.ShapeDtypeStruct((rows, cols), BF16),
            jax.ShapeDtypeStruct((1, 128), F32),
        ),
        in_specs=[vmem] * 6 + [hbm] * 2,
        out_specs=(vmem, vmem),
        scratch_shapes=[
            pltpu.VMEM((groups, 2 * n, 2 * pad, HEAD_SIZE), BF16),
            pltpu.VMEM((n * pad, per * pad), BF16),
            pltpu.VMEM(((n + 1) * pad, per * pad), BF16),
            pltpu.VMEM((rows, 1), jnp.int32),
            pltpu.VMEM((2, 8, per * pad), jnp.int32),
            pltpu.VMEM((groups, 2, per * pad, HEAD_SIZE), BF16),
            pltpu.VMEM((2, per * pad, HEAD_SIZE), F32),
            pltpu.VMEM((n, chunks, rows, width // chunks), BF16),
            pltpu.VMEM((tn, width, cb), BF16),
            pltpu.VMEM((2, tn, rows, cb), F32),
            pltpu.VMEM((n, 2, rows, cb), BF16),
            pltpu.VMEM((n, 2, rows, cb), BF16),
            pltpu.VMEM((n, 2, rows, cb), BF16),
            pltpu.VMEM((n, rows, cb), BF16),
            pltpu.VMEM((n, rows, cb), BF16),
            pltpu.VMEM((n, rows, cb), BF16),
            pltpu.VMEM((tn, rows, cb), BF16),
            pltpu.VMEM((rows, cols), BF16),
            pltpu.VMEM((n * tn, 1, 128), F32),
            dma((groups, 2 * n, 2)), dma((groups, 2 * n)),
            dma((2, n, chunks)), dma((n, chunks)),
            dma((n, 2)), dma((n, 2)),
            dma((n, pieces)), dma((n, pieces)),
            dma((n, pieces)), dma((tn, pieces)),
            dma((n * tn,)), dma((n * tn,)),
            dma((tn,)), dma(()), pltpu.SemaphoreType.REGULAR,
        ],
        compiler_params=pltpu.CompilerParams(
            collective_id=0, has_side_effects=True, vmem_limit_bytes=56 * 1024 * 1024
        ),
    )(
        keys, values, positions, turn_ids, value_head, queries, residual, out_weight,
    )
    return out, means[0, :TURNS] / jnp.maximum(means[0, 64:64 + TURNS], 1.0)


def body(n, tn, *args):
    queries, keys, weight = args[0], args[1], args[4]
    rows = queries.shape[0]
    per = queries.shape[1] // keys.shape[1]
    longest = 7 * n * rows // (4 * (TURNS // 4))
    reach = -(-(longest - 1) // (rows // 2))
    lanes = per * (-(-(rows // 2) // 16) * 16)
    fits = (
        n == tn == 4 and reach == n and rows % 16 == 0 and weight.shape[1] % (128 * tn) == 0
        and lanes % 128 == 0
    )
    if fits:
        return fused(n, tn, reach, *args)
    return shards(*args)


def solution(mesh):
    return jax.shard_map(
        functools.partial(body, mesh.shape["ctx"], mesh.shape["tp"]),
        mesh=mesh,
        in_specs=(
            P(("groups", "ctx"), "tp"),
            P(("groups", "ctx"), "tp"),
            P(("groups", "ctx"), "tp"),
            P(("groups", "ctx"), "tp"),
            P("tp", "ctx"),
            P("tp"),
            P(("groups", "ctx")),
            P(("groups", "ctx")),
            P(("groups", "ctx")),
        ),
        out_specs=(P(("groups", "ctx"), "tp"), P("groups")),
        check_vma=False,
    )
```

```python
import functools
import math

import jax
import jax.numpy as jnp
from jax import lax
from jax.experimental import pallas as pl
from jax.experimental.pallas import tpu as pltpu
from jax.sharding import PartitionSpec as P

HEAD_SIZE = 128
TURNS = 16


def shards(
    queries, keys, values, residual, out_weight, value_head, segment_ids, positions, turn_ids
):
    tok_rows = queries.shape[0]
    kv_heads = keys.shape[1] // HEAD_SIZE
    query_head_group = queries.shape[1] // keys.shape[1]
    query_rows = query_head_group * tok_rows
    score_scale = 1.0 / math.sqrt(HEAD_SIZE)
    grouped = (
        queries.reshape(tok_rows, kv_heads, query_head_group, HEAD_SIZE)
        .transpose(1, 2, 0, 3)
        .reshape(kv_heads, query_rows, HEAD_SIZE)
    )
    seg_rows = jnp.tile(segment_ids, query_head_group)
    pos_rows = jnp.tile(positions, query_head_group)

    def update(running, key_block, value_block, seg_block, pos_block):
        allowed = (seg_rows[:, None] == seg_block[None, :]) & (
            pos_block[None, :] <= pos_rows[:, None]
        )
        numerator, row_max, denominator = running
        scores = (
            jnp.einsum("hqd,khd->hqk", grouped, key_block, preferred_element_type=jnp.float32)
            * score_scale
        )
        scores = jnp.where(allowed[None], scores, -1e30)
        new_max = jnp.maximum(row_max, jnp.max(scores, axis=2))
        weights = jnp.where(allowed[None], jnp.exp(scores - new_max[..., None]), 0.0)
        factor = jnp.exp(row_max - new_max)
        denominator = denominator * factor + jnp.sum(weights, axis=2)
        product = jnp.einsum(
            "hqk,khd->hqd",
            weights.astype(jnp.bfloat16),
            value_block,
            preferred_element_type=jnp.float32,
        )
        numerator = numerator * factor[..., None] + product
        return (numerator, new_max, denominator)

    initial = (
        jnp.zeros((kv_heads, query_rows, HEAD_SIZE), jnp.float32),
        jnp.full((kv_heads, query_rows), -1e30, jnp.float32),
        jnp.zeros((kv_heads, query_rows), jnp.float32),
    )
    running = initial
    key_piece = lax.all_gather(keys, "ctx", axis=0, tiled=True)
    value_piece = lax.all_gather(values, "ctx", axis=0, tiled=True)
    seg_piece = lax.all_gather(segment_ids, "ctx", axis=0, tiled=True)
    pos_piece = lax.all_gather(positions, "ctx", axis=0, tiled=True)
    row_count = key_piece.shape[0]
    key_piece = key_piece.reshape(row_count, kv_heads, HEAD_SIZE)
    value_piece = value_piece.reshape(row_count, kv_heads, HEAD_SIZE)
    block_width = math.gcd(row_count, 512)
    block_steps = row_count // block_width
    stacked = (
        key_piece.reshape(block_steps, block_width, kv_heads, HEAD_SIZE),
        value_piece.reshape(block_steps, block_width, kv_heads, HEAD_SIZE),
        seg_piece.reshape(block_steps, block_width),
        pos_piece.reshape(block_steps, block_width),
    )

    def block_step(running_state, block_set):
        return (update(running_state, block_set[0], block_set[1], block_set[2], block_set[3]), None)

    running, _ = lax.scan(block_step, running, stacked)
    numerator, row_max, denominator = running
    attention = (numerator / denominator[..., None]).reshape(
        kv_heads, query_head_group, tok_rows, HEAD_SIZE
    )
    attention = (
        attention.transpose(2, 0, 1, 3)
        .reshape(tok_rows, kv_heads * query_head_group * HEAD_SIZE)
        .astype(jnp.bfloat16)
    )
    partial_value = jnp.dot(
        lax.all_gather(attention, "ctx", axis=0, tiled=True),
        out_weight,
        preferred_element_type=jnp.float32,
    ).astype(jnp.bfloat16)
    term_rows = lax.all_to_all(
        partial_value, "ctx", split_axis=0, concat_axis=1, tiled=True
    ).astype(jnp.float32)
    summed = lax.psum_scatter(
        term_rows.astype(jnp.bfloat16), "tp", scatter_dimension=1, tiled=True
    ).astype(jnp.float32)
    hidden_out = (residual.astype(jnp.float32) + summed).astype(jnp.bfloat16)
    token_score = jnp.dot(hidden_out, value_head, preferred_element_type=jnp.float32)
    one_hot = (turn_ids[:, None] == jnp.arange(TURNS, dtype=jnp.int32)[None, :]).astype(jnp.float32)
    local_sum = jnp.dot(token_score, one_hot, precision=lax.Precision.HIGHEST)
    local_count = jnp.where(lax.axis_index("tp") == 0, jnp.sum(one_hot, axis=0), 0.0)
    totals, counts = lax.psum((local_sum, local_count), ("ctx", "tp"))
    turn_means = totals / jnp.maximum(counts, 1.0)
    return (hidden_out, turn_means)


MESH = pl.DeviceIdType.MESH
F32 = jnp.float32
BF16 = jnp.bfloat16
MASKED = -1e30


def split(rows):
    first = -(-rows // 32) * 16
    return ((0, first), (first, rows))


def kernel(
    dims, k_ref, v_ref, pos_ref, tid_ref, vh_ref, q_ref, res_hbm, w_hbm,
    out_ref, mean_ref,
    kvb, bias0, bias1, tcol, qrow, qs, ot, att, wv, acc, keep, sib_out, sib_in,
    xs_out, xs_in, red, fin, resv, tot,
    kv_send, kv_recv, att_send, att_recv, sib_send, sib_recv, xs_send, xs_recv,
    fin_send, fin_recv, tot_send, tot_recv, w_sem, res_sem, go_sem,
    far_send, far_recv,
):
    n, tn, rows, groups, per, cb, reach = dims
    bands = split(rows)
    pieces = len(bands)
    half = rows // 2
    pad = -(-half // 16) * 16
    blocks = 2 * n
    lanes = per * pad
    chunks = groups * 2
    chunk = groups * per * HEAD_SIZE // chunks
    c = lax.axis_index("ctx")
    t = lax.axis_index("tp")
    core = lax.rem(t, 2)
    col = t // 2
    sibling = t + 1 - 2 * core
    across = lax.rem(t + 2, tn)
    own_q = 2 * core + col
    far_q = 2 * core + 1 - col
    scale = 1.0 / math.sqrt(HEAD_SIZE) * math.log2(math.e)

    barrier = pltpu.get_barrier_semaphore()

    for j in range(1, tn):
        pl.semaphore_signal(
            barrier, inc=1, device_id={"tp": lax.rem(t + j, tn)}, device_id_type=MESH
        )
    for away in (-1, 1):
        @pl.when((c + away >= 0) & (c + away < n))
        def _():
            pl.semaphore_signal(
                barrier, inc=1, device_id={"ctx": c + away}, device_id_type=MESH
            )

    def w_copy(i):
        return pltpu.make_async_copy(
            w_hbm.at[:, pl.ds(pl.multiple_of(i * cb, 128), cb)], wv.at[i], w_sem.at[i]
        )

    res_copy = pltpu.make_async_copy(res_hbm, resv, res_sem)

    def needs(d, b):
        late = blocks - 1 - d
        return d - reach <= b <= d or late - reach <= b <= late

    def owner(b):
        return b if b < n else blocks - 1 - b

    def carried(d, e, b):
        if not 0 <= e < n:
            return False
        beyond = range(0, e + 1) if e < d else range(e, n)
        behind = owner(b) >= d if e < d else owner(b) <= d
        return behind and any(needs(x, b) for x in beyond)

    def kv_copy(g, b, e, way):
        return pltpu.make_async_remote_copy(
            src_ref=kvb.at[g, b], dst_ref=kvb.at[g, b],
            send_sem=kv_send.at[g, b, way], recv_sem=kv_recv.at[g, b],
            device_id={"ctx": e}, device_id_type=MESH,
        )

    def on(d):
        return pl.when(c == d)

    def kv_pass(d, g, b):
        for way, e in ((0, d - 1), (1, d + 1)):
            if carried(d, e, b):
                kv_copy(g, b, e, way).start()

    def kv_arrivals(d, dist):
        return [
            b for b in range(blocks)
            if abs(owner(b) - d) == dist
            and (carried(d - 1, d, b) if owner(b) < d else carried(d + 1, d, b))
        ]

    def kv_own(g):
        for d in range(n):
            @on(d)
            def _():
                for b in (d, blocks - 1 - d):
                    kv_pass(d, g, b)

    def kv_take(g, dists):
        for d in range(n):
            @on(d)
            def _():
                for dist in dists:
                    for b in kv_arrivals(d, dist):
                        kv_copy(g, b, d, 0).wait_recv()
                        kv_pass(d, g, b)

    zeros = jnp.zeros((pad - half, HEAD_SIZE), F32)
    for g in range(groups):
        span = slice(g * HEAD_SIZE, (g + 1) * HEAD_SIZE)
        for ref, low in ((k_ref, 0), (v_ref, pad)):
            x = ref[:, span].astype(F32)
            kvb[g, c, low:low + pad, :] = jnp.concatenate([x[:half], zeros]).astype(BF16)
            kvb[g, blocks - 1 - c, low:low + pad, :] = jnp.concatenate(
                [x[half:], zeros]
            ).astype(BF16)
    for d in range(n):
        window = set(range(n)) | set(range(n - 1 - d, blocks - d))
        missing = [b for b in sorted(window) if owner(b) != d and not any(
            b in kv_arrivals(d, dist) for dist in range(1, n))]
        if missing:
            @on(d)
            def _():
                for g in range(groups):
                    for b in missing:
                        kvb[g, b] = jnp.zeros((2 * pad, HEAD_SIZE), BF16)


    def att_copy(s, q, d):
        return pltpu.make_async_remote_copy(
            src_ref=att.at[s, q], dst_ref=att.at[s, q],
            send_sem=att_send.at[d, s, q], recv_sem=att_recv.at[s, q],
            device_id={"ctx": c + 1 - 2 * d}, device_id_type=MESH,
        )

    def goes(s, d):
        if d == 0:
            return (s <= c) & (c < n - 1)
        return (s >= c) & (c > 0)

    def band(p):
        return slice(*bands[p])

    def far_copy(s, q, p, d):
        return pltpu.make_async_remote_copy(
            src_ref=att.at[s, q, band(p)], dst_ref=att.at[s, q, band(p)],
            send_sem=far_send.at[q, p], recv_sem=far_recv.at[q, p],
            device_id={"ctx": c + 1 - 2 * d}, device_id_type=MESH,
        )

    def sib_copy(s, j, p):
        return pltpu.make_async_remote_copy(
            src_ref=sib_out.at[s, j, band(p)], dst_ref=sib_in.at[s, j, band(p)],
            send_sem=sib_send.at[s, j, p], recv_sem=sib_recv.at[s, j, p],
            device_id={"tp": sibling}, device_id_type=MESH,
        )

    def xs_copy(s, p):
        return pltpu.make_async_remote_copy(
            src_ref=xs_out.at[s, band(p)], dst_ref=xs_in.at[s, band(p)],
            send_sem=xs_send.at[s, p], recv_sem=xs_recv.at[s, p],
            device_id={"tp": across}, device_id_type=MESH,
        )

    def fin_copy(s, p):
        return pltpu.make_async_remote_copy(
            src_ref=red.at[s, band(p)], dst_ref=fin.at[own_q, band(p)],
            send_sem=fin_send.at[s, p], recv_sem=fin_recv.at[own_q, p],
            device_id={"ctx": s, "tp": c}, device_id_type=MESH,
        )

    def fin_arrival(i, p):
        return pltpu.make_async_remote_copy(
            src_ref=red.at[0, band(p)], dst_ref=fin.at[i, band(p)],
            send_sem=fin_send.at[0, p], recv_sem=fin_recv.at[i, p],
            device_id={"ctx": t}, device_id_type=MESH,
        )

    for i in range(tn):
        w_copy(i).start()
    res_copy.start()

    ids = jnp.concatenate(
        [pos_ref[...].reshape(1, rows), tid_ref[...].reshape(1, rows),
         jnp.zeros((126, rows), jnp.int32)], axis=0
    )
    idcol = jnp.concatenate(
        [ids, jnp.zeros((128, -rows % 128), jnp.int32)], axis=1
    ).T[:rows, :]
    tcol[...] = idcol[:, 1:2]
    offs = lax.broadcasted_iota(jnp.int32, (pad, 128), 0)
    blank = jnp.zeros((pad - half, 128), jnp.int32)
    for hh in range(2):
        place = (c if hh == 0 else blocks - 1 - c) * half
        posc = jnp.concatenate([idcol[hh * half:(hh + 1) * half, :], blank], axis=0)
        tok = place + offs
        lane = lax.broadcasted_iota(jnp.int32, (pad, 128), 1)
        both = jnp.where(lane == 0, tok - posc, tok)
        qrow[hh] = jnp.concatenate([both] * per, axis=0).T[0:8, :]

    first = n - 1 - c
    for hh, count, base, mask in ((0, n, 0, bias0), (1, n + 1, first, bias1)):
        b = lax.broadcasted_iota(jnp.int32, (count, pad, lanes), 0) + base
        r = lax.broadcasted_iota(jnp.int32, (count, pad, lanes), 1)
        tok = jnp.where(r < half, b * half + r, blocks * rows).reshape(count * pad, lanes)
        ok = (tok <= qrow[hh, 1:2, :]) & (tok >= qrow[hh, 0:1, :])
        mask[...] = jnp.where(ok, 0.0, MASKED).astype(BF16)

    zrow = jnp.zeros((pad - half, HEAD_SIZE), F32)

    def load_q(g):
        for h in range(per):
            at = (g * per + h) * HEAD_SIZE
            x = q_ref[:, at:at + HEAD_SIZE].astype(F32)
            for hh in range(2):
                qs[g, hh, h * pad:(h + 1) * pad, :] = jnp.concatenate(
                    [x[hh * half:(hh + 1) * half], zrow]
                ).astype(BF16)

    def attend(g):
        for hh, count, base, mask in ((0, n, 0, bias0), (1, n + 1, first, bias1)):
            keys = kvb[g, pl.ds(base, count), 0:pad, :].reshape(count * pad, HEAD_SIZE)
            vals = kvb[g, pl.ds(base, count), pad:2 * pad, :].reshape(count * pad, HEAD_SIZE)
            s = lax.dot_general(
                keys, qs[g, hh], (((1,), (1,)), ((), ())), preferred_element_type=F32
            ) * scale + mask[...].astype(F32)
            top = jnp.max(s, axis=0, keepdims=True)
            p = jnp.exp2(s - top)
            den = jnp.sum(p, axis=0, keepdims=True)
            o = lax.dot_general(
                vals, p.astype(BF16), (((0,), (0,)), ((), ())), preferred_element_type=F32
            )
            ot[hh] = (o * (1.0 / den)).T
        for h in range(per):
            q, at = divmod((g * per + h) * HEAD_SIZE, chunk)
            att[c, q, :, at:at + HEAD_SIZE] = jnp.concatenate(
                [ot[0, h * pad:h * pad + half, :], ot[1, h * pad:h * pad + half, :]]
            ).astype(BF16)
        for q in range(g * chunks // groups, (g + 1) * chunks // groups):
            for d in range(2):
                @pl.when(goes(c, d))
                def _():
                    att_copy(c, q, d).start()

    pl.semaphore_wait(barrier, tn - 1 + jnp.where((c == 0) | (c == n - 1), 1, 2))
    kv_own(0)
    load_q(0)
    kv_take(0, (1,))
    for g in range(1, groups):
        kv_own(g)
    load_q(1)
    kv_take(0, range(2, n))
    attend(0)
    kv_take(1, range(1, n))
    attend(1)

    for i in range(tn):
        w_copy(i).wait()

    def column_of(j):
        k = jnp.where(lax.rem(j, 2) == 0, 1 - core, core)
        return 2 * k + jnp.where(j < 2, 1 - col, col)

    def project(s, side, q, whole):
        def column(j, _):
            i = column_of(j)
            if whole:
                prod = jnp.zeros((rows, cb), F32)
                for z in range(chunks):
                    prod = prod + jnp.dot(
                        att[s, z], wv[i, z * chunk:(z + 1) * chunk, :], preferred_element_type=F32
                    )
            else:
                prod = jnp.dot(
                    att[s, q], wv[i, q * chunk:(q + 1) * chunk, :], preferred_element_type=F32
                )
                if q > 0:
                    prod = acc[side, i] + prod
                if q < chunks - 1:
                    acc[side, i] = prod
                    return 0
            value = prod.astype(BF16)
            at = j // 2

            @pl.when(lax.rem(j, 2) == 0)
            def _():
                sib_out[s, at] = value
                for p in range(pieces):
                    sib_copy(s, at, p).start()

            @pl.when(lax.rem(j, 2) == 1)
            def _():
                keep[s, at] = value

            return 0

        lax.fori_loop(0, tn, column, 0)

    def far_project(s, q, p):
        def column(j, _):
            i = column_of(j)
            prod = acc[0, i, band(p)] + jnp.dot(
                att[s, q, band(p)],
                wv[i, pl.ds(pl.multiple_of(q * chunk, chunk), chunk), :],
                preferred_element_type=F32,
            )
            acc[0, i, band(p)] = prod
            at = j // 2

            @pl.when((q == chunks - 1) & (lax.rem(j, 2) == 0))
            def _():
                sib_out[s, at, band(p)] = prod.astype(BF16)
                sib_copy(s, at, p).start()

            @pl.when((q == chunks - 1) & (lax.rem(j, 2) == 1))
            def _():
                keep[s, at, band(p)] = prod.astype(BF16)

            return 0

        lax.fori_loop(0, tn, column, 0)

    def pair_band(s, p):
        sib_copy(s, 0, p).wait_recv()
        xs_out[s, band(p)] = (
            keep[s, 0, band(p)].astype(F32) + sib_in[s, 0, band(p)].astype(F32)
        ).astype(BF16)
        xs_copy(s, p).start()
        sib_copy(s, 1, p).wait_recv()

    def pair_send(s):
        for p in range(pieces):
            pair_band(s, p)

    def reduce_band(s, p):
        mine = (s == c) & (t == c)
        xs_copy(s, p).wait_recv()
        summed = (
            keep[s, 1, band(p)].astype(F32) + sib_in[s, 1, band(p)].astype(F32)
            + xs_in[s, band(p)].astype(F32)
        ).astype(BF16)

        @pl.when(mine)
        def _():
            fin[own_q, band(p)] = summed

        @pl.when(jnp.logical_not(mine))
        def _():
            red[s, band(p)] = summed
            fin_copy(s, p).start()

    def reduce_send(s):
        for p in range(pieces):
            reduce_band(s, p)

    inner = (c > 0) & (c < n - 1)

    near = jnp.where(c < n // 2, 0, n - 1)
    far = n - 1 - near

    def passes_far(s):
        return inner & (s == far)

    def att_drain(d):
        def one(s, _):
            @pl.when(goes(s, d) & jnp.logical_not(passes_far(s)))
            def _():
                for q in range(chunks):
                    att_copy(s, q, d).wait_send()

            @pl.when(goes(s, d) & passes_far(s))
            def _():
                for q in range(chunks):
                    for p in range(pieces):
                        far_copy(s, q, p, d).wait_send()

            return 0

        lax.fori_loop(0, n, one, 0)

    def both_sides(k, act):
        def one(side, _):
            s = c + k * (2 * side - 1)

            @pl.when((s >= 0) & (s < n))
            def _():
                act(s, side)

            return 0

        lax.fori_loop(0, 2, one, 0)

    project(c, 0, 0, True)

    def step(k, _):
        for q in range(chunks):
            def take(s, side):
                att_copy(s, q, 0).wait_recv()
                for d in range(2):
                    @pl.when(goes(s, d) & jnp.logical_not(passes_far(s)))
                    def _():
                        att_copy(s, q, d).start()

                    @pl.when(goes(s, d) & passes_far(s))
                    def _():
                        far_copy(s, q, 0, d).start()
                        if q == chunks - 1:
                            for p in range(1, pieces):
                                for z in range(chunks):
                                    far_copy(s, z, p, d).start()

            both_sides(k, take)
            if q == 0:
                @pl.when(k == 1)
                def _():
                    pair_send(c)

                @pl.when(k > 1)
                def _():
                    both_sides(k - 1, lambda s, side: pair_send(s))
            both_sides(k, lambda s, side: project(s, side, q, False))
            if q == chunks - 1:
                @pl.when(k == 1)
                def _():
                    reduce_send(c)

                @pl.when(k > 1)
                def _():
                    def now(s, side):
                        @pl.when(jnp.logical_not(inner & (s == near)))
                        def _():
                            reduce_send(s)

                    both_sides(k - 1, now)
        return 0

    lax.fori_loop(1, n - 1, step, 0)
    both_sides(n - 2, lambda s, side: pair_send(s))

    @pl.when(inner)
    def _():
        for d in range(2):
            @pl.when((c < n // 2) == (d == 1))
            def _():
                att_drain(d)
        pl.semaphore_signal(go_sem, inc=1, device_id={"ctx": n - 1 - c}, device_id_type=MESH)
        reduce_send(near)
        pl.semaphore_wait(go_sem, 1)
        reduce_send(far)

    @pl.when(jnp.logical_not(inner))
    def _():
        acc[0] = jnp.zeros(acc.shape[1:], F32)

        def far_step(p):
            def one(q, _):
                far_copy(far, q, p, 0).wait_recv()
                far_project(far, q, p)
                return 0

            return one

        lax.fori_loop(0, chunks, far_step(0), 0)
        both_sides(n - 2, lambda s, side: reduce_send(s))
        pair_band(far, 0)
        lax.fori_loop(0, chunks - 1, far_step(1), 0)
        reduce_band(far, 0)
        lax.fori_loop(chunks - 1, chunks, far_step(1), 0)
        pair_band(far, 1)
        reduce_band(far, 1)

    res_copy.wait()
    line = jnp.zeros((1, 128), F32)
    one = jnp.where(t == 0, 1.0, 0.0)
    for p in range(pieces):
        rng = band(p)
        piece = bands[p][1] - bands[p][0]
        lane = lax.broadcasted_iota(jnp.int32, (piece, 128), 1)
        score = jnp.zeros((piece, 1), F32)
        for i in range(tn):
            @pl.when(jnp.logical_not((c == t) & (own_q == i)))
            def _():
                fin_arrival(i, p).wait_recv()
            span = slice(i * cb, (i + 1) * cb)
            hidden = (resv[rng, span].astype(F32) + fin[i, rng, :].astype(F32)).astype(BF16)
            out_ref[rng, span] = hidden
            score = score + jnp.sum(
                hidden.astype(F32) * vh_ref[span].astype(F32).reshape(1, cb), axis=1, keepdims=True
            )
        turn = tcol[rng, :]
        terms = jnp.where(turn == lane, score, jnp.where(turn + 64 == lane, one, 0.0))
        line = line + jnp.sum(terms, axis=0, keepdims=True)
    me = c * tn + t
    tot[me] = line

    def tot_copy(j):
        other = lax.rem(me + j, n * tn)
        return pltpu.make_async_remote_copy(
            src_ref=tot.at[me], dst_ref=tot.at[me],
            send_sem=tot_send.at[other], recv_sem=tot_recv.at[me],
            device_id={"ctx": other // tn, "tp": lax.rem(other, tn)}, device_id_type=MESH,
        )

    def tot_arrival(j):
        other = lax.rem(me + j, n * tn)
        return pltpu.make_async_remote_copy(
            src_ref=tot.at[me], dst_ref=tot.at[other],
            send_sem=tot_send.at[other], recv_sem=tot_recv.at[other],
            device_id={"ctx": other // tn, "tp": lax.rem(other, tn)}, device_id_type=MESH,
        )

    def tot_start(j, _):
        tot_copy(j).start()
        return 0

    lax.fori_loop(1, n * tn, tot_start, 0)

    for d in range(n):
        @on(d)
        def _():
            for g in range(groups):
                for b in range(blocks):
                    held = owner(b) == d or any(
                        b in kv_arrivals(d, dist) for dist in range(1, n)
                    )
                    for way, e in ((0, d - 1), (1, d + 1)):
                        if held and carried(d, e, b):
                            kv_copy(g, b, e, way).wait_send()

    def drain(s, _):
        for j in range(2):
            for p in range(pieces):
                sib_copy(s, j, p).wait_send()
        for p in range(pieces):
            xs_copy(s, p).wait_send()

        @pl.when(jnp.logical_not((s == c) & (t == c)))
        def _():
            for p in range(pieces):
                fin_copy(s, p).wait_send()

        return 0

    lax.fori_loop(0, n, drain, 0)
    for d in range(2):
        @pl.when(jnp.logical_not(inner & ((c < n // 2) == (d == 1))))
        def _():
            att_drain(d)


    def tot_wait(j, _):
        tot_arrival(j).wait_recv()
        tot_copy(j).wait_send()
        return 0

    lax.fori_loop(1, n * tn, tot_wait, 0)
    total = jnp.sum(tot[...], axis=0)
    mean_ref[...] = (
        total[:, :TURNS] / jnp.maximum(total[:, 64:64 + TURNS], 1.0)
    ).reshape(TURNS)


def fused(
    n, tn, reach, queries, keys, values, residual, out_weight, value_head, segment_ids,
    positions, turn_ids
):
    rows, width = queries.shape
    groups = keys.shape[1] // HEAD_SIZE
    per = width // keys.shape[1]
    cols = out_weight.shape[1]
    cb = cols // tn
    pad = -(-(rows // 2) // 16) * 16
    pieces = len(split(rows))
    chunks = 2 * groups
    dims = (n, tn, rows, groups, per, cb, reach)
    vmem = pl.BlockSpec(memory_space=pltpu.VMEM)
    hbm = pl.BlockSpec(memory_space=pl.ANY)
    dma = pltpu.SemaphoreType.DMA
    out, means = pl.pallas_call(
        functools.partial(kernel, dims),
        out_shape=(
            jax.ShapeDtypeStruct((rows, cols), BF16),
            jax.ShapeDtypeStruct((TURNS,), F32),
        ),
        in_specs=[vmem] * 6 + [hbm] * 2,
        out_specs=(vmem, vmem),
        scratch_shapes=[
            pltpu.VMEM((groups, 2 * n, 2 * pad, HEAD_SIZE), BF16),
            pltpu.VMEM((n * pad, per * pad), BF16),
            pltpu.VMEM(((n + 1) * pad, per * pad), BF16),
            pltpu.VMEM((rows, 1), jnp.int32),
            pltpu.VMEM((2, 8, per * pad), jnp.int32),
            pltpu.VMEM((groups, 2, per * pad, HEAD_SIZE), BF16),
            pltpu.VMEM((2, per * pad, HEAD_SIZE), F32),
            pltpu.VMEM((n, chunks, rows, width // chunks), BF16),
            pltpu.VMEM((tn, width, cb), BF16),
            pltpu.VMEM((2, tn, rows, cb), F32),
            pltpu.VMEM((n, 2, rows, cb), BF16),
            pltpu.VMEM((n, 2, rows, cb), BF16),
            pltpu.VMEM((n, 2, rows, cb), BF16),
            pltpu.VMEM((n, rows, cb), BF16),
            pltpu.VMEM((n, rows, cb), BF16),
            pltpu.VMEM((n, rows, cb), BF16),
            pltpu.VMEM((tn, rows, cb), BF16),
            pltpu.VMEM((rows, cols), BF16),
            pltpu.VMEM((n * tn, 1, 128), F32),
            dma((groups, 2 * n, 2)), dma((groups, 2 * n)),
            dma((2, n, chunks)), dma((n, chunks)),
            dma((n, 2, pieces)), dma((n, 2, pieces)),
            dma((n, pieces)), dma((n, pieces)),
            dma((n, pieces)), dma((tn, pieces)),
            dma((n * tn,)), dma((n * tn,)),
            dma((tn,)), dma(()), pltpu.SemaphoreType.REGULAR,
            dma((chunks, pieces)), dma((chunks, pieces)),
        ],
        compiler_params=pltpu.CompilerParams(
            collective_id=0, has_side_effects=True, vmem_limit_bytes=56 * 1024 * 1024
        ),
    )(
        keys, values, positions, turn_ids, value_head, queries, residual, out_weight,
    )
    return out, means


def body(n, tn, *args):
    queries, keys, weight = args[0], args[1], args[4]
    rows = queries.shape[0]
    per = queries.shape[1] // keys.shape[1]
    longest = 7 * n * rows // (4 * (TURNS // 4))
    reach = -(-(longest - 1) // (rows // 2))
    lanes = per * (-(-(rows // 2) // 16) * 16)
    fits = (
        n == tn == 4 and reach == n and rows % 16 == 0 and weight.shape[1] % (128 * tn) == 0
        and lanes % 128 == 0
    )
    if fits:
        return fused(n, tn, reach, *args)
    return shards(*args)


def solution(mesh):
    return jax.shard_map(
        functools.partial(body, mesh.shape["ctx"], mesh.shape["tp"]),
        mesh=mesh,
        in_specs=(
            P(("groups", "ctx"), "tp"),
            P(("groups", "ctx"), "tp"),
            P(("groups", "ctx"), "tp"),
            P(("groups", "ctx"), "tp"),
            P("tp", "ctx"),
            P("tp"),
            P(("groups", "ctx")),
            P(("groups", "ctx")),
            P(("groups", "ctx")),
        ),
        out_specs=(P(("groups", "ctx"), "tp"), P("groups")),
        check_vma=False,
    )
```

```python
import functools
import math

import jax
import jax.numpy as jnp
from jax import lax
from jax.experimental import pallas as pl
from jax.experimental.pallas import tpu as pltpu
from jax.sharding import PartitionSpec as P

HEAD_SIZE = 128
TURNS = 16


def shards(
    queries, keys, values, residual, out_weight, value_head, segment_ids, positions, turn_ids
):
    tok_rows = queries.shape[0]
    kv_heads = keys.shape[1] // HEAD_SIZE
    query_head_group = queries.shape[1] // keys.shape[1]
    query_rows = query_head_group * tok_rows
    score_scale = 1.0 / math.sqrt(HEAD_SIZE)
    grouped = (
        queries.reshape(tok_rows, kv_heads, query_head_group, HEAD_SIZE)
        .transpose(1, 2, 0, 3)
        .reshape(kv_heads, query_rows, HEAD_SIZE)
    )
    seg_rows = jnp.tile(segment_ids, query_head_group)
    pos_rows = jnp.tile(positions, query_head_group)

    def update(running, key_block, value_block, seg_block, pos_block):
        allowed = (seg_rows[:, None] == seg_block[None, :]) & (
            pos_block[None, :] <= pos_rows[:, None]
        )
        numerator, row_max, denominator = running
        scores = (
            jnp.einsum("hqd,khd->hqk", grouped, key_block, preferred_element_type=jnp.float32)
            * score_scale
        )
        scores = jnp.where(allowed[None], scores, -1e30)
        new_max = jnp.maximum(row_max, jnp.max(scores, axis=2))
        weights = jnp.where(allowed[None], jnp.exp(scores - new_max[..., None]), 0.0)
        factor = jnp.exp(row_max - new_max)
        denominator = denominator * factor + jnp.sum(weights, axis=2)
        product = jnp.einsum(
            "hqk,khd->hqd",
            weights.astype(jnp.bfloat16),
            value_block,
            preferred_element_type=jnp.float32,
        )
        numerator = numerator * factor[..., None] + product
        return (numerator, new_max, denominator)

    initial = (
        jnp.zeros((kv_heads, query_rows, HEAD_SIZE), jnp.float32),
        jnp.full((kv_heads, query_rows), -1e30, jnp.float32),
        jnp.zeros((kv_heads, query_rows), jnp.float32),
    )
    running = initial
    key_piece = lax.all_gather(keys, "ctx", axis=0, tiled=True)
    value_piece = lax.all_gather(values, "ctx", axis=0, tiled=True)
    seg_piece = lax.all_gather(segment_ids, "ctx", axis=0, tiled=True)
    pos_piece = lax.all_gather(positions, "ctx", axis=0, tiled=True)
    row_count = key_piece.shape[0]
    key_piece = key_piece.reshape(row_count, kv_heads, HEAD_SIZE)
    value_piece = value_piece.reshape(row_count, kv_heads, HEAD_SIZE)
    block_width = math.gcd(row_count, 512)
    block_steps = row_count // block_width
    stacked = (
        key_piece.reshape(block_steps, block_width, kv_heads, HEAD_SIZE),
        value_piece.reshape(block_steps, block_width, kv_heads, HEAD_SIZE),
        seg_piece.reshape(block_steps, block_width),
        pos_piece.reshape(block_steps, block_width),
    )

    def block_step(running_state, block_set):
        return (update(running_state, block_set[0], block_set[1], block_set[2], block_set[3]), None)

    running, _ = lax.scan(block_step, running, stacked)
    numerator, row_max, denominator = running
    attention = (numerator / denominator[..., None]).reshape(
        kv_heads, query_head_group, tok_rows, HEAD_SIZE
    )
    attention = (
        attention.transpose(2, 0, 1, 3)
        .reshape(tok_rows, kv_heads * query_head_group * HEAD_SIZE)
        .astype(jnp.bfloat16)
    )
    partial_value = jnp.dot(
        lax.all_gather(attention, "ctx", axis=0, tiled=True),
        out_weight,
        preferred_element_type=jnp.float32,
    ).astype(jnp.bfloat16)
    term_rows = lax.all_to_all(
        partial_value, "ctx", split_axis=0, concat_axis=1, tiled=True
    ).astype(jnp.float32)
    summed = lax.psum_scatter(
        term_rows.astype(jnp.bfloat16), "tp", scatter_dimension=1, tiled=True
    ).astype(jnp.float32)
    hidden_out = (residual.astype(jnp.float32) + summed).astype(jnp.bfloat16)
    token_score = jnp.dot(hidden_out, value_head, preferred_element_type=jnp.float32)
    one_hot = (turn_ids[:, None] == jnp.arange(TURNS, dtype=jnp.int32)[None, :]).astype(jnp.float32)
    local_sum = jnp.dot(token_score, one_hot, precision=lax.Precision.HIGHEST)
    local_count = jnp.where(lax.axis_index("tp") == 0, jnp.sum(one_hot, axis=0), 0.0)
    totals, counts = lax.psum((local_sum, local_count), ("ctx", "tp"))
    turn_means = totals / jnp.maximum(counts, 1.0)
    return (hidden_out, turn_means)


MESH = pl.DeviceIdType.MESH
F32 = jnp.float32
BF16 = jnp.bfloat16
MASKED = -1e30


def split(rows):
    first = -(-rows // 32) * 16
    return ((0, first), (first, rows))


def kernel(
    dims, k_ref, v_ref, pos_ref, tid_ref, vh_ref, q_ref, res_hbm, w_hbm,
    out_ref, mean_ref,
    kvb, bias0, bias1, tcol, qrow, qs, ot, att, wv, acc, keep, sib_out, sib_in,
    xs_out, xs_in, red, fin, resv, tot,
    kv_send, kv_recv, att_send, att_recv, sib_send, sib_recv, xs_send, xs_recv,
    fin_send, fin_recv, tot_send, tot_recv, w_sem, res_sem, go_sem,
    far_send, far_recv, ys_send, ys_recv, two_send, ys_out, ys_in, two,
):
    n, tn, rows, groups, per, cb, reach = dims
    bands = split(rows)
    pieces = len(bands)
    half = rows // 2
    pad = -(-half // 16) * 16
    blocks = 2 * n
    lanes = per * pad
    chunks = groups * 2
    chunk = groups * per * HEAD_SIZE // chunks
    c = lax.axis_index("ctx")
    t = lax.axis_index("tp")
    core = lax.rem(t, 2)
    col = t // 2
    sibling = t + 1 - 2 * core
    across = lax.rem(t + 2, tn)
    own_q = 2 * core + col
    far_q = 2 * core + 1 - col
    inner = (c > 0) & (c < n - 1)
    keeper = col == c // 2
    scale = 1.0 / math.sqrt(HEAD_SIZE) * math.log2(math.e)

    barrier = pltpu.get_barrier_semaphore()

    for j in range(1, tn):
        pl.semaphore_signal(
            barrier, inc=1, device_id={"tp": lax.rem(t + j, tn)}, device_id_type=MESH
        )
    for away in (-1, 1):
        @pl.when((c + away >= 0) & (c + away < n))
        def _():
            pl.semaphore_signal(
                barrier, inc=1, device_id={"ctx": c + away}, device_id_type=MESH
            )

    def w_copy(i):
        return pltpu.make_async_copy(
            w_hbm.at[:, pl.ds(pl.multiple_of(i * cb, 128), cb)], wv.at[i], w_sem.at[i]
        )

    res_copy = pltpu.make_async_copy(res_hbm, resv, res_sem)

    def needs(d, b):
        late = blocks - 1 - d
        return d - reach <= b <= d or late - reach <= b <= late

    def owner(b):
        return b if b < n else blocks - 1 - b

    def carried(d, e, b):
        if not 0 <= e < n:
            return False
        beyond = range(0, e + 1) if e < d else range(e, n)
        behind = owner(b) >= d if e < d else owner(b) <= d
        return behind and any(needs(x, b) for x in beyond)

    def kv_copy(g, b, e, way):
        return pltpu.make_async_remote_copy(
            src_ref=kvb.at[g, b], dst_ref=kvb.at[g, b],
            send_sem=kv_send.at[g, b, way], recv_sem=kv_recv.at[g, b],
            device_id={"ctx": e}, device_id_type=MESH,
        )

    def on(d):
        return pl.when(c == d)

    def kv_pass(d, g, b):
        for way, e in ((0, d - 1), (1, d + 1)):
            if carried(d, e, b):
                kv_copy(g, b, e, way).start()

    def kv_arrivals(d, dist):
        return [
            b for b in range(blocks)
            if abs(owner(b) - d) == dist
            and (carried(d - 1, d, b) if owner(b) < d else carried(d + 1, d, b))
        ]

    def kv_own(g):
        for d in range(n):
            @on(d)
            def _():
                for b in (d, blocks - 1 - d):
                    kv_pass(d, g, b)

    def kv_take(g, dists):
        for d in range(n):
            @on(d)
            def _():
                for dist in dists:
                    for b in kv_arrivals(d, dist):
                        kv_copy(g, b, d, 0).wait_recv()
                        kv_pass(d, g, b)

    zeros = jnp.zeros((pad - half, HEAD_SIZE), F32)
    for g in range(groups):
        span = slice(g * HEAD_SIZE, (g + 1) * HEAD_SIZE)
        for ref, low in ((k_ref, 0), (v_ref, pad)):
            x = ref[:, span].astype(F32)
            kvb[g, c, low:low + pad, :] = jnp.concatenate([x[:half], zeros]).astype(BF16)
            kvb[g, blocks - 1 - c, low:low + pad, :] = jnp.concatenate(
                [x[half:], zeros]
            ).astype(BF16)
    for d in range(n):
        window = set(range(n)) | set(range(n - 1 - d, blocks - d))
        missing = [b for b in sorted(window) if owner(b) != d and not any(
            b in kv_arrivals(d, dist) for dist in range(1, n))]
        if missing:
            @on(d)
            def _():
                for g in range(groups):
                    for b in missing:
                        kvb[g, b] = jnp.zeros((2 * pad, HEAD_SIZE), BF16)


    def att_copy(s, q, d):
        return pltpu.make_async_remote_copy(
            src_ref=att.at[s, q], dst_ref=att.at[s, q],
            send_sem=att_send.at[d, s, q], recv_sem=att_recv.at[s, q],
            device_id={"ctx": c + 1 - 2 * d}, device_id_type=MESH,
        )

    def goes(s, d):
        if d == 0:
            return (s <= c) & (c < n - 1)
        return (s >= c) & (c > 0)

    def band(p):
        return slice(*bands[p])

    def far_copy(s, q, p, d):
        return pltpu.make_async_remote_copy(
            src_ref=att.at[s, q, band(p)], dst_ref=att.at[s, q, band(p)],
            send_sem=far_send.at[q, p], recv_sem=far_recv.at[q, p],
            device_id={"ctx": c + 1 - 2 * d}, device_id_type=MESH,
        )

    def sib_copy(s, j, p):
        return pltpu.make_async_remote_copy(
            src_ref=sib_out.at[s, j, band(p)], dst_ref=sib_in.at[s, j, band(p)],
            send_sem=sib_send.at[s, j, p], recv_sem=sib_recv.at[s, j, p],
            device_id={"tp": sibling}, device_id_type=MESH,
        )

    def xs_copy(s, p):
        return pltpu.make_async_remote_copy(
            src_ref=xs_out.at[s, band(p)], dst_ref=xs_in.at[s, band(p)],
            send_sem=xs_send.at[s, p], recv_sem=xs_recv.at[s, p],
            device_id={"tp": across}, device_id_type=MESH,
        )

    def fin_copy(s, p):
        return pltpu.make_async_remote_copy(
            src_ref=red.at[s, band(p)], dst_ref=fin.at[own_q, band(p)],
            send_sem=fin_send.at[s, p], recv_sem=fin_recv.at[own_q, p],
            device_id={"ctx": s, "tp": c}, device_id_type=MESH,
        )

    def ys_copy(s, p):
        return pltpu.make_async_remote_copy(
            src_ref=ys_out.at[s, band(p)], dst_ref=ys_in.at[s, band(p)],
            send_sem=ys_send.at[s, p], recv_sem=ys_recv.at[s, p],
            device_id={"tp": across}, device_id_type=MESH,
        )

    def two_copy(s, p):
        return pltpu.make_async_remote_copy(
            src_ref=two.at[s, band(p)], dst_ref=fin.at[far_q, band(p)],
            send_sem=two_send.at[s, p], recv_sem=fin_recv.at[far_q, p],
            device_id={"ctx": s, "tp": c}, device_id_type=MESH,
        )

    def gathers(s):
        return inner & ((s == 0) | (s == n - 1))

    def fin_arrival(i, p):
        return pltpu.make_async_remote_copy(
            src_ref=red.at[0, band(p)], dst_ref=fin.at[i, band(p)],
            send_sem=fin_send.at[0, p], recv_sem=fin_recv.at[i, p],
            device_id={"ctx": t}, device_id_type=MESH,
        )

    for i in range(tn):
        w_copy(i).start()
    res_copy.start()

    ids = jnp.concatenate(
        [pos_ref[...].reshape(1, rows), tid_ref[...].reshape(1, rows),
         jnp.zeros((126, rows), jnp.int32)], axis=0
    )
    idcol = jnp.concatenate(
        [ids, jnp.zeros((128, -rows % 128), jnp.int32)], axis=1
    ).T[:rows, :]
    tcol[...] = idcol[:, 1:2]
    offs = lax.broadcasted_iota(jnp.int32, (pad, 128), 0)
    blank = jnp.zeros((pad - half, 128), jnp.int32)
    for hh in range(2):
        place = (c if hh == 0 else blocks - 1 - c) * half
        posc = jnp.concatenate([idcol[hh * half:(hh + 1) * half, :], blank], axis=0)
        tok = place + offs
        lane = lax.broadcasted_iota(jnp.int32, (pad, 128), 1)
        both = jnp.where(lane == 0, tok - posc, tok)
        qrow[hh] = jnp.concatenate([both] * per, axis=0).T[0:8, :]

    first = n - 1 - c
    for hh, count, base, mask in ((0, n, 0, bias0), (1, n + 1, first, bias1)):
        b = lax.broadcasted_iota(jnp.int32, (count, pad, lanes), 0) + base
        r = lax.broadcasted_iota(jnp.int32, (count, pad, lanes), 1)
        tok = jnp.where(r < half, b * half + r, blocks * rows).reshape(count * pad, lanes)
        ok = (tok <= qrow[hh, 1:2, :]) & (tok >= qrow[hh, 0:1, :])
        mask[...] = jnp.where(ok, 0.0, MASKED).astype(BF16)

    zrow = jnp.zeros((pad - half, HEAD_SIZE), F32)

    def load_q(g):
        for h in range(per):
            at = (g * per + h) * HEAD_SIZE
            x = q_ref[:, at:at + HEAD_SIZE].astype(F32)
            for hh in range(2):
                qs[g, hh, h * pad:(h + 1) * pad, :] = jnp.concatenate(
                    [x[hh * half:(hh + 1) * half], zrow]
                ).astype(BF16)

    def attend(g):
        for hh, count, base, mask in ((0, n, 0, bias0), (1, n + 1, first, bias1)):
            keys = kvb[g, pl.ds(base, count), 0:pad, :].reshape(count * pad, HEAD_SIZE)
            vals = kvb[g, pl.ds(base, count), pad:2 * pad, :].reshape(count * pad, HEAD_SIZE)
            s = lax.dot_general(
                keys, qs[g, hh], (((1,), (1,)), ((), ())), preferred_element_type=F32
            ) * scale + mask[...].astype(F32)
            top = jnp.max(s, axis=0, keepdims=True)
            p = jnp.exp2(s - top)
            den = jnp.sum(p, axis=0, keepdims=True)
            o = lax.dot_general(
                vals, p.astype(BF16), (((0,), (0,)), ((), ())), preferred_element_type=F32
            )
            ot[hh] = (o * (1.0 / den)).T
        for h in range(per):
            q, at = divmod((g * per + h) * HEAD_SIZE, chunk)
            att[c, q, :, at:at + HEAD_SIZE] = jnp.concatenate(
                [ot[0, h * pad:h * pad + half, :], ot[1, h * pad:h * pad + half, :]]
            ).astype(BF16)
        for q in range(g * chunks // groups, (g + 1) * chunks // groups):
            for d in range(2):
                @pl.when(goes(c, d))
                def _():
                    att_copy(c, q, d).start()

    pl.semaphore_wait(barrier, tn - 1 + jnp.where((c == 0) | (c == n - 1), 1, 2))
    kv_own(0)
    load_q(0)
    kv_take(0, (1,))
    for g in range(1, groups):
        kv_own(g)
    load_q(1)
    kv_take(0, range(2, n))
    attend(0)
    kv_take(1, range(1, n))
    attend(1)

    for i in range(tn):
        w_copy(i).wait()

    def column_of(j):
        k = jnp.where(lax.rem(j, 2) == 0, 1 - core, core)
        return 2 * k + jnp.where(j < 2, 1 - col, col)

    def project(s, side, q, whole):
        def column(j, _):
            i = column_of(j)
            if whole:
                prod = jnp.zeros((rows, cb), F32)
                for z in range(chunks):
                    prod = prod + jnp.dot(
                        att[s, z], wv[i, z * chunk:(z + 1) * chunk, :], preferred_element_type=F32
                    )
            else:
                prod = jnp.dot(
                    att[s, q], wv[i, q * chunk:(q + 1) * chunk, :], preferred_element_type=F32
                )
                if q > 0:
                    prod = acc[side, i] + prod
                if q < chunks - 1:
                    acc[side, i] = prod
                    return 0
            value = prod.astype(BF16)
            at = j // 2

            @pl.when(lax.rem(j, 2) == 0)
            def _():
                sib_out[s, at] = value
                for p in range(pieces):
                    sib_copy(s, at, p).start()

            @pl.when(lax.rem(j, 2) == 1)
            def _():
                keep[s, at] = value

            return 0

        lax.fori_loop(0, tn, column, 0)

    def far_project(s, q, p):
        def column(j, _):
            i = column_of(j)
            prod = acc[0, i, band(p)] + jnp.dot(
                att[s, q, band(p)],
                wv[i, pl.ds(pl.multiple_of(q * chunk, chunk), chunk), :],
                preferred_element_type=F32,
            )
            acc[0, i, band(p)] = prod
            at = j // 2

            @pl.when((q == chunks - 1) & (lax.rem(j, 2) == 0))
            def _():
                sib_out[s, at, band(p)] = prod.astype(BF16)
                sib_copy(s, at, p).start()

            @pl.when((q == chunks - 1) & (lax.rem(j, 2) == 1))
            def _():
                keep[s, at, band(p)] = prod.astype(BF16)

            return 0

        lax.fori_loop(0, tn, column, 0)

    def pair_sum(s, j, p):
        return keep[s, j, band(p)].astype(F32) + sib_in[s, j, band(p)].astype(F32)

    def pair_band(s, p):
        sib_copy(s, 0, p).wait_recv()

        @pl.when(jnp.logical_not(gathers(s) & keeper))
        def _():
            xs_out[s, band(p)] = pair_sum(s, 0, p).astype(BF16)
            xs_copy(s, p).start()

        sib_copy(s, 1, p).wait_recv()

        @pl.when(gathers(s) & jnp.logical_not(keeper))
        def _():
            ys_out[s, band(p)] = pair_sum(s, 1, p).astype(BF16)
            ys_copy(s, p).start()

    def pair_send(s):
        for p in range(pieces):
            pair_band(s, p)

    def reduce_band(s, p):
        mine = (s == c) & (t == c)

        @pl.when(jnp.logical_not(gathers(s)) | keeper)
        def _():
            xs_copy(s, p).wait_recv()
            summed = (pair_sum(s, 1, p) + xs_in[s, band(p)].astype(F32)).astype(BF16)

            @pl.when(mine)
            def _():
                fin[own_q, band(p)] = summed

            @pl.when(jnp.logical_not(mine))
            def _():
                red[s, band(p)] = summed
                fin_copy(s, p).start()

        @pl.when(gathers(s) & keeper)
        def _():
            ys_copy(s, p).wait_recv()
            two[s, band(p)] = (pair_sum(s, 0, p) + ys_in[s, band(p)].astype(F32)).astype(BF16)
            two_copy(s, p).start()

    def reduce_send(s):
        for p in range(pieces):
            reduce_band(s, p)

    near = jnp.where(c < n // 2, 0, n - 1)
    far = n - 1 - near

    def passes_far(s):
        return inner & (s == far)

    def att_drain(d):
        def one(s, _):
            @pl.when(goes(s, d) & jnp.logical_not(passes_far(s)))
            def _():
                for q in range(chunks):
                    att_copy(s, q, d).wait_send()

            @pl.when(goes(s, d) & passes_far(s))
            def _():
                for q in range(chunks):
                    for p in range(pieces):
                        far_copy(s, q, p, d).wait_send()

            return 0

        lax.fori_loop(0, n, one, 0)

    def both_sides(k, act):
        def one(side, _):
            s = c + k * (2 * side - 1)

            @pl.when((s >= 0) & (s < n))
            def _():
                act(s, side)

            return 0

        lax.fori_loop(0, 2, one, 0)

    project(c, 0, 0, True)

    def step(k, _):
        for q in range(chunks):
            def take(s, side):
                att_copy(s, q, 0).wait_recv()
                for d in range(2):
                    @pl.when(goes(s, d) & jnp.logical_not(passes_far(s)))
                    def _():
                        att_copy(s, q, d).start()

                    @pl.when(goes(s, d) & passes_far(s))
                    def _():
                        far_copy(s, q, 0, d).start()
                        if q == chunks - 1:
                            for p in range(1, pieces):
                                for z in range(chunks):
                                    far_copy(s, z, p, d).start()

            both_sides(k, take)
            if q == 0:
                @pl.when(k == 1)
                def _():
                    pair_send(c)

                @pl.when(k > 1)
                def _():
                    both_sides(k - 1, lambda s, side: pair_send(s))
            both_sides(k, lambda s, side: project(s, side, q, False))
            if q == chunks - 1:
                @pl.when(k == 1)
                def _():
                    reduce_send(c)

                @pl.when(k > 1)
                def _():
                    def now(s, side):
                        @pl.when(jnp.logical_not(inner & (s == near)))
                        def _():
                            reduce_send(s)

                    both_sides(k - 1, now)
        return 0

    lax.fori_loop(1, n - 1, step, 0)
    both_sides(n - 2, lambda s, side: pair_send(s))

    @pl.when(inner)
    def _():
        for d in range(2):
            @pl.when((c < n // 2) == (d == 1))
            def _():
                att_drain(d)
        pl.semaphore_signal(go_sem, inc=1, device_id={"ctx": n - 1 - c}, device_id_type=MESH)
        reduce_send(near)
        pl.semaphore_wait(go_sem, 1)
        reduce_send(far)

    @pl.when(jnp.logical_not(inner))
    def _():
        acc[0] = jnp.zeros(acc.shape[1:], F32)

        def far_step(p):
            def one(q, _):
                far_copy(far, q, p, 0).wait_recv()
                far_project(far, q, p)
                return 0

            return one

        lax.fori_loop(0, chunks, far_step(0), 0)
        both_sides(n - 2, lambda s, side: reduce_send(s))
        pair_band(far, 0)
        lax.fori_loop(0, chunks - 1, far_step(1), 0)
        reduce_band(far, 0)
        lax.fori_loop(chunks - 1, chunks, far_step(1), 0)
        pair_band(far, 1)
        reduce_band(far, 1)

    res_copy.wait()
    line = jnp.zeros((1, 128), F32)
    one = jnp.where(t == 0, 1.0, 0.0)
    for p in range(pieces):
        rng = band(p)
        piece = bands[p][1] - bands[p][0]
        lane = lax.broadcasted_iota(jnp.int32, (piece, 128), 1)
        score = jnp.zeros((piece, 1), F32)
        for i in range(tn):
            @pl.when(jnp.logical_not((c == t) & (own_q == i)))
            def _():
                fin_arrival(i, p).wait_recv()
            span = slice(i * cb, (i + 1) * cb)
            hidden = (resv[rng, span].astype(F32) + fin[i, rng, :].astype(F32)).astype(BF16)
            out_ref[rng, span] = hidden
            score = score + jnp.sum(
                hidden.astype(F32) * vh_ref[span].astype(F32).reshape(1, cb), axis=1, keepdims=True
            )
        turn = tcol[rng, :]
        terms = jnp.where(turn == lane, score, jnp.where(turn + 64 == lane, one, 0.0))
        line = line + jnp.sum(terms, axis=0, keepdims=True)
    me = c * tn + t
    tot[me] = line

    def tot_copy(j):
        other = lax.rem(me + j, n * tn)
        return pltpu.make_async_remote_copy(
            src_ref=tot.at[me], dst_ref=tot.at[me],
            send_sem=tot_send.at[other], recv_sem=tot_recv.at[me],
            device_id={"ctx": other // tn, "tp": lax.rem(other, tn)}, device_id_type=MESH,
        )

    def tot_arrival(j):
        other = lax.rem(me + j, n * tn)
        return pltpu.make_async_remote_copy(
            src_ref=tot.at[me], dst_ref=tot.at[other],
            send_sem=tot_send.at[other], recv_sem=tot_recv.at[other],
            device_id={"ctx": other // tn, "tp": lax.rem(other, tn)}, device_id_type=MESH,
        )

    def tot_start(j, _):
        tot_copy(j).start()
        return 0

    lax.fori_loop(1, n * tn, tot_start, 0)

    for d in range(n):
        @on(d)
        def _():
            for g in range(groups):
                for b in range(blocks):
                    held = owner(b) == d or any(
                        b in kv_arrivals(d, dist) for dist in range(1, n)
                    )
                    for way, e in ((0, d - 1), (1, d + 1)):
                        if held and carried(d, e, b):
                            kv_copy(g, b, e, way).wait_send()

    def drain(s, _):
        for j in range(2):
            for p in range(pieces):
                sib_copy(s, j, p).wait_send()
        for p in range(pieces):
            @pl.when(jnp.logical_not(gathers(s) & keeper))
            def _():
                xs_copy(s, p).wait_send()

            @pl.when(gathers(s) & jnp.logical_not(keeper))
            def _():
                ys_copy(s, p).wait_send()

            @pl.when(gathers(s) & keeper)
            def _():
                two_copy(s, p).wait_send()

            @pl.when(
                jnp.logical_not((s == c) & (t == c)) & (jnp.logical_not(gathers(s)) | keeper)
            )
            def _():
                fin_copy(s, p).wait_send()

        return 0

    lax.fori_loop(0, n, drain, 0)
    for d in range(2):
        @pl.when(jnp.logical_not(inner & ((c < n // 2) == (d == 1))))
        def _():
            att_drain(d)


    def tot_wait(j, _):
        tot_arrival(j).wait_recv()
        tot_copy(j).wait_send()
        return 0

    lax.fori_loop(1, n * tn, tot_wait, 0)
    total = jnp.sum(tot[...], axis=0)
    mean_ref[...] = (
        total[:, :TURNS] / jnp.maximum(total[:, 64:64 + TURNS], 1.0)
    ).reshape(TURNS)


def deliver(hidden, means, hidden_out, means_out):
    hidden_out[...] = hidden[...]
    means_out[...] = means[...]


def fused(
    n, tn, reach, queries, keys, values, residual, out_weight, value_head, segment_ids,
    positions, turn_ids
):
    rows, width = queries.shape
    groups = keys.shape[1] // HEAD_SIZE
    per = width // keys.shape[1]
    cols = out_weight.shape[1]
    cb = cols // tn
    pad = -(-(rows // 2) // 16) * 16
    pieces = len(split(rows))
    chunks = 2 * groups
    dims = (n, tn, rows, groups, per, cb, reach)
    vmem = pl.BlockSpec(memory_space=pltpu.VMEM)
    hbm = pl.BlockSpec(memory_space=pl.ANY)
    dma = pltpu.SemaphoreType.DMA
    results = pl.pallas_call(
        functools.partial(kernel, dims),
        out_shape=(
            jax.ShapeDtypeStruct((rows, cols), BF16),
            jax.ShapeDtypeStruct((TURNS,), F32),
        ),
        in_specs=[vmem] * 6 + [hbm] * 2,
        out_specs=(vmem, vmem),
        scratch_shapes=[
            pltpu.VMEM((groups, 2 * n, 2 * pad, HEAD_SIZE), BF16),
            pltpu.VMEM((n * pad, per * pad), BF16),
            pltpu.VMEM(((n + 1) * pad, per * pad), BF16),
            pltpu.VMEM((rows, 1), jnp.int32),
            pltpu.VMEM((2, 8, per * pad), jnp.int32),
            pltpu.VMEM((groups, 2, per * pad, HEAD_SIZE), BF16),
            pltpu.VMEM((2, per * pad, HEAD_SIZE), F32),
            pltpu.VMEM((n, chunks, rows, width // chunks), BF16),
            pltpu.VMEM((tn, width, cb), BF16),
            pltpu.VMEM((2, tn, rows, cb), F32),
            pltpu.VMEM((n, 2, rows, cb), BF16),
            pltpu.VMEM((n, 2, rows, cb), BF16),
            pltpu.VMEM((n, 2, rows, cb), BF16),
            pltpu.VMEM((n, rows, cb), BF16),
            pltpu.VMEM((n, rows, cb), BF16),
            pltpu.VMEM((n, rows, cb), BF16),
            pltpu.VMEM((tn, rows, cb), BF16),
            pltpu.VMEM((rows, cols), BF16),
            pltpu.VMEM((n * tn, 1, 128), F32),
            dma((groups, 2 * n, 2)), dma((groups, 2 * n)),
            dma((2, n, chunks)), dma((n, chunks)),
            dma((n, 2, pieces)), dma((n, 2, pieces)),
            dma((n, pieces)), dma((n, pieces)),
            dma((n, pieces)), dma((tn, pieces)),
            dma((n * tn,)), dma((n * tn,)),
            dma((tn,)), dma(()), pltpu.SemaphoreType.REGULAR,
            dma((chunks, pieces)), dma((chunks, pieces)),
            dma((n, pieces)), dma((n, pieces)), dma((n, pieces)),
            pltpu.VMEM((n, rows, cb), BF16),
            pltpu.VMEM((n, rows, cb), BF16),
            pltpu.VMEM((n, rows, cb), BF16),
        ],
        compiler_params=pltpu.CompilerParams(
            collective_id=0, has_side_effects=True, vmem_limit_bytes=56 * 1024 * 1024
        ),
    )(
        keys, values, positions, turn_ids, value_head, queries, residual, out_weight,
    )
    return pl.pallas_call(
        deliver,
        out_shape=(
            jax.ShapeDtypeStruct((rows, cols), BF16),
            jax.ShapeDtypeStruct((TURNS,), F32),
        ),
        in_specs=[vmem, vmem],
        out_specs=(vmem, vmem),
    )(*results)


def body(n, tn, *args):
    queries, keys, weight = args[0], args[1], args[4]
    rows = queries.shape[0]
    per = queries.shape[1] // keys.shape[1]
    longest = 7 * n * rows // (4 * (TURNS // 4))
    reach = -(-(longest - 1) // (rows // 2))
    lanes = per * (-(-(rows // 2) // 16) * 16)
    fits = (
        n == tn == 4 and reach == n and rows % 16 == 0 and weight.shape[1] % (128 * tn) == 0
        and lanes % 128 == 0
    )
    if fits:
        return fused(n, tn, reach, *args)
    return shards(*args)


def solution(mesh):
    return jax.shard_map(
        functools.partial(body, mesh.shape["ctx"], mesh.shape["tp"]),
        mesh=mesh,
        in_specs=(
            P(("groups", "ctx"), "tp"),
            P(("groups", "ctx"), "tp"),
            P(("groups", "ctx"), "tp"),
            P(("groups", "ctx"), "tp"),
            P("tp", "ctx"),
            P("tp"),
            P(("groups", "ctx")),
            P(("groups", "ctx")),
            P(("groups", "ctx")),
        ),
        out_specs=(P(("groups", "ctx"), "tp"), P("groups")),
        check_vma=False,
    )
```

```python
import functools
import math

import jax
import jax.numpy as jnp
from jax import lax
from jax.experimental import pallas as pl
from jax.experimental.pallas import tpu as pltpu
from jax.sharding import PartitionSpec as P

HEAD_SIZE = 128
TURNS = 16


def shards(
    queries, keys, values, residual, out_weight, value_head, segment_ids, positions, turn_ids
):
    tok_rows = queries.shape[0]
    kv_heads = keys.shape[1] // HEAD_SIZE
    query_head_group = queries.shape[1] // keys.shape[1]
    query_rows = query_head_group * tok_rows
    score_scale = 1.0 / math.sqrt(HEAD_SIZE)
    grouped = (
        queries.reshape(tok_rows, kv_heads, query_head_group, HEAD_SIZE)
        .transpose(1, 2, 0, 3)
        .reshape(kv_heads, query_rows, HEAD_SIZE)
    )
    seg_rows = jnp.tile(segment_ids, query_head_group)
    pos_rows = jnp.tile(positions, query_head_group)

    def update(running, key_block, value_block, seg_block, pos_block):
        allowed = (seg_rows[:, None] == seg_block[None, :]) & (
            pos_block[None, :] <= pos_rows[:, None]
        )
        numerator, row_max, denominator = running
        scores = (
            jnp.einsum("hqd,khd->hqk", grouped, key_block, preferred_element_type=jnp.float32)
            * score_scale
        )
        scores = jnp.where(allowed[None], scores, -1e30)
        new_max = jnp.maximum(row_max, jnp.max(scores, axis=2))
        weights = jnp.where(allowed[None], jnp.exp(scores - new_max[..., None]), 0.0)
        factor = jnp.exp(row_max - new_max)
        denominator = denominator * factor + jnp.sum(weights, axis=2)
        product = jnp.einsum(
            "hqk,khd->hqd",
            weights.astype(jnp.bfloat16),
            value_block,
            preferred_element_type=jnp.float32,
        )
        numerator = numerator * factor[..., None] + product
        return (numerator, new_max, denominator)

    initial = (
        jnp.zeros((kv_heads, query_rows, HEAD_SIZE), jnp.float32),
        jnp.full((kv_heads, query_rows), -1e30, jnp.float32),
        jnp.zeros((kv_heads, query_rows), jnp.float32),
    )
    running = initial
    key_piece = lax.all_gather(keys, "ctx", axis=0, tiled=True)
    value_piece = lax.all_gather(values, "ctx", axis=0, tiled=True)
    seg_piece = lax.all_gather(segment_ids, "ctx", axis=0, tiled=True)
    pos_piece = lax.all_gather(positions, "ctx", axis=0, tiled=True)
    row_count = key_piece.shape[0]
    key_piece = key_piece.reshape(row_count, kv_heads, HEAD_SIZE)
    value_piece = value_piece.reshape(row_count, kv_heads, HEAD_SIZE)
    block_width = math.gcd(row_count, 512)
    block_steps = row_count // block_width
    stacked = (
        key_piece.reshape(block_steps, block_width, kv_heads, HEAD_SIZE),
        value_piece.reshape(block_steps, block_width, kv_heads, HEAD_SIZE),
        seg_piece.reshape(block_steps, block_width),
        pos_piece.reshape(block_steps, block_width),
    )

    def block_step(running_state, block_set):
        return (update(running_state, block_set[0], block_set[1], block_set[2], block_set[3]), None)

    running, _ = lax.scan(block_step, running, stacked)
    numerator, row_max, denominator = running
    attention = (numerator / denominator[..., None]).reshape(
        kv_heads, query_head_group, tok_rows, HEAD_SIZE
    )
    attention = (
        attention.transpose(2, 0, 1, 3)
        .reshape(tok_rows, kv_heads * query_head_group * HEAD_SIZE)
        .astype(jnp.bfloat16)
    )
    partial_value = jnp.dot(
        lax.all_gather(attention, "ctx", axis=0, tiled=True),
        out_weight,
        preferred_element_type=jnp.float32,
    ).astype(jnp.bfloat16)
    term_rows = lax.all_to_all(
        partial_value, "ctx", split_axis=0, concat_axis=1, tiled=True
    ).astype(jnp.float32)
    summed = lax.psum_scatter(
        term_rows.astype(jnp.bfloat16), "tp", scatter_dimension=1, tiled=True
    ).astype(jnp.float32)
    hidden_out = (residual.astype(jnp.float32) + summed).astype(jnp.bfloat16)
    token_score = jnp.dot(hidden_out, value_head, preferred_element_type=jnp.float32)
    one_hot = (turn_ids[:, None] == jnp.arange(TURNS, dtype=jnp.int32)[None, :]).astype(jnp.float32)
    local_sum = jnp.dot(token_score, one_hot, precision=lax.Precision.HIGHEST)
    local_count = jnp.where(lax.axis_index("tp") == 0, jnp.sum(one_hot, axis=0), 0.0)
    totals, counts = lax.psum((local_sum, local_count), ("ctx", "tp"))
    turn_means = totals / jnp.maximum(counts, 1.0)
    return (hidden_out, turn_means)


MESH = pl.DeviceIdType.MESH
F32 = jnp.float32
BF16 = jnp.bfloat16
MASKED = -1e30


def split(rows):
    first = -(-2 * rows // 48) * 16
    return ((0, first), (first, rows))


def kernel(
    dims, k_hbm, v_hbm, pos_hbm, tid_hbm, vh_hbm, q_hbm, res_hbm, w_hbm,
    out_hbm, mean_ref, k_ref, v_ref, pos_ref, tid_ref, vh_ref, q_ref, out_ref, in_sem, out_sem,
    own_send, own_recv,
    kvb, bias0, bias1, tcol, qrow, qs, ot, att, wv, acc, keep, sib_out, sib_in,
    xs_out, xs_in, red, fin, resv, tot,
    kv_send, kv_recv, att_send, att_recv, sib_send, sib_recv, xs_send, xs_recv,
    fin_send, fin_recv, tot_send, tot_recv, w_sem, res_sem, go_sem,
    far_send, far_recv, ys_send, ys_recv, two_send, ys_out, ys_in, two,
):
    n, tn, rows, groups, per, cb, reach = dims
    bands = split(rows)
    pieces = len(bands)
    half = rows // 2
    pad = -(-half // 16) * 16
    blocks = 2 * n
    lanes = per * pad
    chunks = groups * 2
    chunk = groups * per * HEAD_SIZE // chunks
    c = lax.axis_index("ctx")
    t = lax.axis_index("tp")
    core = lax.rem(t, 2)
    col = t // 2
    sibling = t + 1 - 2 * core
    across = lax.rem(t + 2, tn)
    own_q = 2 * core + col
    far_q = 2 * core + 1 - col
    inner = (c > 0) & (c < n - 1)
    keeper = col == c // 2
    scale = 1.0 / math.sqrt(HEAD_SIZE) * math.log2(math.e)

    arrays = [
        pltpu.make_async_copy(a, b, in_sem.at[i])
        for i, (a, b) in enumerate((
            (k_hbm, k_ref), (v_hbm, v_ref), (pos_hbm, pos_ref), (tid_hbm, tid_ref),
            (vh_hbm, vh_ref), (q_hbm, q_ref),
        ))
    ]
    barrier = pltpu.get_barrier_semaphore()

    for j in range(1, tn):
        pl.semaphore_signal(
            barrier, inc=1, device_id={"tp": lax.rem(t + j, tn)}, device_id_type=MESH
        )
    for away in (-1, 1):
        @pl.when((c + away >= 0) & (c + away < n))
        def _():
            pl.semaphore_signal(
                barrier, inc=1, device_id={"ctx": c + away}, device_id_type=MESH
            )

    for cp in arrays:
        cp.start()

    def w_copy(i):
        return pltpu.make_async_copy(
            w_hbm.at[:, pl.ds(pl.multiple_of(i * cb, 128), cb)], wv.at[i], w_sem.at[i]
        )

    res_copy = pltpu.make_async_copy(res_hbm, resv, res_sem)

    def needs(d, b):
        late = blocks - 1 - d
        return d - reach <= b <= d or late - reach <= b <= late

    def owner(b):
        return b if b < n else blocks - 1 - b

    def carried(d, e, b):
        if not 0 <= e < n:
            return False
        beyond = range(0, e + 1) if e < d else range(e, n)
        behind = owner(b) >= d if e < d else owner(b) <= d
        return behind and any(needs(x, b) for x in beyond)

    def kv_copy(g, b, e, way):
        return pltpu.make_async_remote_copy(
            src_ref=kvb.at[g, b], dst_ref=kvb.at[g, b],
            send_sem=kv_send.at[g, b, way], recv_sem=kv_recv.at[g, b],
            device_id={"ctx": e}, device_id_type=MESH,
        )

    def on(d):
        return pl.when(c == d)

    def kv_pass(d, g, b):
        for way, e in ((0, d - 1), (1, d + 1)):
            if carried(d, e, b):
                kv_copy(g, b, e, way).start()

    def kv_arrivals(d, dist):
        return [
            b for b in range(blocks)
            if abs(owner(b) - d) == dist
            and (carried(d - 1, d, b) if owner(b) < d else carried(d + 1, d, b))
        ]

    def kv_own(g):
        for d in range(n):
            @on(d)
            def _():
                for b in (d, blocks - 1 - d):
                    kv_pass(d, g, b)

    def kv_take(g, dists):
        for d in range(n):
            @on(d)
            def _():
                for dist in dists:
                    for b in kv_arrivals(d, dist):
                        kv_copy(g, b, d, 0).wait_recv()
                        kv_pass(d, g, b)

    for cp in arrays[:2]:
        cp.wait()
    zeros = jnp.zeros((pad - half, HEAD_SIZE), F32)
    for g in range(groups):
        span = slice(g * HEAD_SIZE, (g + 1) * HEAD_SIZE)
        for ref, low in ((k_ref, 0), (v_ref, pad)):
            x = ref[:, span].astype(F32)
            kvb[g, c, low:low + pad, :] = jnp.concatenate([x[:half], zeros]).astype(BF16)
            kvb[g, blocks - 1 - c, low:low + pad, :] = jnp.concatenate(
                [x[half:], zeros]
            ).astype(BF16)
    for d in range(n):
        window = set(range(n)) | set(range(n - 1 - d, blocks - d))
        missing = [b for b in sorted(window) if owner(b) != d and not any(
            b in kv_arrivals(d, dist) for dist in range(1, n))]
        if missing:
            @on(d)
            def _():
                for g in range(groups):
                    for b in missing:
                        kvb[g, b] = jnp.zeros((2 * pad, HEAD_SIZE), BF16)


    def att_copy(s, q, d):
        return pltpu.make_async_remote_copy(
            src_ref=att.at[s, q], dst_ref=att.at[s, q],
            send_sem=att_send.at[d, s, q], recv_sem=att_recv.at[s, q],
            device_id={"ctx": c + 1 - 2 * d}, device_id_type=MESH,
        )

    lead = half // 16 * 16

    def piece_rows(s, e):
        at = jnp.where(s < n // 2, 0, rows - lead) if e == 0 else jnp.where(s < n // 2, lead, 0)
        return pl.ds(pl.multiple_of(at, 16), lead if e == 0 else rows - lead)

    def own_copy(q, d, e):
        return pltpu.make_async_remote_copy(
            src_ref=att.at[c, q, piece_rows(c, e)], dst_ref=att.at[c, q, piece_rows(c, e)],
            send_sem=own_send.at[d, q, e], recv_sem=own_recv.at[d, q, e],
            device_id={"ctx": c + 1 - 2 * d}, device_id_type=MESH,
        )

    def next_copy(s, side, q, e):
        return pltpu.make_async_remote_copy(
            src_ref=att.at[s, q, piece_rows(s, e)], dst_ref=att.at[s, q, piece_rows(s, e)],
            send_sem=own_send.at[0, q, e], recv_sem=own_recv.at[side, q, e],
            device_id={"ctx": c}, device_id_type=MESH,
        )

    def goes(s, d):
        if d == 0:
            return (s <= c) & (c < n - 1)
        return (s >= c) & (c > 0)

    def band(p):
        return slice(*bands[p])

    def far_copy(s, q, p, d):
        return pltpu.make_async_remote_copy(
            src_ref=att.at[s, q, band(p)], dst_ref=att.at[s, q, band(p)],
            send_sem=far_send.at[q, p], recv_sem=far_recv.at[q, p],
            device_id={"ctx": c + 1 - 2 * d}, device_id_type=MESH,
        )

    def sib_copy(s, j, p):
        return pltpu.make_async_remote_copy(
            src_ref=sib_out.at[s, j, band(p)], dst_ref=sib_in.at[s, j, band(p)],
            send_sem=sib_send.at[s, j, p], recv_sem=sib_recv.at[s, j, p],
            device_id={"tp": sibling}, device_id_type=MESH,
        )

    def xs_copy(s, p):
        return pltpu.make_async_remote_copy(
            src_ref=xs_out.at[s, band(p)], dst_ref=xs_in.at[s, band(p)],
            send_sem=xs_send.at[s, p], recv_sem=xs_recv.at[s, p],
            device_id={"tp": across}, device_id_type=MESH,
        )

    def fin_copy(s, p):
        return pltpu.make_async_remote_copy(
            src_ref=red.at[s, band(p)], dst_ref=fin.at[own_q, band(p)],
            send_sem=fin_send.at[s, p], recv_sem=fin_recv.at[own_q, p],
            device_id={"ctx": s, "tp": c}, device_id_type=MESH,
        )

    def ys_copy(s, p):
        return pltpu.make_async_remote_copy(
            src_ref=ys_out.at[s, band(p)], dst_ref=ys_in.at[s, band(p)],
            send_sem=ys_send.at[s, p], recv_sem=ys_recv.at[s, p],
            device_id={"tp": across}, device_id_type=MESH,
        )

    def two_copy(s, p):
        return pltpu.make_async_remote_copy(
            src_ref=two.at[s, band(p)], dst_ref=fin.at[far_q, band(p)],
            send_sem=two_send.at[s, p], recv_sem=fin_recv.at[far_q, p],
            device_id={"ctx": s, "tp": c}, device_id_type=MESH,
        )

    def gathers(s):
        return inner & ((s == 0) | (s == n - 1))

    def fin_arrival(i, p):
        return pltpu.make_async_remote_copy(
            src_ref=red.at[0, band(p)], dst_ref=fin.at[i, band(p)],
            send_sem=fin_send.at[0, p], recv_sem=fin_recv.at[i, p],
            device_id={"ctx": t}, device_id_type=MESH,
        )

    pl.semaphore_wait(barrier, tn - 1 + jnp.where((c == 0) | (c == n - 1), 1, 2))
    for g in range(groups):
        kv_own(g)

    for cp in arrays[2:5]:
        cp.wait()
    ids = jnp.concatenate(
        [pos_ref[...].reshape(1, rows), tid_ref[...].reshape(1, rows),
         jnp.zeros((126, rows), jnp.int32)], axis=0
    )
    idcol = jnp.concatenate(
        [ids, jnp.zeros((128, -rows % 128), jnp.int32)], axis=1
    ).T[:rows, :]
    tcol[...] = idcol[:, 1:2]
    offs = lax.broadcasted_iota(jnp.int32, (pad, 128), 0)
    blank = jnp.zeros((pad - half, 128), jnp.int32)
    for hh in range(2):
        place = (c if hh == 0 else blocks - 1 - c) * half
        posc = jnp.concatenate([idcol[hh * half:(hh + 1) * half, :], blank], axis=0)
        tok = place + offs
        lane = lax.broadcasted_iota(jnp.int32, (pad, 128), 1)
        both = jnp.where(lane == 0, tok - posc, tok)
        qrow[hh] = jnp.concatenate([both] * per, axis=0).T[0:8, :]

    first = n - 1 - c

    zrow = jnp.zeros((pad - half, HEAD_SIZE), F32)

    def load_q(g):
        for h in range(per):
            at = (g * per + h) * HEAD_SIZE
            x = q_ref[:, at:at + HEAD_SIZE].astype(F32)
            for hh in range(2):
                qs[g, hh, h * pad:(h + 1) * pad, :] = jnp.concatenate(
                    [x[hh * half:(hh + 1) * half], zrow]
                ).astype(BF16)

    def attend(g, hh, count, base, mask):
        keys = kvb[g, pl.ds(base, count), 0:pad, :].reshape(count * pad, HEAD_SIZE)
        vals = kvb[g, pl.ds(base, count), pad:2 * pad, :].reshape(count * pad, HEAD_SIZE)
        s = lax.dot_general(
            keys, qs[g, hh], (((1,), (1,)), ((), ())), preferred_element_type=F32
        ) * scale + mask[0:count * pad, :].astype(F32)
        top = jnp.max(s, axis=0, keepdims=True)
        p = jnp.exp2(s - top)
        den = jnp.sum(p, axis=0, keepdims=True)
        o = lax.dot_general(
            vals, p.astype(BF16), (((0,), (0,)), ((), ())), preferred_element_type=F32
        )
        ot[g, hh] = (o * (1.0 / den)).T

    low_one, high_one = n // 2 - 1, n // 2

    def place(g, at_row, spans):
        for h in range(per):
            q, at = divmod((g * per + h) * HEAD_SIZE, chunk)
            parts = [ot[g, hh, h * pad + a:h * pad + b, :] for hh, a, b in spans]
            size = sum(b - a for _, a, b in spans)
            whole = parts[0] if len(parts) == 1 else jnp.concatenate(parts)
            att[c, q, at_row:at_row + size, at:at + HEAD_SIZE] = whole.astype(BF16)

    def send_own(g, e):
        for q in range(g * chunks // groups, (g + 1) * chunks // groups):
            for d in range(2):
                @pl.when(goes(c, d))
                def _():
                    own_copy(q, d, e).start()

    def early(g):
        @on(low_one)
        def _():
            attend(g, 0, low_one + 1, 0, bias0)
            place(g, 0, ((0, 0, lead),))
            send_own(g, 0)

        @on(high_one)
        def _():
            attend(g, 1, n + 1, first, bias1)
            place(g, rows - lead, ((1, half - lead, half),))
            send_own(g, 0)

    def late(g):
        @pl.when(c != low_one)
        def _():
            attend(g, 0, n, 0, bias0)

        @pl.when(c != high_one)
        def _():
            attend(g, 1, n + 1, first, bias1)

        @pl.when(c < n // 2)
        def _():
            place(g, lead, ((0, lead, half), (1, 0, half)))

        @pl.when(c >= n // 2)
        def _():
            place(g, 0, ((0, 0, half), (1, 0, half - lead)))

        @pl.when(c == 0)
        def _():
            place(g, 0, ((0, 0, lead),))

        @pl.when(c == n - 1)
        def _():
            place(g, rows - lead, ((1, half - lead, half),))

        @pl.when((c == 0) | (c == n - 1))
        def _():
            send_own(g, 0)

        send_own(g, 1)

    arrays[5].wait()
    load_q(0)
    for hh, count, base, mask in ((0, n, 0, bias0), (1, n + 1, first, bias1)):
        b = lax.broadcasted_iota(jnp.int32, (count, pad, lanes), 0) + base
        r = lax.broadcasted_iota(jnp.int32, (count, pad, lanes), 1)
        tok = jnp.where(r < half, b * half + r, blocks * rows).reshape(count * pad, lanes)
        ok = (tok <= qrow[hh, 1:2, :]) & (tok >= qrow[hh, 0:1, :])
        mask[...] = jnp.where(ok, 0.0, MASKED).astype(BF16)

    kv_take(0, (1,))
    early(0)
    load_q(1)
    kv_take(1, (1,))
    early(1)
    kv_take(0, range(2, n))
    late(0)
    for i in range(tn):
        w_copy(i).start()
    kv_take(1, range(2, n))
    late(1)

    res_copy.start()
    for i in range(tn):
        w_copy(i).wait()

    def column_of(j):
        k = jnp.where(lax.rem(j, 2) == 0, 1 - core, core)
        return 2 * k + jnp.where(j < 2, 1 - col, col)

    def project(s, side, q, whole):
        def column(j, _):
            i = column_of(j)
            if whole:
                prod = jnp.zeros((rows, cb), F32)
                for z in range(chunks):
                    prod = prod + jnp.dot(
                        att[s, z], wv[i, z * chunk:(z + 1) * chunk, :], preferred_element_type=F32
                    )
            else:
                prod = jnp.dot(
                    att[s, q], wv[i, q * chunk:(q + 1) * chunk, :], preferred_element_type=F32
                )
                if q > 0:
                    prod = acc[side, i] + prod
                if q < chunks - 1:
                    acc[side, i] = prod
                    return 0
            value = prod.astype(BF16)
            at = j // 2

            @pl.when(lax.rem(j, 2) == 0)
            def _():
                sib_out[s, at] = value
                for p in range(pieces):
                    sib_copy(s, at, p).start()

            @pl.when(lax.rem(j, 2) == 1)
            def _():
                keep[s, at] = value

            return 0

        lax.fori_loop(0, tn, column, 0)

    def far_project(s, q, p):
        def column(j, _):
            i = column_of(j)
            prod = acc[0, i, band(p)] + jnp.dot(
                att[s, q, band(p)],
                wv[i, pl.ds(pl.multiple_of(q * chunk, chunk), chunk), :],
                preferred_element_type=F32,
            )
            acc[0, i, band(p)] = prod
            at = j // 2

            @pl.when((q == chunks - 1) & (lax.rem(j, 2) == 0))
            def _():
                sib_out[s, at, band(p)] = prod.astype(BF16)
                sib_copy(s, at, p).start()

            @pl.when((q == chunks - 1) & (lax.rem(j, 2) == 1))
            def _():
                keep[s, at, band(p)] = prod.astype(BF16)

            return 0

        lax.fori_loop(0, tn, column, 0)

    def pair_sum(s, j, p):
        return keep[s, j, band(p)].astype(F32) + sib_in[s, j, band(p)].astype(F32)

    def pair_band(s, p):
        sib_copy(s, 0, p).wait_recv()

        @pl.when(jnp.logical_not(gathers(s) & keeper))
        def _():
            xs_out[s, band(p)] = pair_sum(s, 0, p).astype(BF16)
            xs_copy(s, p).start()

        sib_copy(s, 1, p).wait_recv()

        @pl.when(gathers(s) & jnp.logical_not(keeper))
        def _():
            ys_out[s, band(p)] = pair_sum(s, 1, p).astype(BF16)
            ys_copy(s, p).start()

    def pair_send(s):
        for p in range(pieces):
            pair_band(s, p)

    def reduce_band(s, p):
        mine = (s == c) & (t == c)

        @pl.when(jnp.logical_not(gathers(s)) | keeper)
        def _():
            xs_copy(s, p).wait_recv()
            summed = (pair_sum(s, 1, p) + xs_in[s, band(p)].astype(F32)).astype(BF16)

            @pl.when(mine)
            def _():
                fin[own_q, band(p)] = summed

            @pl.when(jnp.logical_not(mine))
            def _():
                red[s, band(p)] = summed
                fin_copy(s, p).start()

        @pl.when(gathers(s) & keeper)
        def _():
            ys_copy(s, p).wait_recv()
            two[s, band(p)] = (pair_sum(s, 0, p) + ys_in[s, band(p)].astype(F32)).astype(BF16)
            two_copy(s, p).start()

    def reduce_send(s):
        for p in range(pieces):
            reduce_band(s, p)

    near = jnp.where(c < n // 2, 0, n - 1)
    far = n - 1 - near

    def passes_far(s):
        return inner & (s == far)

    def att_drain(d):
        def one(s, _):
            @pl.when(goes(s, d) & jnp.logical_not(passes_far(s)) & (s != c))
            def _():
                for q in range(chunks):
                    att_copy(s, q, d).wait_send()

            @pl.when(goes(s, d) & (s == c))
            def _():
                for q in range(chunks):
                    for e in range(2):
                        own_copy(q, d, e).wait_send()

            @pl.when(goes(s, d) & passes_far(s))
            def _():
                for q in range(chunks):
                    for p in range(pieces):
                        far_copy(s, q, p, d).wait_send()

            return 0

        lax.fori_loop(0, n, one, 0)

    def both_sides(k, act):
        def one(side, _):
            s = c + k * (2 * side - 1)

            @pl.when((s >= 0) & (s < n))
            def _():
                act(s, side)

            return 0

        lax.fori_loop(0, 2, one, 0)

    project(c, 0, 0, True)

    def step(k, _):
        for q in range(chunks):
            def take(s, side):
                @pl.when(k == 1)
                def _():
                    for e in range(2):
                        next_copy(s, side, q, e).wait_recv()

                @pl.when(k > 1)
                def _():
                    att_copy(s, q, 0).wait_recv()

                for d in range(2):
                    @pl.when(goes(s, d) & jnp.logical_not(passes_far(s)))
                    def _():
                        att_copy(s, q, d).start()

                    @pl.when(goes(s, d) & passes_far(s))
                    def _():
                        far_copy(s, q, 0, d).start()
                        if q == chunks - 1:
                            for p in range(1, pieces):
                                for z in range(chunks):
                                    far_copy(s, z, p, d).start()

            both_sides(k, take)
            if q == 0:
                @pl.when(k == 1)
                def _():
                    pair_send(c)

                @pl.when(k > 1)
                def _():
                    both_sides(k - 1, lambda s, side: pair_send(s))
            both_sides(k, lambda s, side: project(s, side, q, False))
            if q == chunks - 1:
                @pl.when(k == 1)
                def _():
                    reduce_send(c)

                @pl.when(k > 1)
                def _():
                    def now(s, side):
                        @pl.when(jnp.logical_not(inner & (s == near)))
                        def _():
                            reduce_send(s)

                    both_sides(k - 1, now)
        return 0

    lax.fori_loop(1, n - 1, step, 0)
    both_sides(n - 2, lambda s, side: pair_send(s))

    @pl.when(inner)
    def _():
        for d in range(2):
            @pl.when((c < n // 2) == (d == 1))
            def _():
                att_drain(d)
        pl.semaphore_signal(go_sem, inc=1, device_id={"ctx": n - 1 - c}, device_id_type=MESH)
        reduce_send(near)
        pl.semaphore_wait(go_sem, 1)
        reduce_send(far)

    @pl.when(jnp.logical_not(inner))
    def _():
        acc[0] = jnp.zeros(acc.shape[1:], F32)

        def far_step(p):
            def one(q, _):
                far_copy(far, q, p, 0).wait_recv()
                far_project(far, q, p)
                return 0

            return one

        lax.fori_loop(0, chunks, far_step(0), 0)
        both_sides(n - 2, lambda s, side: reduce_send(s))
        pair_band(far, 0)
        lax.fori_loop(0, chunks - 1, far_step(1), 0)
        reduce_band(far, 0)
        lax.fori_loop(chunks - 1, chunks, far_step(1), 0)
        pair_band(far, 1)
        reduce_band(far, 1)

    def out_copy(p):
        return pltpu.make_async_copy(
            out_ref.at[band(p)], out_hbm.at[band(p)], out_sem.at[p]
        )

    res_copy.wait()
    line = jnp.zeros((1, 128), F32)
    one = jnp.where(t == 0, 1.0, 0.0)
    for p in range(pieces):
        rng = band(p)
        piece = bands[p][1] - bands[p][0]
        lane = lax.broadcasted_iota(jnp.int32, (piece, 128), 1)
        score = jnp.zeros((piece, 1), F32)
        for i in range(tn):
            @pl.when(jnp.logical_not((c == t) & (own_q == i)))
            def _():
                fin_arrival(i, p).wait_recv()
            span = slice(i * cb, (i + 1) * cb)
            hidden = (resv[rng, span].astype(F32) + fin[i, rng, :].astype(F32)).astype(BF16)
            out_ref[rng, span] = hidden
            score = score + jnp.sum(
                hidden.astype(F32) * vh_ref[span].astype(F32).reshape(1, cb), axis=1, keepdims=True
            )
        turn = tcol[rng, :]
        terms = jnp.where(turn == lane, score, jnp.where(turn + 64 == lane, one, 0.0))
        line = line + jnp.sum(terms, axis=0, keepdims=True)
        out_copy(p).start()
    me = c * tn + t
    tot[me] = line

    def tot_copy(j):
        other = lax.rem(me + jnp.where(c < n // 2, n * tn - j, j), n * tn)
        return pltpu.make_async_remote_copy(
            src_ref=tot.at[me], dst_ref=tot.at[me],
            send_sem=tot_send.at[other], recv_sem=tot_recv.at[me],
            device_id={"ctx": other // tn, "tp": lax.rem(other, tn)}, device_id_type=MESH,
        )

    def tot_arrival(j):
        other = lax.rem(me + jnp.where(c < n // 2, n * tn - j, j), n * tn)
        return pltpu.make_async_remote_copy(
            src_ref=tot.at[me], dst_ref=tot.at[other],
            send_sem=tot_send.at[other], recv_sem=tot_recv.at[other],
            device_id={"ctx": other // tn, "tp": lax.rem(other, tn)}, device_id_type=MESH,
        )

    def tot_start(j, _):
        tot_copy(j).start()
        return 0

    lax.fori_loop(1, n * tn, tot_start, 0)

    for d in range(n):
        @on(d)
        def _():
            for g in range(groups):
                for b in range(blocks):
                    held = owner(b) == d or any(
                        b in kv_arrivals(d, dist) for dist in range(1, n)
                    )
                    for way, e in ((0, d - 1), (1, d + 1)):
                        if held and carried(d, e, b):
                            kv_copy(g, b, e, way).wait_send()

    def drain(s, _):
        for j in range(2):
            for p in range(pieces):
                sib_copy(s, j, p).wait_send()
        for p in range(pieces):
            @pl.when(jnp.logical_not(gathers(s) & keeper))
            def _():
                xs_copy(s, p).wait_send()

            @pl.when(gathers(s) & jnp.logical_not(keeper))
            def _():
                ys_copy(s, p).wait_send()

            @pl.when(gathers(s) & keeper)
            def _():
                two_copy(s, p).wait_send()

            @pl.when(
                jnp.logical_not((s == c) & (t == c)) & (jnp.logical_not(gathers(s)) | keeper)
            )
            def _():
                fin_copy(s, p).wait_send()

        return 0

    lax.fori_loop(0, n, drain, 0)
    for d in range(2):
        @pl.when(jnp.logical_not(inner & ((c < n // 2) == (d == 1))))
        def _():
            att_drain(d)


    def tot_wait(j, _):
        tot_arrival(j).wait_recv()
        tot_copy(j).wait_send()
        return 0

    lax.fori_loop(1, n * tn, tot_wait, 0)
    total = jnp.sum(tot[...], axis=0)
    for p in range(pieces):
        out_copy(p).wait()
    mean_ref[...] = (
        total[:, :TURNS] / jnp.maximum(total[:, 64:64 + TURNS], 1.0)
    ).reshape(TURNS)


def deliver(hidden, means, hidden_out, means_out):
    hidden_out[...] = hidden[...]
    means_out[...] = means[...]


def fused(
    n, tn, reach, queries, keys, values, residual, out_weight, value_head, segment_ids,
    positions, turn_ids
):
    rows, width = queries.shape
    groups = keys.shape[1] // HEAD_SIZE
    per = width // keys.shape[1]
    cols = out_weight.shape[1]
    cb = cols // tn
    pad = -(-(rows // 2) // 16) * 16
    pieces = len(split(rows))
    chunks = 2 * groups
    dims = (n, tn, rows, groups, per, cb, reach)
    vmem = pl.BlockSpec(memory_space=pltpu.VMEM)
    hbm = pl.BlockSpec(memory_space=pl.ANY)
    dma = pltpu.SemaphoreType.DMA
    results = pl.pallas_call(
        functools.partial(kernel, dims),
        out_shape=(
            jax.ShapeDtypeStruct((rows, cols), BF16),
            jax.ShapeDtypeStruct((TURNS,), F32),
        ),
        in_specs=[hbm] * 8,
        out_specs=(hbm, vmem),
        scratch_shapes=[
            pltpu.VMEM(keys.shape, BF16),
            pltpu.VMEM(values.shape, BF16),
            pltpu.VMEM((rows,), jnp.int32),
            pltpu.VMEM((rows,), jnp.int32),
            pltpu.VMEM(value_head.shape, BF16),
            pltpu.VMEM((rows, width), BF16),
            pltpu.VMEM((rows, cols), BF16),
            dma((6,)), dma((pieces,)),
            dma((2, chunks, 2)), dma((2, chunks, 2)),
            pltpu.VMEM((groups, 2 * n, 2 * pad, HEAD_SIZE), BF16),
            pltpu.VMEM((n * pad, per * pad), BF16),
            pltpu.VMEM(((n + 1) * pad, per * pad), BF16),
            pltpu.VMEM((rows, 1), jnp.int32),
            pltpu.VMEM((2, 8, per * pad), jnp.int32),
            pltpu.VMEM((groups, 2, per * pad, HEAD_SIZE), BF16),
            pltpu.VMEM((groups, 2, per * pad, HEAD_SIZE), F32),
            pltpu.VMEM((n, chunks, rows, width // chunks), BF16),
            pltpu.VMEM((tn, width, cb), BF16),
            pltpu.VMEM((2, tn, rows, cb), F32),
            pltpu.VMEM((n, 2, rows, cb), BF16),
            pltpu.VMEM((n, 2, rows, cb), BF16),
            pltpu.VMEM((n, 2, rows, cb), BF16),
            pltpu.VMEM((n, rows, cb), BF16),
            pltpu.VMEM((n, rows, cb), BF16),
            pltpu.VMEM((n, rows, cb), BF16),
            pltpu.VMEM((tn, rows, cb), BF16),
            pltpu.VMEM((rows, cols), BF16),
            pltpu.VMEM((n * tn, 1, 128), F32),
            dma((groups, 2 * n, 2)), dma((groups, 2 * n)),
            dma((2, n, chunks)), dma((n, chunks)),
            dma((n, 2, pieces)), dma((n, 2, pieces)),
            dma((n, pieces)), dma((n, pieces)),
            dma((n, pieces)), dma((tn, pieces)),
            dma((n * tn,)), dma((n * tn,)),
            dma((tn,)), dma(()), pltpu.SemaphoreType.REGULAR,
            dma((chunks, pieces)), dma((chunks, pieces)),
            dma((n, pieces)), dma((n, pieces)), dma((n, pieces)),
            pltpu.VMEM((n, rows, cb), BF16),
            pltpu.VMEM((n, rows, cb), BF16),
            pltpu.VMEM((n, rows, cb), BF16),
        ],
        compiler_params=pltpu.CompilerParams(
            collective_id=0, has_side_effects=True, vmem_limit_bytes=56 * 1024 * 1024
        ),
    )(
        keys, values, positions, turn_ids, value_head, queries, residual, out_weight,
    )
    return pl.pallas_call(
        deliver,
        out_shape=(
            jax.ShapeDtypeStruct((rows, cols), BF16),
            jax.ShapeDtypeStruct((TURNS,), F32),
        ),
        in_specs=[vmem, vmem],
        out_specs=(vmem, vmem),
    )(*results)


def body(n, tn, *args):
    queries, keys, weight = args[0], args[1], args[4]
    rows = queries.shape[0]
    per = queries.shape[1] // keys.shape[1]
    longest = 7 * n * rows // (4 * (TURNS // 4))
    reach = -(-(longest - 1) // (rows // 2))
    lanes = per * (-(-(rows // 2) // 16) * 16)
    fits = (
        n == tn == 4 and reach == n and rows % 16 == 0 and weight.shape[1] % (128 * tn) == 0
        and lanes % 128 == 0
    )
    if fits:
        return fused(n, tn, reach, *args)
    return shards(*args)


def solution(mesh):
    return jax.shard_map(
        functools.partial(body, mesh.shape["ctx"], mesh.shape["tp"]),
        mesh=mesh,
        in_specs=(
            P(("groups", "ctx"), "tp"),
            P(("groups", "ctx"), "tp"),
            P(("groups", "ctx"), "tp"),
            P(("groups", "ctx"), "tp"),
            P("tp", "ctx"),
            P("tp"),
            P(("groups", "ctx")),
            P(("groups", "ctx")),
            P(("groups", "ctx")),
        ),
        out_specs=(P(("groups", "ctx"), "tp"), P("groups")),
        check_vma=False,
    )
```

```python
import functools
import math

import jax
import jax.numpy as jnp
from jax import lax
from jax.experimental import pallas as pl
from jax.experimental.pallas import tpu as pltpu
from jax.sharding import PartitionSpec as P

HEAD_SIZE = 128
TURNS = 16


def shards(
    queries, keys, values, residual, out_weight, value_head, segment_ids, positions, turn_ids
):
    tok_rows = queries.shape[0]
    kv_heads = keys.shape[1] // HEAD_SIZE
    query_head_group = queries.shape[1] // keys.shape[1]
    query_rows = query_head_group * tok_rows
    score_scale = 1.0 / math.sqrt(HEAD_SIZE)
    grouped = (
        queries.reshape(tok_rows, kv_heads, query_head_group, HEAD_SIZE)
        .transpose(1, 2, 0, 3)
        .reshape(kv_heads, query_rows, HEAD_SIZE)
    )
    seg_rows = jnp.tile(segment_ids, query_head_group)
    pos_rows = jnp.tile(positions, query_head_group)

    def update(running, key_block, value_block, seg_block, pos_block):
        allowed = (seg_rows[:, None] == seg_block[None, :]) & (
            pos_block[None, :] <= pos_rows[:, None]
        )
        numerator, row_max, denominator = running
        scores = (
            jnp.einsum("hqd,khd->hqk", grouped, key_block, preferred_element_type=jnp.float32)
            * score_scale
        )
        scores = jnp.where(allowed[None], scores, -1e30)
        new_max = jnp.maximum(row_max, jnp.max(scores, axis=2))
        weights = jnp.where(allowed[None], jnp.exp(scores - new_max[..., None]), 0.0)
        factor = jnp.exp(row_max - new_max)
        denominator = denominator * factor + jnp.sum(weights, axis=2)
        product = jnp.einsum(
            "hqk,khd->hqd",
            weights.astype(jnp.bfloat16),
            value_block,
            preferred_element_type=jnp.float32,
        )
        numerator = numerator * factor[..., None] + product
        return (numerator, new_max, denominator)

    initial = (
        jnp.zeros((kv_heads, query_rows, HEAD_SIZE), jnp.float32),
        jnp.full((kv_heads, query_rows), -1e30, jnp.float32),
        jnp.zeros((kv_heads, query_rows), jnp.float32),
    )
    running = initial
    key_piece = lax.all_gather(keys, "ctx", axis=0, tiled=True)
    value_piece = lax.all_gather(values, "ctx", axis=0, tiled=True)
    seg_piece = lax.all_gather(segment_ids, "ctx", axis=0, tiled=True)
    pos_piece = lax.all_gather(positions, "ctx", axis=0, tiled=True)
    row_count = key_piece.shape[0]
    key_piece = key_piece.reshape(row_count, kv_heads, HEAD_SIZE)
    value_piece = value_piece.reshape(row_count, kv_heads, HEAD_SIZE)
    block_width = math.gcd(row_count, 512)
    block_steps = row_count // block_width
    stacked = (
        key_piece.reshape(block_steps, block_width, kv_heads, HEAD_SIZE),
        value_piece.reshape(block_steps, block_width, kv_heads, HEAD_SIZE),
        seg_piece.reshape(block_steps, block_width),
        pos_piece.reshape(block_steps, block_width),
    )

    def block_step(running_state, block_set):
        return (update(running_state, block_set[0], block_set[1], block_set[2], block_set[3]), None)

    running, _ = lax.scan(block_step, running, stacked)
    numerator, row_max, denominator = running
    attention = (numerator / denominator[..., None]).reshape(
        kv_heads, query_head_group, tok_rows, HEAD_SIZE
    )
    attention = (
        attention.transpose(2, 0, 1, 3)
        .reshape(tok_rows, kv_heads * query_head_group * HEAD_SIZE)
        .astype(jnp.bfloat16)
    )
    partial_value = jnp.dot(
        lax.all_gather(attention, "ctx", axis=0, tiled=True),
        out_weight,
        preferred_element_type=jnp.float32,
    ).astype(jnp.bfloat16)
    term_rows = lax.all_to_all(
        partial_value, "ctx", split_axis=0, concat_axis=1, tiled=True
    ).astype(jnp.float32)
    summed = lax.psum_scatter(
        term_rows.astype(jnp.bfloat16), "tp", scatter_dimension=1, tiled=True
    ).astype(jnp.float32)
    hidden_out = (residual.astype(jnp.float32) + summed).astype(jnp.bfloat16)
    token_score = jnp.dot(hidden_out, value_head, preferred_element_type=jnp.float32)
    one_hot = (turn_ids[:, None] == jnp.arange(TURNS, dtype=jnp.int32)[None, :]).astype(jnp.float32)
    local_sum = jnp.dot(token_score, one_hot, precision=lax.Precision.HIGHEST)
    local_count = jnp.where(lax.axis_index("tp") == 0, jnp.sum(one_hot, axis=0), 0.0)
    totals, counts = lax.psum((local_sum, local_count), ("ctx", "tp"))
    turn_means = totals / jnp.maximum(counts, 1.0)
    return (hidden_out, turn_means)


MESH = pl.DeviceIdType.MESH
F32 = jnp.float32
BF16 = jnp.bfloat16
MASKED = -1e30


def split(rows):
    third = -(-rows // 48) * 16
    return ((0, third), (third, 2 * third), (2 * third, rows))


def kernel(
    dims, k_hbm, v_hbm, pos_hbm, tid_hbm, vh_hbm, q_hbm, res_hbm, w_hbm,
    out_hbm, mean_ref, k_ref, v_ref, pos_ref, tid_ref, vh_ref, q_ref, out_ref, in_sem, out_sem,
    own_send, own_recv,
    kvb, bias0, bias1, tcol, qrow, qs, ot, att, wv, acc, keep, sib_out, sib_in,
    xs_out, xs_in, red, fin, resv, tot,
    kv_send, kv_recv, att_send, att_recv, sib_send, sib_recv, xs_send, xs_recv,
    fin_send, fin_recv, tot_send, tot_recv, w_sem, res_sem, go_sem,
    far_send, far_recv, ys_send, ys_recv, two_send, ys_out, ys_in, two,
):
    n, tn, rows, groups, per, cb, reach = dims
    bands = split(rows)
    pieces = len(bands)
    half = rows // 2
    pad = -(-half // 16) * 16
    blocks = 2 * n
    lanes = per * pad
    chunks = groups * 2
    chunk = groups * per * HEAD_SIZE // chunks
    c = lax.axis_index("ctx")
    t = lax.axis_index("tp")
    core = lax.rem(t, 2)
    col = t // 2
    sibling = t + 1 - 2 * core
    across = lax.rem(t + 2, tn)
    own_q = 2 * core + col
    far_q = 2 * core + 1 - col
    inner = (c > 0) & (c < n - 1)
    keeper = col == c // 2
    scale = 1.0 / math.sqrt(HEAD_SIZE) * math.log2(math.e)

    arrays = [
        pltpu.make_async_copy(a, b, in_sem.at[i])
        for i, (a, b) in enumerate((
            (k_hbm, k_ref), (v_hbm, v_ref), (pos_hbm, pos_ref), (tid_hbm, tid_ref),
            (vh_hbm, vh_ref), (q_hbm, q_ref),
        ))
    ]
    barrier = pltpu.get_barrier_semaphore()

    for j in range(1, tn):
        pl.semaphore_signal(
            barrier, inc=1, device_id={"tp": lax.rem(t + j, tn)}, device_id_type=MESH
        )
    for away in (-1, 1):
        @pl.when((c + away >= 0) & (c + away < n))
        def _():
            pl.semaphore_signal(
                barrier, inc=1, device_id={"ctx": c + away}, device_id_type=MESH
            )

    for cp in arrays:
        cp.start()

    def w_copy(i):
        return pltpu.make_async_copy(
            w_hbm.at[:, pl.ds(pl.multiple_of(i * cb, 128), cb)], wv.at[i], w_sem.at[i]
        )

    res_copy = pltpu.make_async_copy(res_hbm, resv, res_sem)

    def needs(d, b):
        late = blocks - 1 - d
        return d - reach <= b <= d or late - reach <= b <= late

    def owner(b):
        return b if b < n else blocks - 1 - b

    def carried(d, e, b):
        if not 0 <= e < n:
            return False
        beyond = range(0, e + 1) if e < d else range(e, n)
        behind = owner(b) >= d if e < d else owner(b) <= d
        return behind and any(needs(x, b) for x in beyond)

    def kv_copy(g, b, e, way):
        return pltpu.make_async_remote_copy(
            src_ref=kvb.at[g, b], dst_ref=kvb.at[g, b],
            send_sem=kv_send.at[g, b, way], recv_sem=kv_recv.at[g, b],
            device_id={"ctx": e}, device_id_type=MESH,
        )

    def on(d):
        return pl.when(c == d)

    def kv_pass(d, g, b):
        for way, e in ((0, d - 1), (1, d + 1)):
            if carried(d, e, b):
                kv_copy(g, b, e, way).start()

    def kv_arrivals(d, dist):
        return [
            b for b in range(blocks)
            if abs(owner(b) - d) == dist
            and (carried(d - 1, d, b) if owner(b) < d else carried(d + 1, d, b))
        ]

    def kv_own(g):
        for d in range(n):
            @on(d)
            def _():
                for b in (d, blocks - 1 - d):
                    kv_pass(d, g, b)

    def kv_take(g, dists):
        for d in range(n):
            @on(d)
            def _():
                for dist in dists:
                    for b in kv_arrivals(d, dist):
                        kv_copy(g, b, d, 0).wait_recv()
                        kv_pass(d, g, b)

    for cp in arrays[:2]:
        cp.wait()
    zeros = jnp.zeros((pad - half, HEAD_SIZE), F32)
    for g in range(groups):
        span = slice(g * HEAD_SIZE, (g + 1) * HEAD_SIZE)
        for ref, low in ((k_ref, 0), (v_ref, pad)):
            x = ref[:, span].astype(F32)
            kvb[g, c, low:low + pad, :] = jnp.concatenate([x[:half], zeros]).astype(BF16)
            kvb[g, blocks - 1 - c, low:low + pad, :] = jnp.concatenate(
                [x[half:], zeros]
            ).astype(BF16)
    for d in range(n):
        window = set(range(n)) | set(range(n - 1 - d, blocks - d))
        missing = [b for b in sorted(window) if owner(b) != d and not any(
            b in kv_arrivals(d, dist) for dist in range(1, n))]
        if missing:
            @on(d)
            def _():
                for g in range(groups):
                    for b in missing:
                        kvb[g, b] = jnp.zeros((2 * pad, HEAD_SIZE), BF16)


    def att_copy(s, q, d):
        return pltpu.make_async_remote_copy(
            src_ref=att.at[s, q], dst_ref=att.at[s, q],
            send_sem=att_send.at[d, s, q], recv_sem=att_recv.at[s, q],
            device_id={"ctx": c + 1 - 2 * d}, device_id_type=MESH,
        )

    lead = half // 16 * 16

    def piece_rows(s, e):
        at = jnp.where(s < n // 2, 0, rows - lead) if e == 0 else jnp.where(s < n // 2, lead, 0)
        return pl.ds(pl.multiple_of(at, 16), lead if e == 0 else rows - lead)

    def own_copy(q, d, e):
        return pltpu.make_async_remote_copy(
            src_ref=att.at[c, q, piece_rows(c, e)], dst_ref=att.at[c, q, piece_rows(c, e)],
            send_sem=own_send.at[d, q, e], recv_sem=own_recv.at[d, q, e],
            device_id={"ctx": c + 1 - 2 * d}, device_id_type=MESH,
        )

    def next_copy(s, side, q, e):
        return pltpu.make_async_remote_copy(
            src_ref=att.at[s, q, piece_rows(s, e)], dst_ref=att.at[s, q, piece_rows(s, e)],
            send_sem=own_send.at[0, q, e], recv_sem=own_recv.at[side, q, e],
            device_id={"ctx": c}, device_id_type=MESH,
        )

    def goes(s, d):
        if d == 0:
            return (s <= c) & (c < n - 1)
        return (s >= c) & (c > 0)

    def band(p):
        return slice(*bands[p])

    def far_copy(s, q, p, d):
        return pltpu.make_async_remote_copy(
            src_ref=att.at[s, q, band(p)], dst_ref=att.at[s, q, band(p)],
            send_sem=far_send.at[q, p], recv_sem=far_recv.at[q, p],
            device_id={"ctx": c + 1 - 2 * d}, device_id_type=MESH,
        )

    def sib_copy(s, j, p):
        return pltpu.make_async_remote_copy(
            src_ref=sib_out.at[s, j, band(p)], dst_ref=sib_in.at[s, j, band(p)],
            send_sem=sib_send.at[s, j, p], recv_sem=sib_recv.at[s, j, p],
            device_id={"tp": sibling}, device_id_type=MESH,
        )

    def xs_copy(s, p):
        return pltpu.make_async_remote_copy(
            src_ref=xs_out.at[s, band(p)], dst_ref=xs_in.at[s, band(p)],
            send_sem=xs_send.at[s, p], recv_sem=xs_recv.at[s, p],
            device_id={"tp": across}, device_id_type=MESH,
        )

    def fin_copy(s, p):
        return pltpu.make_async_remote_copy(
            src_ref=red.at[s, band(p)], dst_ref=fin.at[own_q, band(p)],
            send_sem=fin_send.at[s, p], recv_sem=fin_recv.at[own_q, p],
            device_id={"ctx": s, "tp": c}, device_id_type=MESH,
        )

    def ys_copy(s, p):
        return pltpu.make_async_remote_copy(
            src_ref=ys_out.at[s, band(p)], dst_ref=ys_in.at[s, band(p)],
            send_sem=ys_send.at[s, p], recv_sem=ys_recv.at[s, p],
            device_id={"tp": across}, device_id_type=MESH,
        )

    def two_copy(s, p):
        return pltpu.make_async_remote_copy(
            src_ref=two.at[s, band(p)], dst_ref=fin.at[far_q, band(p)],
            send_sem=two_send.at[s, p], recv_sem=fin_recv.at[far_q, p],
            device_id={"ctx": s, "tp": c}, device_id_type=MESH,
        )

    def gathers(s):
        return inner & ((s == 0) | (s == n - 1))

    def fin_arrival(i, p):
        return pltpu.make_async_remote_copy(
            src_ref=red.at[0, band(p)], dst_ref=fin.at[i, band(p)],
            send_sem=fin_send.at[0, p], recv_sem=fin_recv.at[i, p],
            device_id={"ctx": t}, device_id_type=MESH,
        )

    pl.semaphore_wait(barrier, tn - 1 + jnp.where((c == 0) | (c == n - 1), 1, 2))
    for g in range(groups):
        kv_own(g)

    for cp in arrays[2:5]:
        cp.wait()
    ids = jnp.concatenate(
        [pos_ref[...].reshape(1, rows), tid_ref[...].reshape(1, rows),
         jnp.zeros((126, rows), jnp.int32)], axis=0
    )
    idcol = jnp.concatenate(
        [ids, jnp.zeros((128, -rows % 128), jnp.int32)], axis=1
    ).T[:rows, :]
    tcol[...] = idcol[:, 1:2]
    offs = lax.broadcasted_iota(jnp.int32, (pad, 128), 0)
    blank = jnp.zeros((pad - half, 128), jnp.int32)
    for hh in range(2):
        place = (c if hh == 0 else blocks - 1 - c) * half
        posc = jnp.concatenate([idcol[hh * half:(hh + 1) * half, :], blank], axis=0)
        tok = place + offs
        lane = lax.broadcasted_iota(jnp.int32, (pad, 128), 1)
        both = jnp.where(lane == 0, tok - posc, tok)
        qrow[hh] = jnp.concatenate([both] * per, axis=0).T[0:8, :]

    first = n - 1 - c

    zrow = jnp.zeros((pad - half, HEAD_SIZE), F32)

    def load_q(g):
        for h in range(per):
            at = (g * per + h) * HEAD_SIZE
            x = q_ref[:, at:at + HEAD_SIZE].astype(F32)
            for hh in range(2):
                qs[g, hh, h * pad:(h + 1) * pad, :] = jnp.concatenate(
                    [x[hh * half:(hh + 1) * half], zrow]
                ).astype(BF16)

    def attend(g, hh, count, base, mask):
        keys = kvb[g, pl.ds(base, count), 0:pad, :].reshape(count * pad, HEAD_SIZE)
        vals = kvb[g, pl.ds(base, count), pad:2 * pad, :].reshape(count * pad, HEAD_SIZE)
        s = lax.dot_general(
            keys, qs[g, hh], (((1,), (1,)), ((), ())), preferred_element_type=F32
        ) * scale + mask[0:count * pad, :].astype(F32)
        top = jnp.max(s, axis=0, keepdims=True)
        p = jnp.exp2(s - top)
        den = jnp.sum(p, axis=0, keepdims=True)
        o = lax.dot_general(
            vals, p.astype(BF16), (((0,), (0,)), ((), ())), preferred_element_type=F32
        )
        ot[g, hh] = (o * (1.0 / den)).T

    low_one, high_one = n // 2 - 1, n // 2

    def place(g, at_row, spans):
        for h in range(per):
            q, at = divmod((g * per + h) * HEAD_SIZE, chunk)
            parts = [ot[g, hh, h * pad + a:h * pad + b, :] for hh, a, b in spans]
            size = sum(b - a for _, a, b in spans)
            whole = parts[0] if len(parts) == 1 else jnp.concatenate(parts)
            att[c, q, at_row:at_row + size, at:at + HEAD_SIZE] = whole.astype(BF16)

    def send_own(g, e):
        for q in range(g * chunks // groups, (g + 1) * chunks // groups):
            for d in range(2):
                @pl.when(goes(c, d))
                def _():
                    own_copy(q, d, e).start()

    def early(g):
        @on(low_one)
        def _():
            attend(g, 0, low_one + 1, 0, bias0)
            place(g, 0, ((0, 0, lead),))
            send_own(g, 0)

        @on(high_one)
        def _():
            attend(g, 1, n + 1, first, bias1)
            place(g, rows - lead, ((1, half - lead, half),))
            send_own(g, 0)

    def late(g):
        @pl.when(c != low_one)
        def _():
            attend(g, 0, n, 0, bias0)

        @pl.when(c != high_one)
        def _():
            attend(g, 1, n + 1, first, bias1)

        @pl.when(c < n // 2)
        def _():
            place(g, lead, ((0, lead, half), (1, 0, half)))

        @pl.when(c >= n // 2)
        def _():
            place(g, 0, ((0, 0, half), (1, 0, half - lead)))

        @pl.when(c == 0)
        def _():
            place(g, 0, ((0, 0, lead),))

        @pl.when(c == n - 1)
        def _():
            place(g, rows - lead, ((1, half - lead, half),))

        @pl.when((c == 0) | (c == n - 1))
        def _():
            send_own(g, 0)

        send_own(g, 1)

    arrays[5].wait()
    load_q(0)
    for hh, count, base, mask in ((0, n, 0, bias0), (1, n + 1, first, bias1)):
        b = lax.broadcasted_iota(jnp.int32, (count, pad, lanes), 0) + base
        r = lax.broadcasted_iota(jnp.int32, (count, pad, lanes), 1)
        tok = jnp.where(r < half, b * half + r, blocks * rows).reshape(count * pad, lanes)
        ok = (tok <= qrow[hh, 1:2, :]) & (tok >= qrow[hh, 0:1, :])
        mask[...] = jnp.where(ok, 0.0, MASKED).astype(BF16)

    kv_take(0, (1,))
    early(0)
    load_q(1)
    kv_take(1, (1,))
    early(1)
    kv_take(0, range(2, n))
    late(0)
    for i in range(tn):
        w_copy(i).start()
    kv_take(1, range(2, n))
    late(1)

    res_copy.start()
    for i in range(tn):
        w_copy(i).wait()

    def column_of(j):
        k = jnp.where(lax.rem(j, 2) == 0, 1 - core, core)
        return 2 * k + jnp.where(j < 2, 1 - col, col)

    def project(s, side, q, whole):
        def column(j, _):
            i = column_of(j)
            if whole:
                prod = jnp.zeros((rows, cb), F32)
                for z in range(chunks):
                    prod = prod + jnp.dot(
                        att[s, z], wv[i, z * chunk:(z + 1) * chunk, :], preferred_element_type=F32
                    )
            else:
                prod = jnp.dot(
                    att[s, q], wv[i, q * chunk:(q + 1) * chunk, :], preferred_element_type=F32
                )
                if q > 0:
                    prod = acc[side, i] + prod
                if q < chunks - 1:
                    acc[side, i] = prod
                    return 0
            value = prod.astype(BF16)
            at = j // 2

            @pl.when(lax.rem(j, 2) == 0)
            def _():
                sib_out[s, at] = value
                for p in range(pieces):
                    sib_copy(s, at, p).start()

            @pl.when(lax.rem(j, 2) == 1)
            def _():
                keep[s, at] = value

            return 0

        lax.fori_loop(0, tn, column, 0)

    def far_project(s, q, p):
        def column(j, _):
            i = column_of(j)
            prod = acc[0, i, band(p)] + jnp.dot(
                att[s, q, band(p)],
                wv[i, pl.ds(pl.multiple_of(q * chunk, chunk), chunk), :],
                preferred_element_type=F32,
            )
            acc[0, i, band(p)] = prod
            at = j // 2

            @pl.when((q == chunks - 1) & (lax.rem(j, 2) == 0))
            def _():
                sib_out[s, at, band(p)] = prod.astype(BF16)
                sib_copy(s, at, p).start()

            @pl.when((q == chunks - 1) & (lax.rem(j, 2) == 1))
            def _():
                keep[s, at, band(p)] = prod.astype(BF16)

            return 0

        lax.fori_loop(0, tn, column, 0)

    def pair_sum(s, j, p):
        return keep[s, j, band(p)].astype(F32) + sib_in[s, j, band(p)].astype(F32)

    def pair_band(s, p):
        sib_copy(s, 0, p).wait_recv()

        @pl.when(jnp.logical_not(gathers(s) & keeper))
        def _():
            xs_out[s, band(p)] = pair_sum(s, 0, p).astype(BF16)
            xs_copy(s, p).start()

        sib_copy(s, 1, p).wait_recv()

        @pl.when(gathers(s) & jnp.logical_not(keeper))
        def _():
            ys_out[s, band(p)] = pair_sum(s, 1, p).astype(BF16)
            ys_copy(s, p).start()

    def pair_send(s):
        for p in range(pieces):
            pair_band(s, p)

    def reduce_band(s, p):
        mine = (s == c) & (t == c)

        @pl.when(jnp.logical_not(gathers(s)) | keeper)
        def _():
            xs_copy(s, p).wait_recv()
            summed = (pair_sum(s, 1, p) + xs_in[s, band(p)].astype(F32)).astype(BF16)

            @pl.when(mine)
            def _():
                fin[own_q, band(p)] = summed

            @pl.when(jnp.logical_not(mine))
            def _():
                red[s, band(p)] = summed
                fin_copy(s, p).start()

        @pl.when(gathers(s) & keeper)
        def _():
            ys_copy(s, p).wait_recv()
            two[s, band(p)] = (pair_sum(s, 0, p) + ys_in[s, band(p)].astype(F32)).astype(BF16)
            two_copy(s, p).start()

    def reduce_send(s):
        for p in range(pieces):
            reduce_band(s, p)

    near = jnp.where(c < n // 2, 0, n - 1)
    far = n - 1 - near

    def passes_far(s):
        return inner & (s == far)

    def att_drain(d):
        def one(s, _):
            @pl.when(goes(s, d) & jnp.logical_not(passes_far(s)) & (s != c))
            def _():
                for q in range(chunks):
                    att_copy(s, q, d).wait_send()

            @pl.when(goes(s, d) & (s == c))
            def _():
                for q in range(chunks):
                    for e in range(2):
                        own_copy(q, d, e).wait_send()

            @pl.when(goes(s, d) & passes_far(s))
            def _():
                for q in range(chunks):
                    for p in range(pieces):
                        far_copy(s, q, p, d).wait_send()

            return 0

        lax.fori_loop(0, n, one, 0)

    def both_sides(k, act):
        def one(side, _):
            s = c + k * (2 * side - 1)

            @pl.when((s >= 0) & (s < n))
            def _():
                act(s, side)

            return 0

        lax.fori_loop(0, 2, one, 0)

    project(c, 0, 0, True)

    def step(k, _):
        for q in range(chunks):
            def take(s, side):
                @pl.when(k == 1)
                def _():
                    for e in range(2):
                        next_copy(s, side, q, e).wait_recv()

                @pl.when(k > 1)
                def _():
                    att_copy(s, q, 0).wait_recv()

                for d in range(2):
                    @pl.when(goes(s, d) & jnp.logical_not(passes_far(s)))
                    def _():
                        att_copy(s, q, d).start()

                    @pl.when(goes(s, d) & passes_far(s))
                    def _():
                        far_copy(s, q, 0, d).start()
                        if q == chunks - 1:
                            for p in range(1, pieces):
                                for z in range(chunks):
                                    far_copy(s, z, p, d).start()

            both_sides(k, take)
            if q == 0:
                @pl.when(k == 1)
                def _():
                    pair_send(c)

                @pl.when(k > 1)
                def _():
                    both_sides(k - 1, lambda s, side: pair_send(s))
            both_sides(k, lambda s, side: project(s, side, q, False))
            if q == chunks - 1:
                @pl.when(k == 1)
                def _():
                    reduce_send(c)

                @pl.when(k > 1)
                def _():
                    def now(s, side):
                        @pl.when(jnp.logical_not(inner & (s == near)))
                        def _():
                            reduce_send(s)

                    both_sides(k - 1, now)
        return 0

    lax.fori_loop(1, n - 1, step, 0)
    both_sides(n - 2, lambda s, side: pair_send(s))

    @pl.when(inner)
    def _():
        for d in range(2):
            @pl.when((c < n // 2) == (d == 1))
            def _():
                att_drain(d)
        pl.semaphore_signal(go_sem, inc=1, device_id={"ctx": n - 1 - c}, device_id_type=MESH)
        reduce_send(near)
        pl.semaphore_wait(go_sem, 1)
        reduce_send(far)

    @pl.when(jnp.logical_not(inner))
    def _():
        acc[0] = jnp.zeros(acc.shape[1:], F32)

        def far_step(p):
            def one(q, _):
                far_copy(far, q, p, 0).wait_recv()
                far_project(far, q, p)
                return 0

            return one

        for p in range(pieces):
            lax.fori_loop(0, chunks - 1, far_step(p), 0)
            if p == 0:
                both_sides(n - 2, lambda s, side: reduce_send(s))
            else:
                reduce_band(far, p - 1)
            lax.fori_loop(chunks - 1, chunks, far_step(p), 0)
            pair_band(far, p)
        reduce_band(far, pieces - 1)

    def out_copy(p):
        return pltpu.make_async_copy(
            out_ref.at[band(p)], out_hbm.at[band(p)], out_sem.at[p]
        )

    res_copy.wait()
    line = jnp.zeros((1, 128), F32)
    one = jnp.where(t == 0, 1.0, 0.0)
    for p in range(pieces):
        rng = band(p)
        piece = bands[p][1] - bands[p][0]
        lane = lax.broadcasted_iota(jnp.int32, (piece, 128), 1)
        score = jnp.zeros((piece, 1), F32)
        for i in range(tn):
            @pl.when(jnp.logical_not((c == t) & (own_q == i)))
            def _():
                fin_arrival(i, p).wait_recv()
            span = slice(i * cb, (i + 1) * cb)
            hidden = (resv[rng, span].astype(F32) + fin[i, rng, :].astype(F32)).astype(BF16)
            out_ref[rng, span] = hidden
            score = score + jnp.sum(
                hidden.astype(F32) * vh_ref[span].astype(F32).reshape(1, cb), axis=1, keepdims=True
            )
        turn = tcol[rng, :]
        terms = jnp.where(turn == lane, score, jnp.where(turn + 64 == lane, one, 0.0))
        line = line + jnp.sum(terms, axis=0, keepdims=True)
        out_copy(p).start()
    me = c * tn + t
    tot[me] = line

    def tot_copy(j):
        other = lax.rem(me + jnp.where(c < n // 2, n * tn - j, j), n * tn)
        return pltpu.make_async_remote_copy(
            src_ref=tot.at[me], dst_ref=tot.at[me],
            send_sem=tot_send.at[other], recv_sem=tot_recv.at[me],
            device_id={"ctx": other // tn, "tp": lax.rem(other, tn)}, device_id_type=MESH,
        )

    def tot_arrival(j):
        other = lax.rem(me + jnp.where(c < n // 2, n * tn - j, j), n * tn)
        return pltpu.make_async_remote_copy(
            src_ref=tot.at[me], dst_ref=tot.at[other],
            send_sem=tot_send.at[other], recv_sem=tot_recv.at[other],
            device_id={"ctx": other // tn, "tp": lax.rem(other, tn)}, device_id_type=MESH,
        )

    for j in range(1, n * tn):
        tot_copy(j).start()

    for d in range(n):
        @on(d)
        def _():
            for g in range(groups):
                for b in range(blocks):
                    held = owner(b) == d or any(
                        b in kv_arrivals(d, dist) for dist in range(1, n)
                    )
                    for way, e in ((0, d - 1), (1, d + 1)):
                        if held and carried(d, e, b):
                            kv_copy(g, b, e, way).wait_send()

    def drain(s, _):
        for j in range(2):
            for p in range(pieces):
                sib_copy(s, j, p).wait_send()
        for p in range(pieces):
            @pl.when(jnp.logical_not(gathers(s) & keeper))
            def _():
                xs_copy(s, p).wait_send()

            @pl.when(gathers(s) & jnp.logical_not(keeper))
            def _():
                ys_copy(s, p).wait_send()

            @pl.when(gathers(s) & keeper)
            def _():
                two_copy(s, p).wait_send()

            @pl.when(
                jnp.logical_not((s == c) & (t == c)) & (jnp.logical_not(gathers(s)) | keeper)
            )
            def _():
                fin_copy(s, p).wait_send()

        return 0

    lax.fori_loop(0, n, drain, 0)
    for d in range(2):
        @pl.when(jnp.logical_not(inner & ((c < n // 2) == (d == 1))))
        def _():
            att_drain(d)


    for j in range(1, n * tn):
        tot_arrival(j).wait_recv()
        tot_copy(j).wait_send()
    total = jnp.sum(tot[...], axis=0)
    for p in range(pieces):
        out_copy(p).wait()
    mean_ref[...] = (
        total[:, :TURNS] / jnp.maximum(total[:, 64:64 + TURNS], 1.0)
    ).reshape(TURNS)


def deliver(hidden, means, hidden_out, means_out):
    hidden_out[...] = hidden[...]
    means_out[...] = means[...]


def fused(
    n, tn, reach, queries, keys, values, residual, out_weight, value_head, segment_ids,
    positions, turn_ids
):
    rows, width = queries.shape
    groups = keys.shape[1] // HEAD_SIZE
    per = width // keys.shape[1]
    cols = out_weight.shape[1]
    cb = cols // tn
    pad = -(-(rows // 2) // 16) * 16
    pieces = len(split(rows))
    chunks = 2 * groups
    dims = (n, tn, rows, groups, per, cb, reach)
    vmem = pl.BlockSpec(memory_space=pltpu.VMEM)
    hbm = pl.BlockSpec(memory_space=pl.ANY)
    dma = pltpu.SemaphoreType.DMA
    results = pl.pallas_call(
        functools.partial(kernel, dims),
        out_shape=(
            jax.ShapeDtypeStruct((rows, cols), BF16),
            jax.ShapeDtypeStruct((TURNS,), F32),
        ),
        in_specs=[hbm] * 8,
        out_specs=(hbm, vmem),
        scratch_shapes=[
            pltpu.VMEM(keys.shape, BF16),
            pltpu.VMEM(values.shape, BF16),
            pltpu.VMEM((rows,), jnp.int32),
            pltpu.VMEM((rows,), jnp.int32),
            pltpu.VMEM(value_head.shape, BF16),
            pltpu.VMEM((rows, width), BF16),
            pltpu.VMEM((rows, cols), BF16),
            dma((6,)), dma((pieces,)),
            dma((2, chunks, 2)), dma((2, chunks, 2)),
            pltpu.VMEM((groups, 2 * n, 2 * pad, HEAD_SIZE), BF16),
            pltpu.VMEM((n * pad, per * pad), BF16),
            pltpu.VMEM(((n + 1) * pad, per * pad), BF16),
            pltpu.VMEM((rows, 1), jnp.int32),
            pltpu.VMEM((2, 8, per * pad), jnp.int32),
            pltpu.VMEM((groups, 2, per * pad, HEAD_SIZE), BF16),
            pltpu.VMEM((groups, 2, per * pad, HEAD_SIZE), F32),
            pltpu.VMEM((n, chunks, rows, width // chunks), BF16),
            pltpu.VMEM((tn, width, cb), BF16),
            pltpu.VMEM((2, tn, rows, cb), F32),
            pltpu.VMEM((n, 2, rows, cb), BF16),
            pltpu.VMEM((n, 2, rows, cb), BF16),
            pltpu.VMEM((n, 2, rows, cb), BF16),
            pltpu.VMEM((n, rows, cb), BF16),
            pltpu.VMEM((n, rows, cb), BF16),
            pltpu.VMEM((n, rows, cb), BF16),
            pltpu.VMEM((tn, rows, cb), BF16),
            pltpu.VMEM((rows, cols), BF16),
            pltpu.VMEM((n * tn, 1, 128), F32),
            dma((groups, 2 * n, 2)), dma((groups, 2 * n)),
            dma((2, n, chunks)), dma((n, chunks)),
            dma((n, 2, pieces)), dma((n, 2, pieces)),
            dma((n, pieces)), dma((n, pieces)),
            dma((n, pieces)), dma((tn, pieces)),
            dma((n * tn,)), dma((n * tn,)),
            dma((tn,)), dma(()), pltpu.SemaphoreType.REGULAR,
            dma((chunks, pieces)), dma((chunks, pieces)),
            dma((n, pieces)), dma((n, pieces)), dma((n, pieces)),
            pltpu.VMEM((n, rows, cb), BF16),
            pltpu.VMEM((n, rows, cb), BF16),
            pltpu.VMEM((n, rows, cb), BF16),
        ],
        compiler_params=pltpu.CompilerParams(
            collective_id=0, has_side_effects=True, vmem_limit_bytes=56 * 1024 * 1024
        ),
    )(
        keys, values, positions, turn_ids, value_head, queries, residual, out_weight,
    )
    return pl.pallas_call(
        deliver,
        out_shape=(
            jax.ShapeDtypeStruct((rows, cols), BF16),
            jax.ShapeDtypeStruct((TURNS,), F32),
        ),
        in_specs=[vmem, vmem],
        out_specs=(vmem, vmem),
    )(*results)


def body(n, tn, *args):
    queries, keys, weight = args[0], args[1], args[4]
    rows = queries.shape[0]
    per = queries.shape[1] // keys.shape[1]
    longest = 7 * n * rows // (4 * (TURNS // 4))
    reach = -(-(longest - 1) // (rows // 2))
    lanes = per * (-(-(rows // 2) // 16) * 16)
    fits = (
        n == tn == 4 and reach == n and rows % 16 == 0 and weight.shape[1] % (128 * tn) == 0
        and lanes % 128 == 0
    )
    if fits:
        return fused(n, tn, reach, *args)
    return shards(*args)


def solution(mesh):
    return jax.shard_map(
        functools.partial(body, mesh.shape["ctx"], mesh.shape["tp"]),
        mesh=mesh,
        in_specs=(
            P(("groups", "ctx"), "tp"),
            P(("groups", "ctx"), "tp"),
            P(("groups", "ctx"), "tp"),
            P(("groups", "ctx"), "tp"),
            P("tp", "ctx"),
            P("tp"),
            P(("groups", "ctx")),
            P(("groups", "ctx")),
            P(("groups", "ctx")),
        ),
        out_specs=(P(("groups", "ctx"), "tp"), P("groups")),
        check_vma=False,
    )
```

```python
import functools
import math

import jax
import jax.numpy as jnp
from jax import lax
from jax.experimental import pallas as pl
from jax.experimental.pallas import tpu as pltpu
from jax.sharding import PartitionSpec as P

HEAD_SIZE = 128
TURNS = 16


def shards(
    queries, keys, values, residual, out_weight, value_head, segment_ids, positions, turn_ids
):
    tok_rows = queries.shape[0]
    kv_heads = keys.shape[1] // HEAD_SIZE
    query_head_group = queries.shape[1] // keys.shape[1]
    query_rows = query_head_group * tok_rows
    score_scale = 1.0 / math.sqrt(HEAD_SIZE)
    grouped = (
        queries.reshape(tok_rows, kv_heads, query_head_group, HEAD_SIZE)
        .transpose(1, 2, 0, 3)
        .reshape(kv_heads, query_rows, HEAD_SIZE)
    )
    seg_rows = jnp.tile(segment_ids, query_head_group)
    pos_rows = jnp.tile(positions, query_head_group)

    def update(running, key_block, value_block, seg_block, pos_block):
        allowed = (seg_rows[:, None] == seg_block[None, :]) & (
            pos_block[None, :] <= pos_rows[:, None]
        )
        numerator, row_max, denominator = running
        scores = (
            jnp.einsum("hqd,khd->hqk", grouped, key_block, preferred_element_type=jnp.float32)
            * score_scale
        )
        scores = jnp.where(allowed[None], scores, -1e30)
        new_max = jnp.maximum(row_max, jnp.max(scores, axis=2))
        weights = jnp.where(allowed[None], jnp.exp(scores - new_max[..., None]), 0.0)
        factor = jnp.exp(row_max - new_max)
        denominator = denominator * factor + jnp.sum(weights, axis=2)
        product = jnp.einsum(
            "hqk,khd->hqd",
            weights.astype(jnp.bfloat16),
            value_block,
            preferred_element_type=jnp.float32,
        )
        numerator = numerator * factor[..., None] + product
        return (numerator, new_max, denominator)

    initial = (
        jnp.zeros((kv_heads, query_rows, HEAD_SIZE), jnp.float32),
        jnp.full((kv_heads, query_rows), -1e30, jnp.float32),
        jnp.zeros((kv_heads, query_rows), jnp.float32),
    )
    running = initial
    key_piece = lax.all_gather(keys, "ctx", axis=0, tiled=True)
    value_piece = lax.all_gather(values, "ctx", axis=0, tiled=True)
    seg_piece = lax.all_gather(segment_ids, "ctx", axis=0, tiled=True)
    pos_piece = lax.all_gather(positions, "ctx", axis=0, tiled=True)
    row_count = key_piece.shape[0]
    key_piece = key_piece.reshape(row_count, kv_heads, HEAD_SIZE)
    value_piece = value_piece.reshape(row_count, kv_heads, HEAD_SIZE)
    block_width = math.gcd(row_count, 512)
    block_steps = row_count // block_width
    stacked = (
        key_piece.reshape(block_steps, block_width, kv_heads, HEAD_SIZE),
        value_piece.reshape(block_steps, block_width, kv_heads, HEAD_SIZE),
        seg_piece.reshape(block_steps, block_width),
        pos_piece.reshape(block_steps, block_width),
    )

    def block_step(running_state, block_set):
        return (update(running_state, block_set[0], block_set[1], block_set[2], block_set[3]), None)

    running, _ = lax.scan(block_step, running, stacked)
    numerator, row_max, denominator = running
    attention = (numerator / denominator[..., None]).reshape(
        kv_heads, query_head_group, tok_rows, HEAD_SIZE
    )
    attention = (
        attention.transpose(2, 0, 1, 3)
        .reshape(tok_rows, kv_heads * query_head_group * HEAD_SIZE)
        .astype(jnp.bfloat16)
    )
    partial_value = jnp.dot(
        lax.all_gather(attention, "ctx", axis=0, tiled=True),
        out_weight,
        preferred_element_type=jnp.float32,
    ).astype(jnp.bfloat16)
    term_rows = lax.all_to_all(
        partial_value, "ctx", split_axis=0, concat_axis=1, tiled=True
    ).astype(jnp.float32)
    summed = lax.psum_scatter(
        term_rows.astype(jnp.bfloat16), "tp", scatter_dimension=1, tiled=True
    ).astype(jnp.float32)
    hidden_out = (residual.astype(jnp.float32) + summed).astype(jnp.bfloat16)
    token_score = jnp.dot(hidden_out, value_head, preferred_element_type=jnp.float32)
    one_hot = (turn_ids[:, None] == jnp.arange(TURNS, dtype=jnp.int32)[None, :]).astype(jnp.float32)
    local_sum = jnp.dot(token_score, one_hot, precision=lax.Precision.HIGHEST)
    local_count = jnp.where(lax.axis_index("tp") == 0, jnp.sum(one_hot, axis=0), 0.0)
    totals, counts = lax.psum((local_sum, local_count), ("ctx", "tp"))
    turn_means = totals / jnp.maximum(counts, 1.0)
    return (hidden_out, turn_means)


MESH = pl.DeviceIdType.MESH
F32 = jnp.float32
BF16 = jnp.bfloat16
MASKED = -1e30


def split(rows):
    third = -(-rows // 48) * 16
    return ((0, third), (third, 2 * third), (2 * third, rows))


def kernel(
    dims, k_hbm, v_hbm, pos_hbm, tid_hbm, vh_hbm, q_hbm, res_hbm, w_hbm,
    out_hbm, mean_ref, k_ref, v_ref, pos_ref, tid_ref, vh_ref, q_ref, out_ref, in_sem, out_sem,
    own_send, own_recv,
    kvb, bias0, bias1, tcol, qrow, qs, ot, att, wv, acc, keep, sib_out, sib_in,
    xs_out, xs_in, red, fin, resv, tot,
    kv_send, kv_recv, att_send, att_recv, sib_send, sib_recv, xs_send, xs_recv,
    fin_send, fin_recv, tot_send, tot_recv, w_sem, res_sem, go_sem,
    far_send, far_recv, ys_send, ys_recv, two_send, ys_out, ys_in, two,
):
    n, tn, rows, groups, per, cb, reach = dims
    bands = split(rows)
    pieces = len(bands)
    half = rows // 2
    pad = -(-half // 16) * 16
    blocks = 2 * n
    lanes = per * pad
    chunks = groups * 2
    chunk = groups * per * HEAD_SIZE // chunks
    c = lax.axis_index("ctx")
    t = lax.axis_index("tp")
    core = lax.rem(t, 2)
    col = t // 2
    sibling = t + 1 - 2 * core
    across = lax.rem(t + 2, tn)
    own_q = 2 * core + col
    far_q = 2 * core + 1 - col
    inner = (c > 0) & (c < n - 1)
    keeper = col == c // 2
    scale = 1.0 / math.sqrt(HEAD_SIZE) * math.log2(math.e)

    arrays = [
        pltpu.make_async_copy(a, b, in_sem.at[i])
        for i, (a, b) in enumerate((
            (k_hbm, k_ref), (v_hbm, v_ref), (pos_hbm, pos_ref), (tid_hbm, tid_ref),
            (vh_hbm, vh_ref), (q_hbm, q_ref),
        ))
    ]
    barrier = pltpu.get_barrier_semaphore()

    for j in range(1, tn):
        pl.semaphore_signal(
            barrier, inc=1, device_id={"tp": lax.rem(t + j, tn)}, device_id_type=MESH
        )
    for away in (-1, 1):
        @pl.when((c + away >= 0) & (c + away < n))
        def _():
            pl.semaphore_signal(
                barrier, inc=1, device_id={"ctx": c + away}, device_id_type=MESH
            )

    for cp in arrays:
        cp.start()

    def w_copy(i):
        return pltpu.make_async_copy(
            w_hbm.at[:, pl.ds(pl.multiple_of(i * cb, 128), cb)], wv.at[i], w_sem.at[i]
        )

    res_copy = pltpu.make_async_copy(res_hbm, resv, res_sem)

    def needs(d, b):
        late = blocks - 1 - d
        return d - reach <= b <= d or late - reach <= b <= late

    def owner(b):
        return b if b < n else blocks - 1 - b

    def carried(d, e, b):
        if not 0 <= e < n:
            return False
        beyond = range(0, e + 1) if e < d else range(e, n)
        behind = owner(b) >= d if e < d else owner(b) <= d
        return behind and any(needs(x, b) for x in beyond)

    def kv_copy(g, b, e, way):
        return pltpu.make_async_remote_copy(
            src_ref=kvb.at[g, b], dst_ref=kvb.at[g, b],
            send_sem=kv_send.at[g, b, way], recv_sem=kv_recv.at[g, b],
            device_id={"ctx": e}, device_id_type=MESH,
        )

    def on(d):
        return pl.when(c == d)

    def kv_pass(d, g, b):
        for way, e in ((0, d - 1), (1, d + 1)):
            if carried(d, e, b):
                kv_copy(g, b, e, way).start()

    def kv_arrivals(d, dist):
        return [
            b for b in range(blocks)
            if abs(owner(b) - d) == dist
            and (carried(d - 1, d, b) if owner(b) < d else carried(d + 1, d, b))
        ]

    def kv_own(g):
        for d in range(n):
            @on(d)
            def _():
                for b in (d, blocks - 1 - d):
                    kv_pass(d, g, b)

    def kv_take(g, dists):
        for d in range(n):
            @on(d)
            def _():
                for dist in dists:
                    for b in kv_arrivals(d, dist):
                        kv_copy(g, b, d, 0).wait_recv()
                        kv_pass(d, g, b)

    for cp in arrays[:2]:
        cp.wait()
    zeros = jnp.zeros((pad - half, HEAD_SIZE), F32)
    for g in range(groups):
        span = slice(g * HEAD_SIZE, (g + 1) * HEAD_SIZE)
        for ref, low in ((k_ref, 0), (v_ref, pad)):
            x = ref[:, span].astype(F32)
            kvb[g, c, low:low + pad, :] = jnp.concatenate([x[:half], zeros]).astype(BF16)
            kvb[g, blocks - 1 - c, low:low + pad, :] = jnp.concatenate(
                [x[half:], zeros]
            ).astype(BF16)
    for d in range(n):
        window = set(range(n)) | set(range(n - 1 - d, blocks - d))
        missing = [b for b in sorted(window) if owner(b) != d and not any(
            b in kv_arrivals(d, dist) for dist in range(1, n))]
        if missing:
            @on(d)
            def _():
                for g in range(groups):
                    for b in missing:
                        kvb[g, b] = jnp.zeros((2 * pad, HEAD_SIZE), BF16)


    def att_copy(s, q, d):
        return pltpu.make_async_remote_copy(
            src_ref=att.at[s, q], dst_ref=att.at[s, q],
            send_sem=att_send.at[d, s, q], recv_sem=att_recv.at[s, q],
            device_id={"ctx": c + 1 - 2 * d}, device_id_type=MESH,
        )

    lead = half // 16 * 16

    def piece_rows(s, e):
        at = jnp.where(s < n // 2, 0, rows - lead) if e == 0 else jnp.where(s < n // 2, lead, 0)
        return pl.ds(pl.multiple_of(at, 16), lead if e == 0 else rows - lead)

    def own_copy(q, d, e):
        return pltpu.make_async_remote_copy(
            src_ref=att.at[c, q, piece_rows(c, e)], dst_ref=att.at[c, q, piece_rows(c, e)],
            send_sem=own_send.at[d, q, e], recv_sem=own_recv.at[d, q, e],
            device_id={"ctx": c + 1 - 2 * d}, device_id_type=MESH,
        )

    def next_copy(s, side, q, e):
        return pltpu.make_async_remote_copy(
            src_ref=att.at[s, q, piece_rows(s, e)], dst_ref=att.at[s, q, piece_rows(s, e)],
            send_sem=own_send.at[0, q, e], recv_sem=own_recv.at[side, q, e],
            device_id={"ctx": c}, device_id_type=MESH,
        )

    def goes(s, d):
        if d == 0:
            return (s <= c) & (c < n - 1)
        return (s >= c) & (c > 0)

    def band(p):
        return slice(*bands[p])

    def far_copy(s, q, p, d):
        return pltpu.make_async_remote_copy(
            src_ref=att.at[s, q, band(p)], dst_ref=att.at[s, q, band(p)],
            send_sem=far_send.at[q, p], recv_sem=far_recv.at[q, p],
            device_id={"ctx": c + 1 - 2 * d}, device_id_type=MESH,
        )

    def sib_copy(s, j, p):
        return pltpu.make_async_remote_copy(
            src_ref=sib_out.at[s, j, band(p)], dst_ref=sib_in.at[s, j, band(p)],
            send_sem=sib_send.at[s, j, p], recv_sem=sib_recv.at[s, j, p],
            device_id={"tp": sibling}, device_id_type=MESH,
        )

    def xs_copy(s, p):
        return pltpu.make_async_remote_copy(
            src_ref=xs_out.at[s, band(p)], dst_ref=xs_in.at[s, band(p)],
            send_sem=xs_send.at[s, p], recv_sem=xs_recv.at[s, p],
            device_id={"tp": across}, device_id_type=MESH,
        )

    def fin_copy(s, p):
        return pltpu.make_async_remote_copy(
            src_ref=red.at[s, band(p)], dst_ref=fin.at[own_q, band(p)],
            send_sem=fin_send.at[s, p], recv_sem=fin_recv.at[own_q, p],
            device_id={"ctx": s, "tp": c}, device_id_type=MESH,
        )

    def ys_copy(s, p):
        return pltpu.make_async_remote_copy(
            src_ref=ys_out.at[s, band(p)], dst_ref=ys_in.at[s, band(p)],
            send_sem=ys_send.at[s, p], recv_sem=ys_recv.at[s, p],
            device_id={"tp": across}, device_id_type=MESH,
        )

    def two_copy(s, p):
        return pltpu.make_async_remote_copy(
            src_ref=two.at[s, band(p)], dst_ref=fin.at[far_q, band(p)],
            send_sem=two_send.at[s, p], recv_sem=fin_recv.at[far_q, p],
            device_id={"ctx": s, "tp": c}, device_id_type=MESH,
        )

    def gathers(s):
        return inner & ((s == 0) | (s == n - 1))

    def fin_arrival(i, p):
        return pltpu.make_async_remote_copy(
            src_ref=red.at[0, band(p)], dst_ref=fin.at[i, band(p)],
            send_sem=fin_send.at[0, p], recv_sem=fin_recv.at[i, p],
            device_id={"ctx": t}, device_id_type=MESH,
        )

    pl.semaphore_wait(barrier, tn - 1 + jnp.where((c == 0) | (c == n - 1), 1, 2))
    for g in range(groups):
        kv_own(g)

    for cp in arrays[2:5]:
        cp.wait()
    ids = jnp.concatenate(
        [pos_ref[...].reshape(1, rows), tid_ref[...].reshape(1, rows),
         jnp.zeros((126, rows), jnp.int32)], axis=0
    )
    idcol = jnp.concatenate(
        [ids, jnp.zeros((128, -rows % 128), jnp.int32)], axis=1
    ).T[:rows, :]
    tcol[...] = idcol[:, 1:2]
    offs = lax.broadcasted_iota(jnp.int32, (pad, 128), 0)
    blank = jnp.zeros((pad - half, 128), jnp.int32)
    for hh in range(2):
        place = (c if hh == 0 else blocks - 1 - c) * half
        posc = jnp.concatenate([idcol[hh * half:(hh + 1) * half, :], blank], axis=0)
        tok = place + offs
        lane = lax.broadcasted_iota(jnp.int32, (pad, 128), 1)
        both = jnp.where(lane == 0, tok - posc, tok)
        qrow[hh] = jnp.concatenate([both] * per, axis=0).T[0:8, :]

    first = n - 1 - c

    zrow = jnp.zeros((pad - half, HEAD_SIZE), F32)

    def load_q(g):
        for h in range(per):
            at = (g * per + h) * HEAD_SIZE
            x = q_ref[:, at:at + HEAD_SIZE].astype(F32)
            for hh in range(2):
                qs[g, hh, h * pad:(h + 1) * pad, :] = jnp.concatenate(
                    [x[hh * half:(hh + 1) * half], zrow]
                ).astype(BF16)

    def attend(g, hh, count, base, mask):
        keys = kvb[g, pl.ds(base, count), 0:pad, :].reshape(count * pad, HEAD_SIZE)
        vals = kvb[g, pl.ds(base, count), pad:2 * pad, :].reshape(count * pad, HEAD_SIZE)
        s = lax.dot_general(
            keys, qs[g, hh], (((1,), (1,)), ((), ())), preferred_element_type=F32
        ) * scale + mask[0:count * pad, :].astype(F32)
        top = jnp.max(s, axis=0, keepdims=True)
        p = jnp.exp2(s - top)
        den = jnp.sum(p, axis=0, keepdims=True)
        o = lax.dot_general(
            vals, p.astype(BF16), (((0,), (0,)), ((), ())), preferred_element_type=F32
        )
        ot[g, hh] = (o * (1.0 / den)).T

    low_one, high_one = n // 2 - 1, n // 2

    def place(g, at_row, spans):
        for h in range(per):
            q, at = divmod((g * per + h) * HEAD_SIZE, chunk)
            parts = [ot[g, hh, h * pad + a:h * pad + b, :] for hh, a, b in spans]
            size = sum(b - a for _, a, b in spans)
            whole = parts[0] if len(parts) == 1 else jnp.concatenate(parts)
            att[c, q, at_row:at_row + size, at:at + HEAD_SIZE] = whole.astype(BF16)

    def send_own(g, e):
        for q in range(g * chunks // groups, (g + 1) * chunks // groups):
            for d in range(2):
                @pl.when(goes(c, d))
                def _():
                    own_copy(q, d, e).start()

    def early(g):
        @on(low_one)
        def _():
            attend(g, 0, low_one + 1, 0, bias0)
            place(g, 0, ((0, 0, lead),))
            send_own(g, 0)

        @on(high_one)
        def _():
            attend(g, 1, n + 1, first, bias1)
            place(g, rows - lead, ((1, half - lead, half),))
            send_own(g, 0)

    def late(g):
        @pl.when(c != low_one)
        def _():
            attend(g, 0, n, 0, bias0)

        @pl.when(c != high_one)
        def _():
            attend(g, 1, n + 1, first, bias1)

        @pl.when(c < n // 2)
        def _():
            place(g, lead, ((0, lead, half), (1, 0, half)))

        @pl.when(c >= n // 2)
        def _():
            place(g, 0, ((0, 0, half), (1, 0, half - lead)))

        @pl.when(c == 0)
        def _():
            place(g, 0, ((0, 0, lead),))

        @pl.when(c == n - 1)
        def _():
            place(g, rows - lead, ((1, half - lead, half),))

        @pl.when((c == 0) | (c == n - 1))
        def _():
            send_own(g, 0)

        send_own(g, 1)

    arrays[5].wait()
    load_q(0)
    for hh, count, base, mask in ((0, n, 0, bias0), (1, n + 1, first, bias1)):
        b = lax.broadcasted_iota(jnp.int32, (count, pad, lanes), 0) + base
        r = lax.broadcasted_iota(jnp.int32, (count, pad, lanes), 1)
        tok = jnp.where(r < half, b * half + r, blocks * rows).reshape(count * pad, lanes)
        ok = (tok <= qrow[hh, 1:2, :]) & (tok >= qrow[hh, 0:1, :])
        mask[...] = jnp.where(ok, 0.0, MASKED).astype(BF16)

    kv_take(0, (1,))
    early(0)
    load_q(1)
    kv_take(0, range(2, n))
    kv_take(1, (1,))
    early(1)
    late(0)
    for i in range(tn):
        w_copy(i).start()
    kv_take(1, range(2, n))
    late(1)

    res_copy.start()
    for i in range(tn):
        w_copy(i).wait()

    def column_of(j):
        k = jnp.where(lax.rem(j, 2) == 0, 1 - core, core)
        return 2 * k + jnp.where(j < 2, 1 - col, col)

    def project(s, side, q, whole):
        def column(j, _):
            i = column_of(j)
            if whole:
                prod = jnp.zeros((rows, cb), F32)
                for z in range(chunks):
                    prod = prod + jnp.dot(
                        att[s, z], wv[i, z * chunk:(z + 1) * chunk, :], preferred_element_type=F32
                    )
            else:
                prod = jnp.dot(
                    att[s, q], wv[i, q * chunk:(q + 1) * chunk, :], preferred_element_type=F32
                )
                if q > 0:
                    prod = acc[side, i] + prod
                if q < chunks - 1:
                    acc[side, i] = prod
                    return 0
            value = prod.astype(BF16)
            at = j // 2

            @pl.when(lax.rem(j, 2) == 0)
            def _():
                sib_out[s, at] = value
                for p in range(pieces):
                    sib_copy(s, at, p).start()

            @pl.when(lax.rem(j, 2) == 1)
            def _():
                keep[s, at] = value

            return 0

        lax.fori_loop(0, tn, column, 0)

    def far_project(s, q, p):
        def column(j, _):
            i = column_of(j)
            prod = acc[0, i, band(p)] + jnp.dot(
                att[s, q, band(p)],
                wv[i, pl.ds(pl.multiple_of(q * chunk, chunk), chunk), :],
                preferred_element_type=F32,
            )
            acc[0, i, band(p)] = prod
            at = j // 2

            @pl.when((q == chunks - 1) & (lax.rem(j, 2) == 0))
            def _():
                sib_out[s, at, band(p)] = prod.astype(BF16)
                sib_copy(s, at, p).start()

            @pl.when((q == chunks - 1) & (lax.rem(j, 2) == 1))
            def _():
                keep[s, at, band(p)] = prod.astype(BF16)

            return 0

        lax.fori_loop(0, tn, column, 0)

    def pair_sum(s, j, p):
        return keep[s, j, band(p)].astype(F32) + sib_in[s, j, band(p)].astype(F32)

    def pair_band(s, p):
        sib_copy(s, 0, p).wait_recv()

        @pl.when(jnp.logical_not(gathers(s) & keeper))
        def _():
            xs_out[s, band(p)] = pair_sum(s, 0, p).astype(BF16)
            xs_copy(s, p).start()

        sib_copy(s, 1, p).wait_recv()

        @pl.when(gathers(s) & jnp.logical_not(keeper))
        def _():
            ys_out[s, band(p)] = pair_sum(s, 1, p).astype(BF16)
            ys_copy(s, p).start()

    def pair_send(s):
        for p in range(pieces):
            pair_band(s, p)

    def reduce_band(s, p):
        mine = (s == c) & (t == c)

        @pl.when(jnp.logical_not(gathers(s)) | keeper)
        def _():
            xs_copy(s, p).wait_recv()
            summed = (pair_sum(s, 1, p) + xs_in[s, band(p)].astype(F32)).astype(BF16)

            @pl.when(mine)
            def _():
                fin[own_q, band(p)] = summed

            @pl.when(jnp.logical_not(mine))
            def _():
                red[s, band(p)] = summed
                fin_copy(s, p).start()

        @pl.when(gathers(s) & keeper)
        def _():
            ys_copy(s, p).wait_recv()
            two[s, band(p)] = (pair_sum(s, 0, p) + ys_in[s, band(p)].astype(F32)).astype(BF16)
            two_copy(s, p).start()

    def reduce_send(s):
        for p in range(pieces):
            reduce_band(s, p)

    near = jnp.where(c < n // 2, 0, n - 1)
    far = n - 1 - near

    def passes_far(s):
        return inner & (s == far)

    def att_drain(d):
        def one(s, _):
            @pl.when(goes(s, d) & jnp.logical_not(passes_far(s)) & (s != c))
            def _():
                for q in range(chunks):
                    att_copy(s, q, d).wait_send()

            @pl.when(goes(s, d) & (s == c))
            def _():
                for q in range(chunks):
                    for e in range(2):
                        own_copy(q, d, e).wait_send()

            @pl.when(goes(s, d) & passes_far(s))
            def _():
                for q in range(chunks):
                    for p in range(pieces):
                        far_copy(s, q, p, d).wait_send()

            return 0

        lax.fori_loop(0, n, one, 0)

    def both_sides(k, act):
        def one(side, _):
            s = c + k * (2 * side - 1)

            @pl.when((s >= 0) & (s < n))
            def _():
                act(s, side)

            return 0

        lax.fori_loop(0, 2, one, 0)

    project(c, 0, 0, True)

    def step(k, _):
        for q in range(chunks):
            def take(s, side):
                @pl.when(k == 1)
                def _():
                    for e in range(2):
                        next_copy(s, side, q, e).wait_recv()

                @pl.when(k > 1)
                def _():
                    att_copy(s, q, 0).wait_recv()

                for d in range(2):
                    @pl.when(goes(s, d) & jnp.logical_not(passes_far(s)))
                    def _():
                        att_copy(s, q, d).start()

                    @pl.when(goes(s, d) & passes_far(s))
                    def _():
                        far_copy(s, q, 0, d).start()
                        if q == chunks - 1:
                            for p in range(1, pieces):
                                for z in range(chunks):
                                    far_copy(s, z, p, d).start()

            both_sides(k, take)
            if q == 0:
                @pl.when(k == 1)
                def _():
                    pair_send(c)

                @pl.when(k > 1)
                def _():
                    both_sides(k - 1, lambda s, side: pair_send(s))
            both_sides(k, lambda s, side: project(s, side, q, False))
            if q == chunks - 1:
                @pl.when(k == 1)
                def _():
                    reduce_send(c)

                @pl.when(k > 1)
                def _():
                    def now(s, side):
                        @pl.when(jnp.logical_not(inner & (s == near)))
                        def _():
                            reduce_send(s)

                    both_sides(k - 1, now)
        return 0

    lax.fori_loop(1, n - 1, step, 0)
    both_sides(n - 2, lambda s, side: pair_send(s))

    @pl.when(inner)
    def _():
        for d in range(2):
            @pl.when((c < n // 2) == (d == 1))
            def _():
                att_drain(d)
        pl.semaphore_signal(go_sem, inc=1, device_id={"ctx": n - 1 - c}, device_id_type=MESH)
        reduce_send(near)
        pl.semaphore_wait(go_sem, 1)
        reduce_send(far)

    @pl.when(jnp.logical_not(inner))
    def _():
        acc[0] = jnp.zeros(acc.shape[1:], F32)

        def far_step(p):
            def one(q, _):
                far_copy(far, q, p, 0).wait_recv()
                far_project(far, q, p)
                return 0

            return one

        for p in range(pieces):
            lax.fori_loop(0, chunks - 1, far_step(p), 0)
            if p == 0:
                both_sides(n - 2, lambda s, side: reduce_send(s))
            else:
                reduce_band(far, p - 1)
            lax.fori_loop(chunks - 1, chunks, far_step(p), 0)
            pair_band(far, p)
        reduce_band(far, pieces - 1)

    def out_copy(p):
        return pltpu.make_async_copy(
            out_ref.at[band(p)], out_hbm.at[band(p)], out_sem.at[p]
        )

    res_copy.wait()
    line = jnp.zeros((1, 128), F32)
    one = jnp.where(t == 0, 1.0, 0.0)
    for p in range(pieces):
        rng = band(p)
        piece = bands[p][1] - bands[p][0]
        lane = lax.broadcasted_iota(jnp.int32, (piece, 128), 1)
        score = jnp.zeros((piece, 1), F32)
        for i in range(tn):
            @pl.when(jnp.logical_not((c == t) & (own_q == i)))
            def _():
                fin_arrival(i, p).wait_recv()
            span = slice(i * cb, (i + 1) * cb)
            hidden = (resv[rng, span].astype(F32) + fin[i, rng, :].astype(F32)).astype(BF16)
            out_ref[rng, span] = hidden
            score = score + jnp.sum(
                hidden.astype(F32) * vh_ref[span].astype(F32).reshape(1, cb), axis=1, keepdims=True
            )
        turn = tcol[rng, :]
        terms = jnp.where(turn == lane, score, jnp.where(turn + 64 == lane, one, 0.0))
        line = line + jnp.sum(terms, axis=0, keepdims=True)
        out_copy(p).start()
    me = c * tn + t
    tot[me] = line

    def tot_copy(j):
        other = lax.rem(me + jnp.where(c < n // 2, n * tn - j, j), n * tn)
        return pltpu.make_async_remote_copy(
            src_ref=tot.at[me], dst_ref=tot.at[me],
            send_sem=tot_send.at[other], recv_sem=tot_recv.at[me],
            device_id={"ctx": other // tn, "tp": lax.rem(other, tn)}, device_id_type=MESH,
        )

    def tot_arrival(j):
        other = lax.rem(me + jnp.where(c < n // 2, n * tn - j, j), n * tn)
        return pltpu.make_async_remote_copy(
            src_ref=tot.at[me], dst_ref=tot.at[other],
            send_sem=tot_send.at[other], recv_sem=tot_recv.at[other],
            device_id={"ctx": other // tn, "tp": lax.rem(other, tn)}, device_id_type=MESH,
        )

    for j in range(1, n * tn):
        tot_copy(j).start()

    for d in range(n):
        @on(d)
        def _():
            for g in range(groups):
                for b in range(blocks):
                    held = owner(b) == d or any(
                        b in kv_arrivals(d, dist) for dist in range(1, n)
                    )
                    for way, e in ((0, d - 1), (1, d + 1)):
                        if held and carried(d, e, b):
                            kv_copy(g, b, e, way).wait_send()

    def drain(s, _):
        for j in range(2):
            for p in range(pieces):
                sib_copy(s, j, p).wait_send()
        for p in range(pieces):
            @pl.when(jnp.logical_not(gathers(s) & keeper))
            def _():
                xs_copy(s, p).wait_send()

            @pl.when(gathers(s) & jnp.logical_not(keeper))
            def _():
                ys_copy(s, p).wait_send()

            @pl.when(gathers(s) & keeper)
            def _():
                two_copy(s, p).wait_send()

            @pl.when(
                jnp.logical_not((s == c) & (t == c)) & (jnp.logical_not(gathers(s)) | keeper)
            )
            def _():
                fin_copy(s, p).wait_send()

        return 0

    lax.fori_loop(0, n, drain, 0)
    for d in range(2):
        @pl.when(jnp.logical_not(inner & ((c < n // 2) == (d == 1))))
        def _():
            att_drain(d)


    for j in range(1, n * tn):
        tot_arrival(j).wait_recv()
        tot_copy(j).wait_send()
    total = jnp.sum(tot[...], axis=0)
    for p in range(pieces):
        out_copy(p).wait()
    mean_ref[...] = (
        total[:, :TURNS] / jnp.maximum(total[:, 64:64 + TURNS], 1.0)
    ).reshape(TURNS)


def deliver(hidden, means, hidden_out, means_out):
    hidden_out[...] = hidden[...]
    means_out[...] = means[...]


def fused(
    n, tn, reach, queries, keys, values, residual, out_weight, value_head, segment_ids,
    positions, turn_ids
):
    rows, width = queries.shape
    groups = keys.shape[1] // HEAD_SIZE
    per = width // keys.shape[1]
    cols = out_weight.shape[1]
    cb = cols // tn
    pad = -(-(rows // 2) // 16) * 16
    pieces = len(split(rows))
    chunks = 2 * groups
    dims = (n, tn, rows, groups, per, cb, reach)
    vmem = pl.BlockSpec(memory_space=pltpu.VMEM)
    hbm = pl.BlockSpec(memory_space=pl.ANY)
    dma = pltpu.SemaphoreType.DMA
    results = pl.pallas_call(
        functools.partial(kernel, dims),
        out_shape=(
            jax.ShapeDtypeStruct((rows, cols), BF16),
            jax.ShapeDtypeStruct((TURNS,), F32),
        ),
        in_specs=[hbm] * 8,
        out_specs=(hbm, vmem),
        scratch_shapes=[
            pltpu.VMEM(keys.shape, BF16),
            pltpu.VMEM(values.shape, BF16),
            pltpu.VMEM((rows,), jnp.int32),
            pltpu.VMEM((rows,), jnp.int32),
            pltpu.VMEM(value_head.shape, BF16),
            pltpu.VMEM((rows, width), BF16),
            pltpu.VMEM((rows, cols), BF16),
            dma((6,)), dma((pieces,)),
            dma((2, chunks, 2)), dma((2, chunks, 2)),
            pltpu.VMEM((groups, 2 * n, 2 * pad, HEAD_SIZE), BF16),
            pltpu.VMEM((n * pad, per * pad), BF16),
            pltpu.VMEM(((n + 1) * pad, per * pad), BF16),
            pltpu.VMEM((rows, 1), jnp.int32),
            pltpu.VMEM((2, 8, per * pad), jnp.int32),
            pltpu.VMEM((groups, 2, per * pad, HEAD_SIZE), BF16),
            pltpu.VMEM((groups, 2, per * pad, HEAD_SIZE), F32),
            pltpu.VMEM((n, chunks, rows, width // chunks), BF16),
            pltpu.VMEM((tn, width, cb), BF16),
            pltpu.VMEM((2, tn, rows, cb), F32),
            pltpu.VMEM((n, 2, rows, cb), BF16),
            pltpu.VMEM((n, 2, rows, cb), BF16),
            pltpu.VMEM((n, 2, rows, cb), BF16),
            pltpu.VMEM((n, rows, cb), BF16),
            pltpu.VMEM((n, rows, cb), BF16),
            pltpu.VMEM((n, rows, cb), BF16),
            pltpu.VMEM((tn, rows, cb), BF16),
            pltpu.VMEM((rows, cols), BF16),
            pltpu.VMEM((n * tn, 1, 128), F32),
            dma((groups, 2 * n, 2)), dma((groups, 2 * n)),
            dma((2, n, chunks)), dma((n, chunks)),
            dma((n, 2, pieces)), dma((n, 2, pieces)),
            dma((n, pieces)), dma((n, pieces)),
            dma((n, pieces)), dma((tn, pieces)),
            dma((n * tn,)), dma((n * tn,)),
            dma((tn,)), dma(()), pltpu.SemaphoreType.REGULAR,
            dma((chunks, pieces)), dma((chunks, pieces)),
            dma((n, pieces)), dma((n, pieces)), dma((n, pieces)),
            pltpu.VMEM((n, rows, cb), BF16),
            pltpu.VMEM((n, rows, cb), BF16),
            pltpu.VMEM((n, rows, cb), BF16),
        ],
        compiler_params=pltpu.CompilerParams(
            collective_id=0, has_side_effects=True, vmem_limit_bytes=56 * 1024 * 1024
        ),
    )(
        keys, values, positions, turn_ids, value_head, queries, residual, out_weight,
    )
    return pl.pallas_call(
        deliver,
        out_shape=(
            jax.ShapeDtypeStruct((rows, cols), BF16),
            jax.ShapeDtypeStruct((TURNS,), F32),
        ),
        in_specs=[vmem, vmem],
        out_specs=(vmem, vmem),
    )(*results)


def body(n, tn, *args):
    queries, keys, weight = args[0], args[1], args[4]
    rows = queries.shape[0]
    per = queries.shape[1] // keys.shape[1]
    longest = 7 * n * rows // (4 * (TURNS // 4))
    reach = -(-(longest - 1) // (rows // 2))
    lanes = per * (-(-(rows // 2) // 16) * 16)
    fits = (
        n == tn == 4 and reach == n and rows % 16 == 0 and weight.shape[1] % (128 * tn) == 0
        and lanes % 128 == 0
    )
    if fits:
        return fused(n, tn, reach, *args)
    return shards(*args)


def solution(mesh):
    return jax.shard_map(
        functools.partial(body, mesh.shape["ctx"], mesh.shape["tp"]),
        mesh=mesh,
        in_specs=(
            P(("groups", "ctx"), "tp"),
            P(("groups", "ctx"), "tp"),
            P(("groups", "ctx"), "tp"),
            P(("groups", "ctx"), "tp"),
            P("tp", "ctx"),
            P("tp"),
            P(("groups", "ctx")),
            P(("groups", "ctx")),
            P(("groups", "ctx")),
        ),
        out_specs=(P(("groups", "ctx"), "tp"), P("groups")),
        check_vma=False,
    )
```
